32 devices in a mesh: wide: 16 (over z, x, core), narrow: 2 (over y).
Axes of the slice: x: 2, y: 2, z: 4, core: 2. Of those that a mesh axis runs over, the one named last changes fastest.
Arguments:
- tracer: float32 [4, 1024, 4000], P('narrow', 'wide'), may hold values from -6 to 6
- courant: float32 [4, 1024, 4000], P('narrow', 'wide'), may hold values from -0.5 to 0.5
- nlon_counts: int32 [1024], P('wide'), may hold values from 20 to 4000, as said below
- band_map: int32 [32], replicated, may hold values from 0 to 31, each once
- owner_map: int32 [32], replicated, may hold values from 0 to 31, each once
- legendre: float32 [32, 2, 16, 512], P(('wide', 'narrow')), may hold values from -0.25 to 0.25
- modes_to: float32 [4, 4], replicated, may hold values from -3 to 3
- modes_from: float32 [4, 4], replicated, may hold values from -3 to 3
- mode_rates: float32 [4], replicated, may hold values from 1e-07 to 1e-05
Outputs:
- solved: float32 [2, 4, 32, 32], P(None, None, 'wide', 'narrow')
The draws below stay inside these ranges and needn't reach their ends.
Inputs may be any that keep to these rules, and one draw needn't show every extreme that they name: `nlon_counts`: multiples of 4; the two rows nearest the equator hold 4000 and the two polar rows hold 20. `band_map`: each wavenumber appears once. `owner_map`: each degree appears once.
All inputs are finite; a program needn't handle non-finite values.
Results may differ from the reference program's by a relative error of at most 0.0003.
Values sent between devices are 32-bit elements; how exact they have to be, the bound alone decides.
A program may use at most 64 MiB of HBM per device.

```python
import math
import jax
import jax.numpy as jnp
from jax import lax

NLON = 4000
NLAT = 1024
LEVELS = 4
M = 32
DEGREES = 32


def draw_nlon_counts(key, part):
    row_ids = jnp.arange(NLAT, dtype=jnp.int32)
    from_pole = jnp.minimum(row_ids, NLAT - 1 - row_ids)
    jitter = jax.random.randint(key, (NLAT,), 0, 10, dtype=jnp.int32)
    counts = 20 + 4 * from_pole + 4 * jitter * (from_pole > 0).astype(jnp.int32)
    counts = jnp.where(from_pole == NLAT // 2 - 1, NLON, counts)
    return jnp.minimum(counts, NLON).astype(jnp.int32)


def level_of(key, dims, shards, low, top_value):
    factor_of, own = 1.0, jax.random.fold_in(key, 6)
    for axis_at, parts in shards:
        draws = jnp.exp(jax.random.uniform(jax.random.fold_in(own, axis_at), (parts,), jnp.float32, low / len(shards), top_value / len(shards)))
        factor_of = factor_of * jnp.repeat(draws, dims[axis_at] // parts).reshape([-1 if axis == axis_at else 1 for axis in range(len(dims))])
    return factor_of


def gaussian(stream_key, extent, spread, reach, shards=(), kind=jnp.bfloat16):
    gain = level_of(stream_key, extent, shards, -0.22, 0.18) if shards else 1.0
    result = jax.random.normal(stream_key, extent, jnp.float32) * spread * gain
    return jnp.minimum(jnp.maximum(result, -reach), reach).astype(kind)


def setup_inputs(seed: int = 0) -> dict:
    splits = jax.random.split(jax.random.key(seed), 10)
    return {
        "tracer": gaussian(splits[0], (LEVELS, NLAT, NLON), 1.0, 6.0, ((0, 2), (1, 16)), jnp.float32),
        "courant": jnp.clip(jax.random.uniform(splits[1], (LEVELS, NLAT, NLON), jnp.float32, -0.5, 0.5) * level_of(splits[1], (LEVELS, NLAT, NLON), ((0, 2), (1, 16)), -0.4, 0.0), -0.5, 0.5),
        "nlon_counts": draw_nlon_counts(jax.random.fold_in(splits[9], 71), 0),
        "band_map": jax.random.permutation(splits[3], M).astype(jnp.int32),
        "owner_map": jax.random.permutation(splits[4], DEGREES).astype(jnp.int32),
        "legendre": gaussian(splits[5], (M, 2, M // 2, NLAT // 2), (NLAT // 2) ** -0.5, 0.25, ((0, 32),), jnp.float32),
        "modes_to": gaussian(splits[6], (LEVELS, LEVELS), LEVELS ** -0.5, 3.0, (), jnp.float32),
        "modes_from": gaussian(splits[7], (LEVELS, LEVELS), LEVELS ** -0.5, 3.0, (), jnp.float32),
        "mode_rates": jnp.clip(jnp.exp(jax.random.uniform(splits[8], (LEVELS,), jnp.float32, math.log(1.0000000116860974e-07), math.log(9.999999747378752e-06))), 1.0000000116860974e-07, 9.999999747378752e-06),
    }


def advect_section(field_ext, rate_ext, open_faces):
    row_total = field_ext.shape[1]
    row_below = field_ext[:, 0:row_total - 3]
    row_here = field_ext[:, 1:row_total - 2]
    row_above = field_ext[:, 2:row_total - 1]
    row_beyond = field_ext[:, 3:row_total]
    face_rate = rate_ext[:, 1:row_total - 2] * open_faces[1:row_total - 2][:, None]
    upwind = (5.0 * row_here + 2.0 * row_above - row_below) / 6.0
    downwind = (5.0 * row_above + 2.0 * row_here - row_beyond) / 6.0
    low_bound = jnp.minimum(row_here, row_above)
    high_bound = jnp.maximum(row_here, row_above)
    face_value = jnp.clip(jnp.where(face_rate >= 0.0, upwind, downwind), low_bound, high_bound)
    face_flux = face_rate * face_value
    return field_ext[:, 2:row_total - 2] - (face_flux[:, 1:] - face_flux[:, :-1])

def reference(tracer, courant, nlon_counts, band_map, owner_map, legendre, modes_to, modes_from, mode_rates):
    padding = ((0, 0), (4, 4), (0, 0))
    field_ext = jnp.pad(tracer, padding)
    rate_ext = jnp.pad(courant, padding)
    row_ids = jnp.arange(NLAT + 8, dtype=jnp.int32) - 4
    open_faces = ((row_ids >= 0) & (row_ids < NLAT - 1)).astype(jnp.float32)
    section_one = advect_section(field_ext, rate_ext, open_faces)
    section_two = advect_section(section_one, rate_ext[:, 2:-2], open_faces[2:-2])
    advected = 0.5 * tracer + 0.5 * section_two
    spectra = jnp.fft.rfft(advected, axis=2)[:, :, :M] / math.sqrt(NLON)
    wave_ids = jnp.arange(M, dtype=jnp.int32)
    kept_mask = (2 * wave_ids[None, :] < nlon_counts[:, None]).astype(jnp.float32)
    fourier = jnp.stack([jnp.real(spectra), jnp.imag(spectra)]) * kept_mask
    fourier = jnp.take(fourier, band_map, axis=3)
    half_rows = NLAT // 2
    north_half = fourier[:, :, :half_rows]
    south_half = jnp.flip(fourier[:, :, half_rows:], axis=2)
    sym_part = jnp.transpose(north_half + south_half, (3, 0, 1, 2))
    anti_part = jnp.transpose(north_half - south_half, (3, 0, 1, 2))

    def per_slot(slot_item):
        table_slot, slot_wave, sym_slot, anti_slot = slot_item
        same_parity = (jnp.arange(2, dtype=jnp.int32) - slot_wave) % 2 == 0
        chosen = jnp.where(same_parity[:, None, None, None], sym_slot[None], anti_slot[None])
        return jnp.einsum('pkj,pclj->pkcl', table_slot, chosen, precision=lax.Precision.HIGHEST)
    spectral = lax.map(per_slot, (legendre, band_map, sym_part, anti_part))
    degree_ids = 2 * jnp.arange(M // 2, dtype=jnp.int32)[None, :] + jnp.arange(2, dtype=jnp.int32)[:, None]
    upper_mask = (degree_ids[None] >= band_map[:, None, None]).astype(jnp.float32)
    spectral = spectral * upper_mask[:, :, :, None, None]
    spectral = jnp.transpose(spectral, (0, 2, 1, 3, 4)).reshape(M, DEGREES, 2, LEVELS)
    spectral = jnp.take(spectral, owner_map, axis=1)
    degree_sq = (owner_map * (owner_map + 1)).astype(jnp.float32)
    damping = 1.0 / (1.0 + degree_sq[None, :] * mode_rates[:, None])
    modal_part = jnp.einsum('kl,stcl->kstc', modes_to, spectral, precision=lax.Precision.HIGHEST)
    scaled = modal_part * damping[:, None, :, None]
    return jnp.einsum('ik,kstc->cist', modes_from, scaled, precision=lax.Precision.HIGHEST)
```

```python
import functools
import math

import jax
import jax.numpy as jnp
import numpy as np
from jax import lax
from jax.experimental import pallas as pl
from jax.experimental.pallas import tpu as pltpu
from jax.sharding import PartitionSpec as P

NLAT = 1024


def extended(array, sides, width):
    for axis, dim in sides:
        devices, length = (lax.axis_size(axis), array.shape[dim])
        up = [(i, (i + 1) % devices) for i in range(devices - 1)]
        down = [(j, i) for i, j in up]
        last = lax.slice_in_dim(array, length - width, length, axis=dim)
        initial = lax.slice_in_dim(array, 0, width, axis=dim)
        before = lax.ppermute(last, axis, up)
        after = lax.ppermute(initial, axis, down)
        array = jnp.concatenate([before, array, after], axis=dim)
    return array


def advect_section(field_ext, rate_ext, open_faces):
    row_total = field_ext.shape[1]
    row_below = field_ext[:, 0 : row_total - 3]
    row_here = field_ext[:, 1 : row_total - 2]
    row_above = field_ext[:, 2 : row_total - 1]
    row_beyond = field_ext[:, 3:row_total]
    face_rate = rate_ext[:, 1 : row_total - 2] * open_faces[1 : row_total - 2][:, None]
    upwind = (5.0 * row_here + 2.0 * row_above - row_below) / 6.0
    downwind = (5.0 * row_above + 2.0 * row_here - row_beyond) / 6.0
    low_bound = jnp.minimum(row_here, row_above)
    high_bound = jnp.maximum(row_here, row_above)
    face_value = jnp.clip(jnp.where(face_rate >= 0.0, upwind, downwind), low_bound, high_bound)
    face_flux = face_rate * face_value
    return field_ext[:, 2 : row_total - 2] - (face_flux[:, 1:] - face_flux[:, :-1])


def valid_rows(first_row, lat_rows, rim_width):
    row_ids = first_row + jnp.arange(lat_rows + 2 * rim_width, dtype=jnp.int32) - rim_width
    return ((row_ids >= 0) & (row_ids < NLAT - 1)).astype(jnp.float32)


def longitude_transform(advected, wave_count):
    levels_dev, lat_rows, lon_count = advected.shape
    short_len = 32
    long_len = lon_count // short_len
    block_count = wave_count // short_len
    row_count = levels_dev * lat_rows
    grid_rows = advected.reshape(row_count, short_len, long_len)
    short_ids = jnp.arange(short_len, dtype=jnp.int32)
    turn_one = short_ids[:, None] * short_ids[None, :] % short_len
    angle_one = 2.0 * math.pi / short_len * turn_one.astype(jnp.float32)
    highest = lax.Precision.HIGHEST
    inner_re = jnp.einsum("pab,ar->prb", grid_rows, jnp.cos(angle_one), precision=highest)
    inner_im = -jnp.einsum("pab,ar->prb", grid_rows, jnp.sin(angle_one), precision=highest)
    long_ids = jnp.arange(long_len, dtype=jnp.int32)
    block_ids = jnp.arange(block_count, dtype=jnp.int32)
    wave_ids = short_len * block_ids[None, None, :] + short_ids[:, None, None]
    turn_two = wave_ids * long_ids[None, :, None] % lon_count
    angle_two = 2.0 * math.pi / lon_count * turn_two.astype(jnp.float32)
    cos_two = jnp.cos(angle_two)
    sin_two = jnp.sin(angle_two)
    outer_re = jnp.einsum("prb,rbc->crp", inner_re, cos_two, precision=highest) + jnp.einsum(
        "prb,rbc->crp", inner_im, sin_two, precision=highest
    )
    outer_im = jnp.einsum("prb,rbc->crp", inner_im, cos_two, precision=highest) - jnp.einsum(
        "prb,rbc->crp", inner_re, sin_two, precision=highest
    )
    outer_re = (outer_re / math.sqrt(lon_count)).reshape(wave_count, levels_dev, lat_rows)
    outer_im = (outer_im / math.sqrt(lon_count)).reshape(wave_count, levels_dev, lat_rows)
    return jnp.stack([outer_re, outer_im], axis=1)


def body(
    tracer, courant, nlon_counts, band_map, owner_map, legendre, modes_to, modes_from, mode_rates
):
    levels_dev = tracer.shape[0]
    lat_rows = tracer.shape[1]
    n_wide = lax.axis_size("wide")
    n_narrow = lax.axis_size("narrow")
    first_row = lax.axis_index("wide") * lat_rows
    stacked = jnp.stack([tracer, courant])
    padded = extended(stacked, (("wide", 2),), 4)
    open_faces = valid_rows(first_row, lat_rows, 4)
    section_one = advect_section(padded[0], padded[1], open_faces)
    section_two = advect_section(section_one, padded[1][:, 2:-2], open_faces[2:-2])
    advected = 0.5 * tracer + 0.5 * section_two
    wave_count = band_map.shape[0]
    fourier = longitude_transform(advected, wave_count)
    wave_ids = jnp.arange(wave_count, dtype=jnp.int32)
    kept_mask = (2 * wave_ids[:, None] < nlon_counts[None, :]).astype(jnp.float32)
    fourier = fourier * kept_mask[:, None, None, :]
    slot_count = wave_count // (n_wide * n_narrow)
    fourier = jnp.einsum(
        "sm,mclj->sclj", (band_map[:, None] == wave_ids[None, :]).astype(jnp.float32), fourier,
        precision=lax.Precision.HIGHEST,
    )
    fourier = lax.all_to_all(fourier, "wide", split_axis=0, concat_axis=3, tiled=True)
    fourier = lax.all_to_all(fourier, "narrow", split_axis=0, concat_axis=2, tiled=True)
    levels_all = levels_dev * n_narrow
    half_rows = fourier.shape[3] // 2
    north_half = fourier[:, :, :, :half_rows]
    south_half = jnp.flip(fourier[:, :, :, half_rows:], axis=3)
    sym_part = north_half + south_half
    anti_part = north_half - south_half
    slot_start = (lax.axis_index("wide") * n_narrow + lax.axis_index("narrow")) * slot_count
    slot_waves = lax.dynamic_slice_in_dim(band_map, slot_start, slot_count)
    same_parity = (jnp.arange(2, dtype=jnp.int32)[None, :] - slot_waves[:, None]) % 2 == 0
    chosen = jnp.where(same_parity[:, :, None, None, None], sym_part[:, None], anti_part[:, None])
    spectral = jnp.einsum("spkj,spclj->spkcl", legendre, chosen, precision=lax.Precision.HIGHEST)
    degree_ids = (
        2 * jnp.arange(wave_count // 2, dtype=jnp.int32)[None, :]
        + jnp.arange(2, dtype=jnp.int32)[:, None]
    )
    upper_mask = (degree_ids[None] >= slot_waves[:, None, None]).astype(jnp.float32)
    spectral = spectral * upper_mask[:, :, :, None, None]
    spectral = jnp.transpose(spectral, (0, 2, 1, 3, 4)).reshape(
        slot_count, wave_count, 2, levels_all
    )
    spectral = jnp.einsum(
        "tn,sncl->stcl", (owner_map[:, None] == wave_ids[None, :]).astype(jnp.float32), spectral,
        precision=lax.Precision.HIGHEST,
    )
    gathered = lax.all_to_all(spectral, "narrow", split_axis=1, concat_axis=0, tiled=True)
    owned = gathered.shape[1]
    owned_degrees = lax.dynamic_slice_in_dim(owner_map, lax.axis_index("narrow") * owned, owned)
    degree_sq = (owned_degrees * (owned_degrees + 1)).astype(jnp.float32)
    damping = 1.0 / (1.0 + degree_sq[None, :] * mode_rates[:, None])
    modal_part = jnp.einsum("kl,stcl->kstc", modes_to, gathered, precision=lax.Precision.HIGHEST)
    scaled = modal_part * damping[:, None, :, None]
    return jnp.einsum("ik,kstc->cist", modes_from, scaled, precision=lax.Precision.HIGHEST)


MESH = pl.DeviceIdType.MESH
LANE = 128
PAD = 8
CUTS = (0, 5, 12, 20, 27, 32)
HALO = {1: (4, 3), 0: (4, 2)}


def chunk_list(lon_count):
    tiles = -(-lon_count // LANE)
    cuts = [min(lon_count, LANE * (tiles * cut // CUTS[-1])) for cut in CUTS]
    return [(lo, hi - lo) for lo, hi in zip(cuts, cuts[1:])]


def fourier_table(lon_count, wave_count):
    rows = -(-lon_count // LANE) * LANE
    turns = np.outer(np.arange(lon_count), np.arange(wave_count)) % lon_count
    angle = 2.0 * np.pi / lon_count * turns
    full = np.concatenate([np.cos(angle), -np.sin(angle)], axis=1) * (0.5 / np.sqrt(lon_count))
    high = full.astype(jnp.bfloat16)
    low = (full - high.astype(np.float64)).astype(jnp.bfloat16)
    table = np.zeros((rows, LANE), jnp.bfloat16)
    table[:lon_count] = np.concatenate([high, low], axis=1)
    return table


def split(value):
    high = value.astype(jnp.bfloat16)
    low = (value - high.astype(jnp.float32)).astype(jnp.bfloat16)
    return high, low


def section(field, rate, ahead):
    rows = field.shape[0]
    above = pltpu.roll(field, rows - 1, 0)
    step = above - field
    near = jnp.where(ahead, pltpu.roll(step, 1, 0), pltpu.roll(step, rows - 1, 0))
    slope = step * (1.0 / 3.0) + near * (1.0 / 6.0)
    slope = jnp.maximum(jnp.minimum(slope, jnp.maximum(step, 0.0)), jnp.minimum(step, 0.0))
    flux = rate * jnp.where(ahead, field + slope, above - slope)
    return field - (flux - pltpu.roll(flux, 1, 0))


def ids(shape, dim):
    return lax.broadcasted_iota(jnp.int32, shape, dim)


def fused_kernel(
    n_wide, n_narrow, lon_count,
    tracer, courant, nlon, band, owner, legendre, modes_to, modes_from, rates, table,
    out,
    q_buf, c_buf, t_buf, a_buf, acc, leg, nlon_s, band_s, owner_s, to_s, from_s, rate_s,
    pick, keep, degree, sent, got, lx, xs,
    small_sem, load_sem, table_sem, halo_send, halo_recv, leg_send, leg_recv, four_send, four_recv,
    entered,
):
    wide, narrow = lax.axis_index("wide"), lax.axis_index("narrow")
    total = n_wide * n_narrow
    me = wide * n_narrow + narrow
    levels, lat_rows = tracer.shape[0], tracer.shape[1]
    wave_count = band_s.shape[0]
    chunks = chunk_list(lon_count)
    owned = wave_count // n_narrow
    half_waves = wave_count // 2

    smalls = []
    for at, (here, there) in enumerate(
        ((nlon, nlon_s), (band, band_s), (owner, owner_s), (modes_to, to_s), (modes_from, from_s), (rates, rate_s))
    ):
        smalls.append(pltpu.make_async_copy(here, there, small_sem.at[at]))
    for copy in smalls:
        copy.start()
    loads = []
    for at, (lo, size) in enumerate(chunks):
        pair = []
        for which, (here, there) in enumerate(((tracer, q_buf), (courant, c_buf))):
            copy = pltpu.make_async_copy(
                here.at[:, :, pl.ds(lo, size)],
                there.at[:, pl.ds(PAD, lat_rows), pl.ds(lo, size)],
                load_sem.at[at, which],
            )
            copy.start()
            pair.append(copy)
        loads.append(pair)
    table_copy = pltpu.make_async_copy(table, t_buf, table_sem)
    table_copy.start()
    own_leg = pltpu.make_async_copy(legendre, leg.at[narrow], leg_recv.at[narrow])
    own_leg.start()

    @pl.when(wide == 0)
    def _():
        q_buf[:, 0:PAD, :] = jnp.zeros((levels, PAD, q_buf.shape[2]), jnp.float32)
        c_buf[:, 0:PAD, :] = jnp.zeros((levels, PAD, q_buf.shape[2]), jnp.float32)

    @pl.when(wide == n_wide - 1)
    def _():
        q_buf[:, PAD + lat_rows :, :] = jnp.zeros((levels, PAD, q_buf.shape[2]), jnp.float32)
        c_buf[:, PAD + lat_rows :, :] = jnp.zeros((levels, PAD, q_buf.shape[2]), jnp.float32)

    barrier = pltpu.get_barrier_semaphore()

    def flipped(bit):
        return wide + bit * (1 - 2 * ((wide // bit) % 2))

    bits = [2**k for k in range(n_wide.bit_length() - 1)]
    cube = [(wide, 1 - narrow)] + [(flipped(bit), narrow) for bit in bits]
    for other in cube:
        pl.semaphore_signal(barrier, inc=1, device_id=other, device_id_type=MESH)
    inner = (wide > 0) & (wide < n_wide - 1)

    @pl.when(inner)
    def _():
        pl.semaphore_signal(
            barrier, inc=1, device_id=(wide - 1 + 2 * (wide % 2), narrow), device_id_type=MESH
        )
        pl.semaphore_wait(barrier, len(cube) + 1)

    @pl.when(jnp.logical_not(inner))
    def _():
        pl.semaphore_wait(barrier, len(cube))

    def tell(stage):
        pl.semaphore_signal(entered.at[stage], inc=1, device_id=cube[stage], device_id_type=MESH)

    tell(1)

    def halo(at, up, which):
        lo, size = chunks[at]
        here, there = ((tracer, q_buf), (courant, c_buf))[which]
        count = HALO[up][which]
        first = lat_rows - count if up else 0
        land = PAD - count if up else PAD + lat_rows
        return pltpu.make_async_remote_copy(
            src_ref=here.at[:, pl.ds(first, count), pl.ds(lo, size)],
            dst_ref=there.at[:, pl.ds(land, count), pl.ds(lo, size)],
            send_sem=halo_send.at[at, up, which],
            recv_sem=halo_recv.at[at, up, which],
            device_id=(wide + 1 if up else wide - 1, narrow),
            device_id_type=MESH,
        )

    for at in range(len(chunks)):
        @pl.when(wide < n_wide - 1)
        def _(at=at):
            halo(at, 1, 0).start()
            halo(at, 1, 1).start()

        @pl.when(wide > 0)
        def _(at=at):
            halo(at, 0, 0).start()
            halo(at, 0, 1).start()

    leg_copy = pltpu.make_async_remote_copy(
        src_ref=legendre,
        dst_ref=leg.at[narrow],
        send_sem=leg_send,
        recv_sem=leg_recv.at[narrow],
        device_id=(wide, 1 - narrow),
        device_id_type=MESH,
    )
    leg_copy.start()

    for copy in smalls:
        copy.wait()
    row8, lane8 = ids((8, LANE), 0), ids((8, LANE), 1)
    for at in range(n_wide):
        wave = jnp.where(row8 < 2, band_s[2 * at], band_s[2 * at + 1])
        column = (row8 % 2) * wave_count + wave
        hit = (row8 < 4) & (lane8 % (2 * wave_count) == column)
        pick[8 * at : 8 * at + 8, :] = jnp.where(hit, 1.0, 0.0)
    for row in range(lat_rows):
        keep[row : row + 1, :] = jnp.full((1, LANE), nlon_s[row], jnp.int32)
    for row in range(owned):
        degree[row : row + 1, :] = jnp.full((1, LANE), owner_s[narrow * owned + row], jnp.int32)

    acc[...] = jnp.zeros_like(acc)
    row_total = levels * lat_rows
    for at, (lo, size) in enumerate(chunks):
        loads[at][0].wait()
        loads[at][1].wait()

        @pl.when(wide > 0)
        def _(at=at):
            halo(at, 1, 0).wait_recv()
            halo(at, 1, 1).wait_recv()

        @pl.when(wide < n_wide - 1)
        def _(at=at):
            halo(at, 0, 0).wait_recv()
            halo(at, 0, 1).wait_recv()

        @pl.when(wide == n_wide - 1)
        def _(lo=lo, size=size):
            last = PAD + lat_rows - 1
            c_buf[:, last : last + 1, lo : lo + size] = jnp.zeros((levels, 1, size), jnp.float32)

        def tile(step, carry, lo=lo, width=LANE):
            start = pl.multiple_of(lo + step * LANE, LANE)
            for level in range(levels):
                field = q_buf[level, :, pl.ds(start, width)]
                rate = c_buf[level, :, pl.ds(start, width)]
                ahead = rate >= 0.0
                twice = section(section(field, rate, ahead), rate, ahead)
                value = (field + twice)[PAD : PAD + lat_rows]
                high, low = split(value)
                first = level * lat_rows
                a_buf[first : first + lat_rows, pl.ds(start, width)] = high
                a_buf[row_total + first : row_total + first + lat_rows, pl.ds(start, width)] = low
            return carry

        whole = size // LANE
        lax.fori_loop(0, whole, tile, 0)
        depth = size
        if size % LANE:
            depth = (whole + 1) * LANE
            a_buf[:, lo + whole * LANE : lo + depth] = jnp.zeros((2 * row_total, LANE), jnp.bfloat16)
            tile(whole, 0, width=size % LANE)
        if at == 0:
            table_copy.wait()
        acc[...] += jnp.dot(
            a_buf[:, lo : lo + depth], t_buf[lo : lo + depth, :], preferred_element_type=jnp.float32
        )

        if at + 1 < len(cube):
            pl.semaphore_wait(entered.at[at + 1], 1)
            if at + 2 < len(cube):
                tell(at + 2)

    spectrum = acc[0:row_total, :] + acc[row_total : 2 * row_total, :]
    kept = 2 * (ids((lat_rows, LANE), 1) % wave_count) < keep[...]
    spectrum = jnp.where(jnp.concatenate([kept] * levels, axis=0), spectrum, 0.0)
    high, low = split(spectrum)
    chooser = pick[...].astype(jnp.bfloat16)
    last_dims = (((1,), (1,)), ((), ()))
    moved = lax.dot_general(chooser, high, last_dims, preferred_element_type=jnp.float32)
    moved = moved + lax.dot_general(chooser, low, last_dims, preferred_element_type=jnp.float32)
    for at in range(n_wide):
        sent[at] = moved[8 * at : 8 * at + 4, :]

    def fourier_copy(step):
        other = lax.rem(me + step, total)
        origin = lax.rem(me + total - step, total)
        to_wide, to_narrow = other // n_narrow, other % n_narrow
        return pltpu.make_async_remote_copy(
            src_ref=sent.at[to_wide],
            dst_ref=got.at[me],
            send_sem=four_send.at[step],
            recv_sem=four_recv.at[step],
            device_id=(to_wide, to_narrow),
            device_id_type=MESH,
        )

    def send(step, carry):
        fourier_copy(step).start()
        return carry

    lax.fori_loop(1, total, send, 0)
    own_part = pltpu.make_async_copy(sent.at[wide], got.at[me], four_recv.at[0])
    own_part.start()

    own_leg.wait()
    pltpu.make_async_remote_copy(
        src_ref=legendre,
        dst_ref=leg.at[1 - narrow],
        send_sem=leg_send,
        recv_sem=leg_recv.at[1 - narrow],
        device_id=(wide, 1 - narrow),
        device_id_type=MESH,
    ).wait_recv()

    degrees = degree[:, 0:wave_count]
    flat = ids((owned, wave_count), 1)
    held = 2 * (flat % half_waves) + flat // half_waves
    north, south = [], []
    for slot in range(n_narrow):
        wave = band_s[wide * n_narrow + slot]
        chosen = jnp.where((held == degrees) & (degrees >= wave), 1.0, 0.0)
        even = ((degrees + wave) % 2) == 0
        north.append(chosen.astype(jnp.bfloat16))
        south.append(jnp.where(even, chosen, -chosen).astype(jnp.bfloat16))
    parts = [split(leg[slot]) for slot in range(n_narrow)]
    block = n_narrow * owned

    def rows_of(picks):
        return jnp.concatenate(
            [
                jnp.dot(picks[slot], parts[slot][half], preferred_element_type=jnp.float32)
                for half in range(2)
                for slot in range(n_narrow)
            ],
            axis=0,
        )

    source, lane = ids((LANE, LANE), 0), ids((LANE, LANE), 1)
    lane_rows = ids((block, LANE), 1)
    tiles = leg.shape[2] // LANE
    for southern, picks in ((False, north), (True, south)):
        rows = rows_of(picks).astype(jnp.bfloat16)
        tall = jnp.concatenate([rows[:, LANE * a : LANE * a + LANE] for a in range(tiles)], axis=0)
        for half in range(2):
            within = lane % lat_rows
            if southern:
                within = lat_rows - 1 - within
            spread = jnp.where(source == half * lat_rows + within, 1.0, 0.0).astype(jnp.bfloat16)
            wide_rows = jnp.dot(tall, spread, preferred_element_type=jnp.float32)
            for a in range(tiles):
                lat_block = 2 * a + half
                if southern:
                    lat_block = n_wide - 1 - lat_block
                for part in range(2):
                    piece = wide_rows[(a * 2 + part) * block : (a * 2 + part + 1) * block]
                    for level in range(levels):
                        kept_piece = jnp.where(lane_rows // lat_rows == level, piece, 0.0)
                        first = (part * levels + level) * block
                        lx[first : first + block, LANE * lat_block : LANE * lat_block + LANE] = (
                            kept_piece.astype(jnp.bfloat16)
                        )

    lane1 = ids((1, LANE), 1)
    number = jnp.zeros((1, LANE), jnp.int32)
    for at in range(owned):
        number = jnp.where(lane1 % owned == at, owner_s[narrow * owned + at], number)
    squared = (number * (number + 1)).astype(jnp.float32)
    levels_all = levels * n_narrow
    damping = [1.0 / (1.0 + squared * rate_s[k]) for k in range(levels_all)]
    mix = [
        [
            sum((from_s[i, k] * to_s[k, l]) * damping[k] for k in range(levels_all))
            for l in range(levels_all)
        ]
        for i in range(levels_all)
    ]

    own_part.wait()

    def receive(step, carry):
        fourier_copy(step).wait_recv()
        return carry

    lax.fori_loop(1, total, receive, 0)
    for at in range(n_wide):
        values = jnp.concatenate([got[n_narrow * at + j] for j in range(n_narrow)], axis=0)
        high, low = split(values)
        xs[:, LANE * at : LANE * at + LANE] = jnp.concatenate([high, low], axis=0)
    product = lax.dot_general(xs[...], lx[...], last_dims, preferred_element_type=jnp.float32)
    product = product[0:8] + product[8:16]
    product = product + pltpu.roll(product, LANE // 2, 1)
    by_level = []
    for level in range(levels):
        moved = product if level == 0 else pltpu.roll(product, LANE - level * block, 1)
        by_level.append(jnp.where(lane8 < owned, moved, pltpu.roll(moved, 6, 0)))
    for c in range(2):
        for i in range(levels_all):
            result = jnp.zeros((1, LANE), jnp.float32)
            for n in range(n_narrow):
                for level in range(levels):
                    row = 4 * n + c
                    result = result + mix[i][levels * n + level] * by_level[level][row : row + 1]
            out[c, i, 0:1, :] = result[:, 0:owned]
            out[c, i, 1:2, :] = pltpu.roll(result, LANE - owned, 1)[:, 0:owned]

    def finish(step, carry):
        fourier_copy(step).wait_send()
        return carry

    lax.fori_loop(1, total, finish, 0)
    leg_copy.wait_send()
    for at in range(len(chunks)):
        @pl.when(wide < n_wide - 1)
        def _(at=at):
            halo(at, 1, 0).wait_send()
            halo(at, 1, 1).wait_send()

        @pl.when(wide > 0)
        def _(at=at):
            halo(at, 0, 0).wait_send()
            halo(at, 0, 1).wait_send()


def fused_fits(tracer, band_map, legendre, n_wide, n_narrow):
    levels, lat_rows, _ = tracer.shape
    waves = band_map.shape[0]
    return (
        levels == 2
        and n_narrow == 2
        and lat_rows * levels == LANE
        and waves == n_wide * n_narrow
        and n_wide & (n_wide - 1) == 0
        and n_wide.bit_length() <= len(CUTS) - 1
        and 4 * waves == LANE
        and legendre.shape[3] * 2 == n_wide * lat_rows
        and 2 * n_wide * 4 == LANE
    )


def fused(
    tracer, courant, nlon_counts, band_map, owner_map, legendre, modes_to, modes_from, mode_rates
):
    n_wide = lax.axis_size("wide")
    n_narrow = lax.axis_size("narrow")
    levels, lat_rows, lon_count = tracer.shape
    waves = band_map.shape[0]
    total = n_wide * n_narrow
    table = fourier_table(lon_count, waves)
    lon_pad = table.shape[0]
    chunk_count = len(CUTS) - 1
    tall = lat_rows + 2 * PAD
    half = legendre.shape[3]
    levels_all = levels * n_narrow
    vmem, smem, dma = pltpu.VMEM, pltpu.SMEM, pltpu.SemaphoreType.DMA
    operands = (
        tracer, courant, nlon_counts, band_map, owner_map,
        legendre.reshape(waves, half), modes_to, modes_from, mode_rates, jnp.asarray(table),
    )
    return pl.pallas_call(
        functools.partial(fused_kernel, n_wide, n_narrow, lon_count),
        out_shape=vmem((2, levels_all, 2, waves // n_narrow), jnp.float32),
        in_specs=[pl.BlockSpec(memory_space=pltpu.HBM)] * 10,
        out_specs=pl.BlockSpec(memory_space=pltpu.VMEM),
        scratch_shapes=[
            vmem((levels, tall, lon_count), jnp.float32),
            vmem((levels, tall, lon_count), jnp.float32),
            vmem((lon_pad, LANE), jnp.bfloat16),
            vmem((2 * levels * lat_rows, lon_pad), jnp.bfloat16),
            vmem((2 * levels * lat_rows, LANE), jnp.float32),
            vmem((n_narrow, waves, half), jnp.float32),
            smem((lat_rows,), jnp.int32),
            smem((waves,), jnp.int32),
            smem((waves,), jnp.int32),
            smem((levels_all, levels_all), jnp.float32),
            smem((levels_all, levels_all), jnp.float32),
            smem((levels_all,), jnp.float32),
            vmem((8 * n_wide, LANE), jnp.float32),
            vmem((lat_rows, LANE), jnp.int32),
            vmem((waves // n_narrow, LANE), jnp.int32),
            vmem((n_wide, 4, LANE), jnp.float32),
            vmem((total, 4, LANE), jnp.float32),
            vmem((LANE, n_wide * LANE), jnp.bfloat16),
            vmem((16, n_wide * LANE), jnp.bfloat16),
            dma((6,)),
            dma((chunk_count, 2)),
            dma,
            dma((chunk_count, 2, 2)),
            dma((chunk_count, 2, 2)),
            dma,
            dma((n_narrow,)),
            dma((total,)),
            dma((total,)),
            pltpu.SemaphoreType.REGULAR((total.bit_length(),)),
        ],
        compiler_params=pltpu.CompilerParams(
            collective_id=0, has_side_effects=True
        ),
    )(*(pltpu.with_memory_space_constraint(operand, pltpu.HBM) for operand in operands))


def program(tracer, courant, nlon_counts, band_map, owner_map, legendre, *modes):
    choose = (
        fused
        if fused_fits(
            tracer, band_map, legendre, lax.axis_size("wide"), lax.axis_size("narrow")
        )
        else body
    )
    return choose(tracer, courant, nlon_counts, band_map, owner_map, legendre, *modes)


def solution(mesh):
    placed = (
        P("narrow", "wide", None),
        P("narrow", "wide", None),
        P("wide"),
        P(),
        P(),
        P(("wide", "narrow"), None, None, None),
        P(),
        P(),
        P(),
    )
    return jax.shard_map(
        program, mesh=mesh, in_specs=placed, out_specs=P(None, None, "wide", "narrow"), check_vma=False
    )
```

```python
import functools
import math

import jax
import jax.numpy as jnp
import numpy as np
from jax import lax
from jax.experimental import pallas as pl
from jax.experimental.pallas import tpu as pltpu
from jax.sharding import PartitionSpec as P

NLAT = 1024


def extended(array, sides, width):
    for axis, dim in sides:
        devices, length = (lax.axis_size(axis), array.shape[dim])
        up = [(i, (i + 1) % devices) for i in range(devices - 1)]
        down = [(j, i) for i, j in up]
        last = lax.slice_in_dim(array, length - width, length, axis=dim)
        initial = lax.slice_in_dim(array, 0, width, axis=dim)
        before = lax.ppermute(last, axis, up)
        after = lax.ppermute(initial, axis, down)
        array = jnp.concatenate([before, array, after], axis=dim)
    return array


def advect_section(field_ext, rate_ext, open_faces):
    row_total = field_ext.shape[1]
    row_below = field_ext[:, 0 : row_total - 3]
    row_here = field_ext[:, 1 : row_total - 2]
    row_above = field_ext[:, 2 : row_total - 1]
    row_beyond = field_ext[:, 3:row_total]
    face_rate = rate_ext[:, 1 : row_total - 2] * open_faces[1 : row_total - 2][:, None]
    upwind = (5.0 * row_here + 2.0 * row_above - row_below) / 6.0
    downwind = (5.0 * row_above + 2.0 * row_here - row_beyond) / 6.0
    low_bound = jnp.minimum(row_here, row_above)
    high_bound = jnp.maximum(row_here, row_above)
    face_value = jnp.clip(jnp.where(face_rate >= 0.0, upwind, downwind), low_bound, high_bound)
    face_flux = face_rate * face_value
    return field_ext[:, 2 : row_total - 2] - (face_flux[:, 1:] - face_flux[:, :-1])


def valid_rows(first_row, lat_rows, rim_width):
    row_ids = first_row + jnp.arange(lat_rows + 2 * rim_width, dtype=jnp.int32) - rim_width
    return ((row_ids >= 0) & (row_ids < NLAT - 1)).astype(jnp.float32)


def longitude_transform(advected, wave_count):
    levels_dev, lat_rows, lon_count = advected.shape
    short_len = 32
    long_len = lon_count // short_len
    block_count = wave_count // short_len
    row_count = levels_dev * lat_rows
    grid_rows = advected.reshape(row_count, short_len, long_len)
    short_ids = jnp.arange(short_len, dtype=jnp.int32)
    turn_one = short_ids[:, None] * short_ids[None, :] % short_len
    angle_one = 2.0 * math.pi / short_len * turn_one.astype(jnp.float32)
    highest = lax.Precision.HIGHEST
    inner_re = jnp.einsum("pab,ar->prb", grid_rows, jnp.cos(angle_one), precision=highest)
    inner_im = -jnp.einsum("pab,ar->prb", grid_rows, jnp.sin(angle_one), precision=highest)
    long_ids = jnp.arange(long_len, dtype=jnp.int32)
    block_ids = jnp.arange(block_count, dtype=jnp.int32)
    wave_ids = short_len * block_ids[None, None, :] + short_ids[:, None, None]
    turn_two = wave_ids * long_ids[None, :, None] % lon_count
    angle_two = 2.0 * math.pi / lon_count * turn_two.astype(jnp.float32)
    cos_two = jnp.cos(angle_two)
    sin_two = jnp.sin(angle_two)
    outer_re = jnp.einsum("prb,rbc->crp", inner_re, cos_two, precision=highest) + jnp.einsum(
        "prb,rbc->crp", inner_im, sin_two, precision=highest
    )
    outer_im = jnp.einsum("prb,rbc->crp", inner_im, cos_two, precision=highest) - jnp.einsum(
        "prb,rbc->crp", inner_re, sin_two, precision=highest
    )
    outer_re = (outer_re / math.sqrt(lon_count)).reshape(wave_count, levels_dev, lat_rows)
    outer_im = (outer_im / math.sqrt(lon_count)).reshape(wave_count, levels_dev, lat_rows)
    return jnp.stack([outer_re, outer_im], axis=1)


def body(
    tracer, courant, nlon_counts, band_map, owner_map, legendre, modes_to, modes_from, mode_rates
):
    levels_dev = tracer.shape[0]
    lat_rows = tracer.shape[1]
    n_wide = lax.axis_size("wide")
    n_narrow = lax.axis_size("narrow")
    first_row = lax.axis_index("wide") * lat_rows
    stacked = jnp.stack([tracer, courant])
    padded = extended(stacked, (("wide", 2),), 4)
    open_faces = valid_rows(first_row, lat_rows, 4)
    section_one = advect_section(padded[0], padded[1], open_faces)
    section_two = advect_section(section_one, padded[1][:, 2:-2], open_faces[2:-2])
    advected = 0.5 * tracer + 0.5 * section_two
    wave_count = band_map.shape[0]
    fourier = longitude_transform(advected, wave_count)
    wave_ids = jnp.arange(wave_count, dtype=jnp.int32)
    kept_mask = (2 * wave_ids[:, None] < nlon_counts[None, :]).astype(jnp.float32)
    fourier = fourier * kept_mask[:, None, None, :]
    slot_count = wave_count // (n_wide * n_narrow)
    fourier = jnp.einsum(
        "sm,mclj->sclj", (band_map[:, None] == wave_ids[None, :]).astype(jnp.float32), fourier,
        precision=lax.Precision.HIGHEST,
    )
    fourier = lax.all_to_all(fourier, "wide", split_axis=0, concat_axis=3, tiled=True)
    fourier = lax.all_to_all(fourier, "narrow", split_axis=0, concat_axis=2, tiled=True)
    levels_all = levels_dev * n_narrow
    half_rows = fourier.shape[3] // 2
    north_half = fourier[:, :, :, :half_rows]
    south_half = jnp.flip(fourier[:, :, :, half_rows:], axis=3)
    sym_part = north_half + south_half
    anti_part = north_half - south_half
    slot_start = (lax.axis_index("wide") * n_narrow + lax.axis_index("narrow")) * slot_count
    slot_waves = lax.dynamic_slice_in_dim(band_map, slot_start, slot_count)
    same_parity = (jnp.arange(2, dtype=jnp.int32)[None, :] - slot_waves[:, None]) % 2 == 0
    chosen = jnp.where(same_parity[:, :, None, None, None], sym_part[:, None], anti_part[:, None])
    spectral = jnp.einsum("spkj,spclj->spkcl", legendre, chosen, precision=lax.Precision.HIGHEST)
    degree_ids = (
        2 * jnp.arange(wave_count // 2, dtype=jnp.int32)[None, :]
        + jnp.arange(2, dtype=jnp.int32)[:, None]
    )
    upper_mask = (degree_ids[None] >= slot_waves[:, None, None]).astype(jnp.float32)
    spectral = spectral * upper_mask[:, :, :, None, None]
    spectral = jnp.transpose(spectral, (0, 2, 1, 3, 4)).reshape(
        slot_count, wave_count, 2, levels_all
    )
    spectral = jnp.einsum(
        "tn,sncl->stcl", (owner_map[:, None] == wave_ids[None, :]).astype(jnp.float32), spectral,
        precision=lax.Precision.HIGHEST,
    )
    gathered = lax.all_to_all(spectral, "narrow", split_axis=1, concat_axis=0, tiled=True)
    owned = gathered.shape[1]
    owned_degrees = lax.dynamic_slice_in_dim(owner_map, lax.axis_index("narrow") * owned, owned)
    degree_sq = (owned_degrees * (owned_degrees + 1)).astype(jnp.float32)
    damping = 1.0 / (1.0 + degree_sq[None, :] * mode_rates[:, None])
    modal_part = jnp.einsum("kl,stcl->kstc", modes_to, gathered, precision=lax.Precision.HIGHEST)
    scaled = modal_part * damping[:, None, :, None]
    return jnp.einsum("ik,kstc->cist", modes_from, scaled, precision=lax.Precision.HIGHEST)


MESH = pl.DeviceIdType.MESH
LANE = 128
PAD = 8
RIM = 4
CHUNKS = 4
EDGE = 512
GROUPS = 2
HALO = {1: (4, 3), 0: (4, 2)}


def chunk_list(lon_count, count):
    tiles = -(-lon_count // LANE)
    cuts = [min(lon_count, LANE * (tiles * cut // count)) for cut in range(count + 1)]
    return [(lo, hi - lo) for lo, hi in zip(cuts, cuts[1:])]


def fourier_table(lon_count, wave_count):
    rows = -(-lon_count // LANE) * LANE
    turns = np.outer(np.arange(lon_count), np.arange(wave_count)) % lon_count
    angle = 2.0 * np.pi / lon_count * turns
    full = np.concatenate([np.cos(angle), -np.sin(angle)], axis=1) * (0.5 / np.sqrt(lon_count))
    high = full.astype(jnp.bfloat16)
    low = (full - high.astype(np.float64)).astype(jnp.bfloat16)
    table = np.zeros((rows, LANE), jnp.bfloat16)
    table[:lon_count] = np.concatenate([high, low], axis=1)
    return table


def split(value):
    high = value.astype(jnp.bfloat16)
    low = (value - high.astype(jnp.float32)).astype(jnp.bfloat16)
    return high, low


def section(field, rate, ahead):
    rows = field.shape[0]
    above = pltpu.roll(field, rows - 1, 0)
    step = above - field
    near = jnp.where(ahead, pltpu.roll(step, 1, 0), pltpu.roll(step, rows - 1, 0))
    slope = step * (1.0 / 3.0) + near * (1.0 / 6.0)
    slope = jnp.maximum(jnp.minimum(slope, jnp.maximum(step, 0.0)), jnp.minimum(step, 0.0))
    flux = rate * jnp.where(ahead, field + slope, above - slope)
    return field - (flux - pltpu.roll(flux, 1, 0))


def ids(shape, dim):
    return lax.broadcasted_iota(jnp.int32, shape, dim)


def fused_kernel(
    n_wide, n_narrow, lon_count,
    tracer, courant, nlon, band, owner, legendre, modes_to, modes_from, rates, table,
    out,
    q_buf, c_buf, t_buf, a_buf, e_buf, acc, spec, leg, nlon_s, band_s, owner_s, to_s, from_s, rate_s,
    pick, keep, degree, sent, got, lx, xs,
    small_sem, load_sem, table_sem, halo_send, halo_recv, leg_send, leg_recv, four_send, four_recv,
    entered,
):
    wide, narrow = lax.axis_index("wide"), lax.axis_index("narrow")
    total = n_wide * n_narrow
    me = wide * n_narrow + narrow
    levels, lat_rows = tracer.shape[0], tracer.shape[1]
    wave_count = band_s.shape[0]
    lon_pad = t_buf.shape[0]
    chunks = chunk_list(lon_count, CHUNKS)
    groups = chunk_list(lon_count, GROUPS)
    owned = wave_count // n_narrow
    half_waves = wave_count // 2
    row_total = levels * lat_rows

    barrier = pltpu.get_barrier_semaphore()

    def flipped(bit):
        return wide + bit * (1 - 2 * ((wide // bit) % 2))

    bits = [2**k for k in range(n_wide.bit_length() - 1)]
    cube = [(wide, 1 - narrow)] + [(flipped(bit), narrow) for bit in bits]
    for other in cube:
        pl.semaphore_signal(barrier, inc=1, device_id=other, device_id_type=MESH)
    inner = (wide > 0) & (wide < n_wide - 1)

    @pl.when(inner)
    def _():
        pl.semaphore_signal(
            barrier, inc=1, device_id=(wide - 1 + 2 * (wide % 2), narrow), device_id_type=MESH
        )

    smalls = []
    for at, (here, there) in enumerate(
        ((nlon, nlon_s), (band, band_s), (owner, owner_s), (modes_to, to_s), (modes_from, from_s), (rates, rate_s))
    ):
        smalls.append(pltpu.make_async_copy(here, there, small_sem.at[at]))
    for copy in smalls:
        copy.start()
    loads = []
    for at, (lo, size) in enumerate(chunks):
        pair = []
        for which, (here, there) in enumerate(((tracer, q_buf), (courant, c_buf))):
            copy = pltpu.make_async_copy(
                here.at[:, :, pl.ds(lo, size)],
                there.at[:, pl.ds(PAD, lat_rows), pl.ds(lo, size)],
                load_sem.at[at, which],
            )
            copy.start()
            pair.append(copy)
        loads.append(pair)
    table_copy = pltpu.make_async_copy(table, t_buf, table_sem)
    table_copy.start()
    own_leg = pltpu.make_async_copy(legendre, leg.at[narrow], leg_recv.at[narrow])
    own_leg.start()

    @pl.when(wide == 0)
    def _():
        q_buf[:, 0:PAD, :] = jnp.zeros((levels, PAD, lon_count), jnp.float32)
        c_buf[:, 0:PAD, :] = jnp.zeros((levels, PAD, lon_count), jnp.float32)

    @pl.when(wide == n_wide - 1)
    def _():
        q_buf[:, PAD + lat_rows :, :] = jnp.zeros((levels, PAD, lon_count), jnp.float32)
        c_buf[:, PAD + lat_rows :, :] = jnp.zeros((levels, PAD, lon_count), jnp.float32)

    @pl.when(inner)
    def _():
        pl.semaphore_wait(barrier, len(cube) + 1)

    @pl.when(jnp.logical_not(inner))
    def _():
        pl.semaphore_wait(barrier, len(cube))

    def tell(stage):
        pl.semaphore_signal(entered.at[stage], inc=1, device_id=cube[stage], device_id_type=MESH)

    tell(1)

    def halo(group, up, which):
        lo, size = groups[group]
        here, there = ((tracer, q_buf), (courant, c_buf))[which]
        count = HALO[up][which]
        first = lat_rows - count if up else 0
        land = PAD - count if up else PAD + lat_rows
        return pltpu.make_async_remote_copy(
            src_ref=here.at[:, pl.ds(first, count), pl.ds(lo, size)],
            dst_ref=there.at[:, pl.ds(land, count), pl.ds(lo, size)],
            send_sem=halo_send.at[group, up, which],
            recv_sem=halo_recv.at[group, up, which],
            device_id=(wide + 1 if up else wide - 1, narrow),
            device_id_type=MESH,
        )

    odd = wide % 2 == 1

    def halo_step(group, up, what, cond):
        @pl.when(cond)
        def _():
            for which in range(2):
                getattr(halo(group, up, which), what)()

    for group in range(GROUPS):
        halo_step(group, 1, "start", odd & (wide < n_wide - 1))
        halo_step(group, 0, "start", jnp.logical_not(odd) & (wide > 0))
    for group in range(GROUPS):
        halo_step(group, 0, "start", odd)
        halo_step(group, 1, "start", jnp.logical_not(odd))

    leg_copy = pltpu.make_async_remote_copy(
        src_ref=legendre,
        dst_ref=leg.at[narrow],
        send_sem=leg_send,
        recv_sem=leg_recv.at[narrow],
        device_id=(wide, 1 - narrow),
        device_id_type=MESH,
    )
    leg_copy.start()

    for copy in smalls:
        copy.wait()
    row8, lane8 = ids((8, LANE), 0), ids((8, LANE), 1)
    for at in range(n_wide):
        wave = jnp.where(row8 < 2, band_s[2 * at], band_s[2 * at + 1])
        column = (row8 % 2) * wave_count + wave
        hit = (row8 < 4) & (lane8 % (2 * wave_count) == column)
        pick[8 * at : 8 * at + 8, :] = jnp.where(hit, 1.0, 0.0)
    for row in range(lat_rows):
        keep[row : row + 1, :] = jnp.full((1, LANE), nlon_s[row], jnp.int32)
    for row in range(owned):
        degree[row : row + 1, :] = jnp.full((1, LANE), owner_s[narrow * owned + row], jnp.int32)

    acc[...] = jnp.zeros_like(acc)
    a_buf[:, lon_pad - LANE :] = jnp.zeros((2 * row_total, LANE), jnp.bfloat16)
    e_buf[:, lon_pad - LANE :] = jnp.zeros((2 * levels * PAD, LANE), jnp.bfloat16)
    width = lon_pad // CHUNKS
    for at in range(CHUNKS):
        loads[at][0].wait()
        loads[at][1].wait()

        def tile(step, carry, lo=at * width, lanes=LANE):
            columns = pl.ds(pl.multiple_of(lo + step * LANE, LANE), lanes)
            for level in range(levels):
                field = q_buf[level, PAD : PAD + lat_rows, columns]
                rate = c_buf[level, PAD : PAD + lat_rows, columns]
                ahead = rate >= 0.0
                twice = section(section(field, rate, ahead), rate, ahead)
                high, low = split(field + twice)
                first = level * lat_rows
                a_buf[first : first + lat_rows, columns] = high
                a_buf[row_total + first : row_total + first + lat_rows, columns] = low
            return carry

        whole, rest = divmod(chunks[at][1], LANE)
        lax.fori_loop(0, whole, tile, 0)
        if rest:
            tile(whole, 0, lanes=rest)
        if at == 0:
            table_copy.wait()
        columns = pl.ds(at * width, width)
        acc[...] += jnp.dot(
            a_buf[:, columns], t_buf[columns, :], preferred_element_type=jnp.float32
        )

        if at + 1 < len(cube):
            pl.semaphore_wait(entered.at[at + 1], 1)
            if at + 2 < len(cube):
                tell(at + 2)

    spectrum = acc[0:row_total, :] + acc[row_total : 2 * row_total, :]
    kept = 2 * (ids((lat_rows, LANE), 1) % wave_count) < keep[...]
    spec[...] = jnp.where(jnp.concatenate([kept] * levels, axis=0), spectrum, 0.0)

    @pl.when(wide == n_wide - 1)
    def _():
        last = PAD + lat_rows - 1
        c_buf[:, last : last + 1, :] = jnp.zeros((levels, 1, lon_count), jnp.float32)

    own_leg.wait()
    pltpu.make_async_remote_copy(
        src_ref=legendre,
        dst_ref=leg.at[1 - narrow],
        send_sem=leg_send,
        recv_sem=leg_recv.at[1 - narrow],
        device_id=(wide, 1 - narrow),
        device_id_type=MESH,
    ).wait_recv()

    degrees = degree[:, 0:wave_count]
    flat = ids((owned, wave_count), 1)
    held = 2 * (flat % half_waves) + flat // half_waves
    north, south = [], []
    for slot in range(n_narrow):
        wave = band_s[wide * n_narrow + slot]
        chosen = jnp.where((held == degrees) & (degrees >= wave), 1.0, 0.0)
        even = ((degrees + wave) % 2) == 0
        north.append(chosen.astype(jnp.bfloat16))
        south.append(jnp.where(even, chosen, -chosen).astype(jnp.bfloat16))
    leg_parts = [split(leg[slot]) for slot in range(n_narrow)]
    block = n_narrow * owned

    def rows_of(picks):
        return jnp.concatenate(
            [
                jnp.dot(picks[slot], leg_parts[slot][half], preferred_element_type=jnp.float32)
                for half in range(2)
                for slot in range(n_narrow)
            ],
            axis=0,
        )

    source, lane = ids((LANE, LANE), 0), ids((LANE, LANE), 1)
    lane_rows = ids((block, LANE), 1)
    tiles = leg.shape[2] // LANE
    for southern, picks in ((False, north), (True, south)):
        rows = rows_of(picks).astype(jnp.bfloat16)
        tall = jnp.concatenate([rows[:, LANE * a : LANE * a + LANE] for a in range(tiles)], axis=0)
        for half in range(2):
            within = lane % lat_rows
            if southern:
                within = lat_rows - 1 - within
            spread = jnp.where(source == half * lat_rows + within, 1.0, 0.0).astype(jnp.bfloat16)
            wide_rows = jnp.dot(tall, spread, preferred_element_type=jnp.float32)
            for a in range(tiles):
                lat_block = 2 * a + half
                if southern:
                    lat_block = n_wide - 1 - lat_block
                for part in range(2):
                    piece = wide_rows[(a * 2 + part) * block : (a * 2 + part + 1) * block]
                    for level in range(levels):
                        kept_piece = jnp.where(lane_rows // lat_rows == level, piece, 0.0)
                        first = (part * levels + level) * block
                        lx[first : first + block, LANE * lat_block : LANE * lat_block + LANE] = (
                            kept_piece.astype(jnp.bfloat16)
                        )

    lane1 = ids((1, LANE), 1)
    number = jnp.zeros((1, LANE), jnp.int32)
    for at in range(owned):
        number = jnp.where(lane1 % owned == at, owner_s[narrow * owned + at], number)
    squared = (number * (number + 1)).astype(jnp.float32)
    levels_all = levels * n_narrow
    damping = [1.0 / (1.0 + squared * rate_s[k]) for k in range(levels_all)]
    mix = [
        [
            sum((from_s[i, k] * to_s[k, l]) * damping[k] for k in range(levels_all))
            for l in range(levels_all)
        ]
        for i in range(levels_all)
    ]

    last_dims = (((1,), (1,)), ((), ()))

    def edge(group, top):
        lo = group * (lon_pad // GROUPS)
        start = pl.multiple_of(jnp.where(top, 0, lat_rows), 8)

        def strip(step, carry, lanes=EDGE):
            columns = pl.ds(pl.multiple_of(lo + step * EDGE, EDGE), lanes)
            rims = []
            for level in range(levels):
                field = q_buf[level, pl.ds(start, 2 * PAD), columns]
                rate = c_buf[level, pl.ds(start, 2 * PAD), columns]
                ahead = rate >= 0.0
                value = field + section(section(field, rate, ahead), rate, ahead)
                rims.append(jnp.where(top, value[PAD:], value[:PAD]))
            high, low = split(jnp.concatenate(rims, axis=0))
            e_buf[0 : levels * PAD, columns] = high
            e_buf[levels * PAD : 2 * levels * PAD, columns] = low
            return carry

        whole, rest = divmod(groups[group][1], EDGE)
        lax.fori_loop(0, whole, strip, 0)
        if rest:
            strip(whole, 0, lanes=rest)
        columns = pl.ds(lo, lon_pad // GROUPS)
        return jnp.dot(
            e_buf[:, columns], t_buf[columns, :], preferred_element_type=jnp.float32
        )

    def rim_rows(parts, top):
        rows = sum(parts)
        rows = rows[0 : levels * PAD] + rows[levels * PAD :]
        first = pl.multiple_of(jnp.where(top, 0, lat_rows - PAD), 8)
        fresh = jnp.where(top, row8, PAD - 1 - row8) < RIM
        cover = 2 * (lane8 % wave_count) < keep[pl.ds(first, PAD), :]
        for level in range(levels):
            place = pl.ds(pl.multiple_of(level * lat_rows + first, 8), PAD)
            mine = jnp.where(cover, rows[level * PAD : level * PAD + PAD], 0.0)
            spec[place, :] = jnp.where(fresh, mine, spec[place, :])

    parts = []
    for group in range(GROUPS):
        halo_step(group, 1, "wait_recv", odd)
        halo_step(group, 0, "wait_recv", jnp.logical_not(odd))
        parts.append(edge(group, odd))
    rim_rows(parts, odd)
    parts = []
    for group in range(GROUPS):
        halo_step(group, 0, "wait_recv", odd & (wide < n_wide - 1))
        halo_step(group, 1, "wait_recv", jnp.logical_not(odd) & (wide > 0))
        parts.append(edge(group, jnp.logical_not(odd)))
    rim_rows(parts, jnp.logical_not(odd))

    high, low = split(spec[...])
    chooser = pick[...].astype(jnp.bfloat16)
    moved = lax.dot_general(chooser, high, last_dims, preferred_element_type=jnp.float32)
    moved = moved + lax.dot_general(chooser, low, last_dims, preferred_element_type=jnp.float32)
    for at in range(n_wide):
        sent[at] = moved[8 * at : 8 * at + 4, :]

    turns = [1 - 2 * ((wide // bit) % 2) for bit in bits]

    def fourier_copy(code):
        to_wide = wide
        for bit, turn in zip(bits, turns):
            if code // n_narrow & bit:
                to_wide = to_wide + bit * turn
        to_narrow = 1 - narrow if code % n_narrow else narrow
        return pltpu.make_async_remote_copy(
            src_ref=sent.at[to_wide],
            dst_ref=got.at[me],
            send_sem=four_send,
            recv_sem=four_recv,
            device_id=(to_wide, to_narrow),
            device_id_type=MESH,
        )

    for code in range(total - 1, 0, -1):
        fourier_copy(code).start()
    got[me] = sent[wide]

    others = got.at[pl.ds(0, total - 1)]
    pltpu.make_async_copy(others, others, four_recv).wait()
    for at in range(n_wide):
        values = jnp.concatenate([got[n_narrow * at + j] for j in range(n_narrow)], axis=0)
        high, low = split(values)
        xs[:, LANE * at : LANE * at + LANE] = jnp.concatenate([high, low], axis=0)
    product = lax.dot_general(xs[...], lx[...], last_dims, preferred_element_type=jnp.float32)
    product = product[0:8] + product[8:16]
    product = product + pltpu.roll(product, LANE // 2, 1)
    by_level = []
    for level in range(levels):
        moved = product if level == 0 else pltpu.roll(product, LANE - level * block, 1)
        by_level.append(jnp.where(lane8 < owned, moved, pltpu.roll(moved, 6, 0)))
    for c in range(2):
        for i in range(levels_all):
            result = jnp.zeros((1, LANE), jnp.float32)
            for n in range(n_narrow):
                for level in range(levels):
                    row = 4 * n + c
                    result = result + mix[i][levels * n + level] * by_level[level][row : row + 1]
            out[c, i, 0:1, :] = result[:, 0:owned]
            out[c, i, 1:2, :] = pltpu.roll(result, LANE - owned, 1)[:, 0:owned]

    pltpu.make_async_copy(others, others, four_send).wait()
    leg_copy.wait_send()
    for group in range(GROUPS):
        halo_step(group, 1, "wait_send", wide < n_wide - 1)
        halo_step(group, 0, "wait_send", wide > 0)


def fused_fits(tracer, band_map, legendre, n_wide, n_narrow):
    levels, lat_rows = tracer.shape[0], tracer.shape[1]
    waves = band_map.shape[0]
    return (
        levels == 2
        and n_narrow == 2
        and lat_rows * levels == LANE
        and waves == n_wide * n_narrow
        and n_wide & (n_wide - 1) == 0
        and n_wide.bit_length() <= CHUNKS + 1
        and -(-tracer.shape[2] // LANE) * LANE % (GROUPS * EDGE) == 0
        and -(-tracer.shape[2] // LANE) % CHUNKS == 0
        and 4 * waves == LANE
        and legendre.shape[3] * 2 == n_wide * lat_rows
        and 2 * n_wide * 4 == LANE
    )


def fused(
    tracer, courant, nlon_counts, band_map, owner_map, legendre, modes_to, modes_from, mode_rates
):
    n_wide = lax.axis_size("wide")
    n_narrow = lax.axis_size("narrow")
    levels, lat_rows, lon_count = tracer.shape
    waves = band_map.shape[0]
    total = n_wide * n_narrow
    table = fourier_table(lon_count, waves)
    lon_pad = table.shape[0]
    tall = lat_rows + 2 * PAD
    half = legendre.shape[3]
    levels_all = levels * n_narrow
    vmem, smem, dma = pltpu.VMEM, pltpu.SMEM, pltpu.SemaphoreType.DMA
    operands = (
        tracer, courant, nlon_counts, band_map, owner_map,
        legendre.reshape(waves, half), modes_to, modes_from, mode_rates, jnp.asarray(table),
    )
    return pl.pallas_call(
        functools.partial(fused_kernel, n_wide, n_narrow, lon_count),
        out_shape=vmem((2, levels_all, 2, waves // n_narrow), jnp.float32),
        in_specs=[pl.BlockSpec(memory_space=pltpu.HBM)] * 10,
        out_specs=pl.BlockSpec(memory_space=pltpu.VMEM),
        scratch_shapes=[
            vmem((levels, tall, lon_count), jnp.float32),
            vmem((levels, tall, lon_count), jnp.float32),
            vmem((lon_pad, LANE), jnp.bfloat16),
            vmem((2 * levels * lat_rows, lon_pad), jnp.bfloat16),
            vmem((2 * levels * PAD, lon_pad), jnp.bfloat16),
            vmem((2 * levels * lat_rows, LANE), jnp.float32),
            vmem((levels * lat_rows, LANE), jnp.float32),
            vmem((n_narrow, waves, half), jnp.float32),
            smem((lat_rows,), jnp.int32),
            smem((waves,), jnp.int32),
            smem((waves,), jnp.int32),
            smem((levels_all, levels_all), jnp.float32),
            smem((levels_all, levels_all), jnp.float32),
            smem((levels_all,), jnp.float32),
            vmem((8 * n_wide, LANE), jnp.float32),
            vmem((lat_rows, LANE), jnp.int32),
            vmem((waves // n_narrow, LANE), jnp.int32),
            vmem((n_wide, 4, LANE), jnp.float32),
            vmem((total, 4, LANE), jnp.float32),
            vmem((LANE, n_wide * LANE), jnp.bfloat16),
            vmem((16, n_wide * LANE), jnp.bfloat16),
            dma((6,)),
            dma((CHUNKS, 2)),
            dma,
            dma((GROUPS, 2, 2)),
            dma((GROUPS, 2, 2)),
            dma,
            dma((n_narrow,)),
            dma,
            dma,
            pltpu.SemaphoreType.REGULAR((total.bit_length(),)),
        ],
        compiler_params=pltpu.CompilerParams(
            collective_id=0, has_side_effects=True
        ),
    )(*(pltpu.with_memory_space_constraint(operand, pltpu.HBM) for operand in operands))


def program(tracer, courant, nlon_counts, band_map, owner_map, legendre, *modes):
    choose = (
        fused
        if fused_fits(
            tracer, band_map, legendre, lax.axis_size("wide"), lax.axis_size("narrow")
        )
        else body
    )
    return choose(tracer, courant, nlon_counts, band_map, owner_map, legendre, *modes)


def solution(mesh):
    placed = (
        P("narrow", "wide", None),
        P("narrow", "wide", None),
        P("wide"),
        P(),
        P(),
        P(("wide", "narrow"), None, None, None),
        P(),
        P(),
        P(),
    )
    return jax.shard_map(
        program, mesh=mesh, in_specs=placed, out_specs=P(None, None, "wide", "narrow"), check_vma=False
    )
```

```python
import functools
import math

import jax
import jax.numpy as jnp
import numpy as np
from jax import lax
from jax.experimental import pallas as pl
from jax.experimental.pallas import tpu as pltpu
from jax.sharding import PartitionSpec as P

NLAT = 1024


def extended(array, sides, width):
    for axis, dim in sides:
        devices, length = (lax.axis_size(axis), array.shape[dim])
        up = [(i, (i + 1) % devices) for i in range(devices - 1)]
        down = [(j, i) for i, j in up]
        last = lax.slice_in_dim(array, length - width, length, axis=dim)
        initial = lax.slice_in_dim(array, 0, width, axis=dim)
        before = lax.ppermute(last, axis, up)
        after = lax.ppermute(initial, axis, down)
        array = jnp.concatenate([before, array, after], axis=dim)
    return array


def advect_section(field_ext, rate_ext, open_faces):
    row_total = field_ext.shape[1]
    row_below = field_ext[:, 0 : row_total - 3]
    row_here = field_ext[:, 1 : row_total - 2]
    row_above = field_ext[:, 2 : row_total - 1]
    row_beyond = field_ext[:, 3:row_total]
    face_rate = rate_ext[:, 1 : row_total - 2] * open_faces[1 : row_total - 2][:, None]
    upwind = (5.0 * row_here + 2.0 * row_above - row_below) / 6.0
    downwind = (5.0 * row_above + 2.0 * row_here - row_beyond) / 6.0
    low_bound = jnp.minimum(row_here, row_above)
    high_bound = jnp.maximum(row_here, row_above)
    face_value = jnp.clip(jnp.where(face_rate >= 0.0, upwind, downwind), low_bound, high_bound)
    face_flux = face_rate * face_value
    return field_ext[:, 2 : row_total - 2] - (face_flux[:, 1:] - face_flux[:, :-1])


def valid_rows(first_row, lat_rows, rim_width):
    row_ids = first_row + jnp.arange(lat_rows + 2 * rim_width, dtype=jnp.int32) - rim_width
    return ((row_ids >= 0) & (row_ids < NLAT - 1)).astype(jnp.float32)


def longitude_transform(advected, wave_count):
    levels_dev, lat_rows, lon_count = advected.shape
    short_len = 32
    long_len = lon_count // short_len
    block_count = wave_count // short_len
    row_count = levels_dev * lat_rows
    grid_rows = advected.reshape(row_count, short_len, long_len)
    short_ids = jnp.arange(short_len, dtype=jnp.int32)
    turn_one = short_ids[:, None] * short_ids[None, :] % short_len
    angle_one = 2.0 * math.pi / short_len * turn_one.astype(jnp.float32)
    highest = lax.Precision.HIGHEST
    inner_re = jnp.einsum("pab,ar->prb", grid_rows, jnp.cos(angle_one), precision=highest)
    inner_im = -jnp.einsum("pab,ar->prb", grid_rows, jnp.sin(angle_one), precision=highest)
    long_ids = jnp.arange(long_len, dtype=jnp.int32)
    block_ids = jnp.arange(block_count, dtype=jnp.int32)
    wave_ids = short_len * block_ids[None, None, :] + short_ids[:, None, None]
    turn_two = wave_ids * long_ids[None, :, None] % lon_count
    angle_two = 2.0 * math.pi / lon_count * turn_two.astype(jnp.float32)
    cos_two = jnp.cos(angle_two)
    sin_two = jnp.sin(angle_two)
    outer_re = jnp.einsum("prb,rbc->crp", inner_re, cos_two, precision=highest) + jnp.einsum(
        "prb,rbc->crp", inner_im, sin_two, precision=highest
    )
    outer_im = jnp.einsum("prb,rbc->crp", inner_im, cos_two, precision=highest) - jnp.einsum(
        "prb,rbc->crp", inner_re, sin_two, precision=highest
    )
    outer_re = (outer_re / math.sqrt(lon_count)).reshape(wave_count, levels_dev, lat_rows)
    outer_im = (outer_im / math.sqrt(lon_count)).reshape(wave_count, levels_dev, lat_rows)
    return jnp.stack([outer_re, outer_im], axis=1)


def body(
    tracer, courant, nlon_counts, band_map, owner_map, legendre, modes_to, modes_from, mode_rates
):
    levels_dev = tracer.shape[0]
    lat_rows = tracer.shape[1]
    n_wide = lax.axis_size("wide")
    n_narrow = lax.axis_size("narrow")
    first_row = lax.axis_index("wide") * lat_rows
    stacked = jnp.stack([tracer, courant])
    padded = extended(stacked, (("wide", 2),), 4)
    open_faces = valid_rows(first_row, lat_rows, 4)
    section_one = advect_section(padded[0], padded[1], open_faces)
    section_two = advect_section(section_one, padded[1][:, 2:-2], open_faces[2:-2])
    advected = 0.5 * tracer + 0.5 * section_two
    wave_count = band_map.shape[0]
    fourier = longitude_transform(advected, wave_count)
    wave_ids = jnp.arange(wave_count, dtype=jnp.int32)
    kept_mask = (2 * wave_ids[:, None] < nlon_counts[None, :]).astype(jnp.float32)
    fourier = fourier * kept_mask[:, None, None, :]
    slot_count = wave_count // (n_wide * n_narrow)
    fourier = jnp.einsum(
        "sm,mclj->sclj", (band_map[:, None] == wave_ids[None, :]).astype(jnp.float32), fourier,
        precision=lax.Precision.HIGHEST,
    )
    fourier = lax.all_to_all(fourier, "wide", split_axis=0, concat_axis=3, tiled=True)
    fourier = lax.all_to_all(fourier, "narrow", split_axis=0, concat_axis=2, tiled=True)
    levels_all = levels_dev * n_narrow
    half_rows = fourier.shape[3] // 2
    north_half = fourier[:, :, :, :half_rows]
    south_half = jnp.flip(fourier[:, :, :, half_rows:], axis=3)
    sym_part = north_half + south_half
    anti_part = north_half - south_half
    slot_start = (lax.axis_index("wide") * n_narrow + lax.axis_index("narrow")) * slot_count
    slot_waves = lax.dynamic_slice_in_dim(band_map, slot_start, slot_count)
    same_parity = (jnp.arange(2, dtype=jnp.int32)[None, :] - slot_waves[:, None]) % 2 == 0
    chosen = jnp.where(same_parity[:, :, None, None, None], sym_part[:, None], anti_part[:, None])
    spectral = jnp.einsum("spkj,spclj->spkcl", legendre, chosen, precision=lax.Precision.HIGHEST)
    degree_ids = (
        2 * jnp.arange(wave_count // 2, dtype=jnp.int32)[None, :]
        + jnp.arange(2, dtype=jnp.int32)[:, None]
    )
    upper_mask = (degree_ids[None] >= slot_waves[:, None, None]).astype(jnp.float32)
    spectral = spectral * upper_mask[:, :, :, None, None]
    spectral = jnp.transpose(spectral, (0, 2, 1, 3, 4)).reshape(
        slot_count, wave_count, 2, levels_all
    )
    spectral = jnp.einsum(
        "tn,sncl->stcl", (owner_map[:, None] == wave_ids[None, :]).astype(jnp.float32), spectral,
        precision=lax.Precision.HIGHEST,
    )
    gathered = lax.all_to_all(spectral, "narrow", split_axis=1, concat_axis=0, tiled=True)
    owned = gathered.shape[1]
    owned_degrees = lax.dynamic_slice_in_dim(owner_map, lax.axis_index("narrow") * owned, owned)
    degree_sq = (owned_degrees * (owned_degrees + 1)).astype(jnp.float32)
    damping = 1.0 / (1.0 + degree_sq[None, :] * mode_rates[:, None])
    modal_part = jnp.einsum("kl,stcl->kstc", modes_to, gathered, precision=lax.Precision.HIGHEST)
    scaled = modal_part * damping[:, None, :, None]
    return jnp.einsum("ik,kstc->cist", modes_from, scaled, precision=lax.Precision.HIGHEST)


MESH = pl.DeviceIdType.MESH
LANE = 128
PAD = 8
RIM = 4
CHUNKS = 4
TALL = 17
HALO = {1: (4, 3), 0: (4, 2)}


def chunk_list(lon_count, count):
    tiles = -(-lon_count // LANE)
    cuts = [min(lon_count, LANE * (tiles * cut // count)) for cut in range(count + 1)]
    return [(lo, hi - lo) for lo, hi in zip(cuts, cuts[1:])]


def fourier_table(lon_count, wave_count):
    rows = -(-lon_count // LANE) * LANE
    turns = np.outer(np.arange(lon_count), np.arange(wave_count)) % lon_count
    angle = 2.0 * np.pi / lon_count * turns
    full = np.concatenate([np.cos(angle), -np.sin(angle)], axis=1) * (0.5 / np.sqrt(lon_count))
    high = full.astype(jnp.bfloat16)
    low = (full - high.astype(np.float64)).astype(jnp.bfloat16)
    table = np.zeros((rows, LANE), jnp.bfloat16)
    table[:lon_count] = np.concatenate([high, low], axis=1)
    return table


def split(value):
    high = value.astype(jnp.bfloat16)
    low = (value - high.astype(jnp.float32)).astype(jnp.bfloat16)
    return high, low


def section(field, rate, ahead):
    rows = field.shape[0]
    above = pltpu.roll(field, rows - 1, 0)
    step = above - field
    near = jnp.where(ahead, pltpu.roll(step, 1, 0), pltpu.roll(step, rows - 1, 0))
    slope = step * (1.0 / 3.0) + near * (1.0 / 6.0)
    slope = jnp.maximum(jnp.minimum(slope, jnp.maximum(step, 0.0)), jnp.minimum(step, 0.0))
    flux = rate * jnp.where(ahead, field + slope, above - slope)
    return field - (flux - pltpu.roll(flux, 1, 0))


def rim_flux(field, step, rate, ahead, face):
    here = step[face]
    near = jnp.where(ahead[face], step[face - 1], step[face + 1])
    slope = here * (1.0 / 3.0) + near * (1.0 / 6.0)
    slope = jnp.maximum(jnp.minimum(slope, jnp.maximum(here, 0.0)), jnp.minimum(here, 0.0))
    return rate[face] * jnp.where(ahead[face], field[face] + slope, field[face + 1] - slope)


def rim_section(field_row, rate_row):
    field = {row: field_row(row) for row in range(-4, RIM + 4)}
    rate = {row: rate_row(row) for row in range(-3, RIM + 2)}
    ahead = {row: rate[row] >= 0.0 for row in rate}
    step = {row: field[row + 1] - field[row] for row in range(-4, RIM + 3)}
    flux = {row: rim_flux(field, step, rate, ahead, row) for row in range(-3, RIM + 2)}
    once = {row: field[row] - (flux[row] - flux[row - 1]) for row in range(-2, RIM + 2)}
    step = {row: once[row + 1] - once[row] for row in range(-2, RIM + 1)}
    flux = {row: rim_flux(once, step, rate, ahead, row) for row in range(-1, RIM)}
    return [field[row] + (once[row] - (flux[row] - flux[row - 1])) for row in range(RIM)]


def ids(shape, dim):
    return lax.broadcasted_iota(jnp.int32, shape, dim)


def fused_kernel(
    n_wide, n_narrow, lon_count,
    tracer, courant, nlon, band, owner, legendre, modes_to, modes_from, rates, table,
    out,
    q_buf, c_buf, t_buf, a_buf, e_buf, q_tall, c_tall, rim, acc, spec, leg, nlon_s, band_s, owner_s, to_s, from_s, rate_s,
    pick, keep, degree, sent, got, lx, xs,
    small_sem, load_sem, table_sem, halo_send, halo_recv, leg_send, leg_recv, four_send, four_recv,
    entered,
):
    wide, narrow = lax.axis_index("wide"), lax.axis_index("narrow")
    total = n_wide * n_narrow
    me = wide * n_narrow + narrow
    levels, lat_rows = tracer.shape[0], tracer.shape[1]
    wave_count = band_s.shape[0]
    lon_pad = t_buf.shape[0]
    chunks = chunk_list(lon_count, CHUNKS)
    owned = wave_count // n_narrow
    half_waves = wave_count // 2
    row_total = levels * lat_rows

    barrier = pltpu.get_barrier_semaphore()

    def flipped(bit):
        return wide + bit * (1 - 2 * ((wide // bit) % 2))

    bits = [2**k for k in range(n_wide.bit_length() - 1)]
    cube = [(wide, 1 - narrow)] + [(flipped(bit), narrow) for bit in bits]
    for other in cube:
        pl.semaphore_signal(barrier, inc=1, device_id=other, device_id_type=MESH)
    inner = (wide > 0) & (wide < n_wide - 1)

    @pl.when(inner)
    def _():
        pl.semaphore_signal(
            barrier, inc=1, device_id=(wide - 1 + 2 * (wide % 2), narrow), device_id_type=MESH
        )

    smalls = []
    for at, (here, there) in enumerate(
        ((nlon, nlon_s), (band, band_s), (owner, owner_s), (modes_to, to_s), (modes_from, from_s), (rates, rate_s))
    ):
        smalls.append(pltpu.make_async_copy(here, there, small_sem.at[at]))
    for copy in smalls:
        copy.start()
    loads = []
    for at, (lo, size) in enumerate(chunks):
        pair = []
        for which, (here, there) in enumerate(((tracer, q_buf), (courant, c_buf))):
            copy = pltpu.make_async_copy(
                here.at[:, :, pl.ds(lo, size)],
                there.at[:, pl.ds(PAD, lat_rows), pl.ds(lo, size)],
                load_sem.at[at, which],
            )
            copy.start()
            pair.append(copy)
        loads.append(pair)
    table_copy = pltpu.make_async_copy(table, t_buf, table_sem)
    table_copy.start()
    own_leg = pltpu.make_async_copy(legendre, leg.at[narrow], leg_recv.at[narrow])
    own_leg.start()

    @pl.when(wide == 0)
    def _():
        q_buf[:, 0:PAD, :] = jnp.zeros((levels, PAD, lon_count), jnp.float32)
        c_buf[:, 0:PAD, :] = jnp.zeros((levels, PAD, lon_count), jnp.float32)

    @pl.when(wide == n_wide - 1)
    def _():
        q_buf[:, PAD + lat_rows :, :] = jnp.zeros((levels, PAD, lon_count), jnp.float32)
        c_buf[:, PAD + lat_rows :, :] = jnp.zeros((levels, PAD, lon_count), jnp.float32)

    @pl.when(inner)
    def _():
        pl.semaphore_wait(barrier, len(cube) + 1)

    @pl.when(jnp.logical_not(inner))
    def _():
        pl.semaphore_wait(barrier, len(cube))

    def tell(stage):
        pl.semaphore_signal(entered.at[stage], inc=1, device_id=cube[stage], device_id_type=MESH)

    tell(1)

    def halo(up, which):
        here, there = ((tracer, q_buf), (courant, c_buf))[which]
        count = HALO[up][which]
        first = lat_rows - count if up else 0
        land = PAD - count if up else PAD + lat_rows
        return pltpu.make_async_remote_copy(
            src_ref=here.at[:, pl.ds(first, count), :],
            dst_ref=there.at[:, pl.ds(land, count), :],
            send_sem=halo_send.at[up, which],
            recv_sem=halo_recv.at[up, which],
            device_id=(wide + 1 if up else wide - 1, narrow),
            device_id_type=MESH,
        )

    odd = wide % 2 == 1

    def halo_step(up, what, cond):
        @pl.when(cond)
        def _():
            for which in range(2):
                getattr(halo(up, which), what)()

    halo_step(1, "start", odd & (wide < n_wide - 1))
    halo_step(0, "start", jnp.logical_not(odd) & (wide > 0))
    halo_step(0, "start", odd)
    halo_step(1, "start", jnp.logical_not(odd))

    leg_copy = pltpu.make_async_remote_copy(
        src_ref=legendre,
        dst_ref=leg.at[narrow],
        send_sem=leg_send,
        recv_sem=leg_recv.at[narrow],
        device_id=(wide, 1 - narrow),
        device_id_type=MESH,
    )
    leg_copy.start()

    for copy in smalls:
        copy.wait()
    row8, lane8 = ids((8, LANE), 0), ids((8, LANE), 1)
    for at in range(n_wide):
        wave = jnp.where(row8 < 2, band_s[2 * at], band_s[2 * at + 1])
        column = (row8 % 2) * wave_count + wave
        hit = (row8 < 4) & (lane8 % (2 * wave_count) == column)
        pick[8 * at : 8 * at + 8, :] = jnp.where(hit, 1.0, 0.0)
    for row in range(lat_rows):
        keep[row : row + 1, :] = jnp.full((1, LANE), nlon_s[row], jnp.int32)
    for row in range(owned):
        degree[row : row + 1, :] = jnp.full((1, LANE), owner_s[narrow * owned + row], jnp.int32)

    acc[...] = jnp.zeros_like(acc)
    a_buf[:, lon_pad - LANE :] = jnp.zeros((2 * row_total, LANE), jnp.bfloat16)
    width = lon_pad // CHUNKS
    for at in range(CHUNKS):
        loads[at][0].wait()
        loads[at][1].wait()

        def tile(step, carry, lo=at * width, lanes=LANE):
            columns = pl.ds(pl.multiple_of(lo + step * LANE, LANE), lanes)
            for level in range(levels):
                field = q_buf[level, PAD : PAD + lat_rows, columns]
                rate = c_buf[level, PAD : PAD + lat_rows, columns]
                ahead = rate >= 0.0
                twice = section(section(field, rate, ahead), rate, ahead)
                high, low = split(field + twice)
                first = level * lat_rows
                a_buf[first : first + lat_rows, columns] = high
                a_buf[row_total + first : row_total + first + lat_rows, columns] = low
            return carry

        whole, rest = divmod(chunks[at][1], LANE)
        lax.fori_loop(0, whole, tile, 0)
        if rest:
            tile(whole, 0, lanes=rest)
        if at == 0:
            table_copy.wait()
        columns = pl.ds(at * width, width)
        acc[...] += jnp.dot(
            a_buf[:, columns], t_buf[columns, :], preferred_element_type=jnp.float32
        )

        if at + 1 < len(cube):
            pl.semaphore_wait(entered.at[at + 1], 1)
            if at + 2 < len(cube):
                tell(at + 2)

    spectrum = acc[0:row_total, :] + acc[row_total : 2 * row_total, :]
    kept = 2 * (ids((lat_rows, LANE), 1) % wave_count) < keep[...]
    spec[...] = jnp.where(jnp.concatenate([kept] * levels, axis=0), spectrum, 0.0)

    @pl.when(wide == n_wide - 1)
    def _():
        last = PAD + lat_rows - 1
        c_buf[:, last : last + 1, :] = jnp.zeros((levels, 1, lon_count), jnp.float32)

    own_leg.wait()
    pltpu.make_async_remote_copy(
        src_ref=legendre,
        dst_ref=leg.at[1 - narrow],
        send_sem=leg_send,
        recv_sem=leg_recv.at[1 - narrow],
        device_id=(wide, 1 - narrow),
        device_id_type=MESH,
    ).wait_recv()

    degrees = degree[:, 0:wave_count]
    flat = ids((owned, wave_count), 1)
    held = 2 * (flat % half_waves) + flat // half_waves
    north, south = [], []
    for slot in range(n_narrow):
        wave = band_s[wide * n_narrow + slot]
        chosen = jnp.where((held == degrees) & (degrees >= wave), 1.0, 0.0)
        even = ((degrees + wave) % 2) == 0
        north.append(chosen.astype(jnp.bfloat16))
        south.append(jnp.where(even, chosen, -chosen).astype(jnp.bfloat16))
    leg_parts = [split(leg[slot]) for slot in range(n_narrow)]
    block = n_narrow * owned

    def rows_of(picks):
        return jnp.concatenate(
            [
                jnp.dot(picks[slot], leg_parts[slot][half], preferred_element_type=jnp.float32)
                for half in range(2)
                for slot in range(n_narrow)
            ],
            axis=0,
        )

    source, lane = ids((LANE, LANE), 0), ids((LANE, LANE), 1)
    lane_rows = ids((block, LANE), 1)
    tiles = leg.shape[2] // LANE
    for southern, picks in ((False, north), (True, south)):
        rows = rows_of(picks).astype(jnp.bfloat16)
        tall = jnp.concatenate([rows[:, LANE * a : LANE * a + LANE] for a in range(tiles)], axis=0)
        for half in range(2):
            within = lane % lat_rows
            if southern:
                within = lat_rows - 1 - within
            spread = jnp.where(source == half * lat_rows + within, 1.0, 0.0).astype(jnp.bfloat16)
            wide_rows = jnp.dot(tall, spread, preferred_element_type=jnp.float32)
            for a in range(tiles):
                lat_block = 2 * a + half
                if southern:
                    lat_block = n_wide - 1 - lat_block
                for part in range(2):
                    piece = wide_rows[(a * 2 + part) * block : (a * 2 + part + 1) * block]
                    for level in range(levels):
                        kept_piece = jnp.where(lane_rows // lat_rows == level, piece, 0.0)
                        first = (part * levels + level) * block
                        lx[first : first + block, LANE * lat_block : LANE * lat_block + LANE] = (
                            kept_piece.astype(jnp.bfloat16)
                        )

    lane1 = ids((1, LANE), 1)
    number = jnp.zeros((1, LANE), jnp.int32)
    for at in range(owned):
        number = jnp.where(lane1 % owned == at, owner_s[narrow * owned + at], number)
    squared = (number * (number + 1)).astype(jnp.float32)
    levels_all = levels * n_narrow
    damping = [1.0 / (1.0 + squared * rate_s[k]) for k in range(levels_all)]
    mix = [
        [
            sum((from_s[i, k] * to_s[k, l]) * damping[k] for k in range(levels_all))
            for l in range(levels_all)
        ]
        for i in range(levels_all)
    ]

    last_dims = (((1,), (1,)), ((), ()))

    def edge(top):
        start = pl.multiple_of(jnp.where(top, 0, lat_rows), 8)
        first = jnp.where(top, PAD, PAD - RIM)

        def strip(step, carry, tiles=(LANE,) * PAD):
            places = [
                pl.ds(pl.multiple_of(step * PAD * LANE + k * LANE, LANE), lanes)
                for k, lanes in enumerate(tiles)
            ]
            for level in range(levels):
                for k, place in enumerate(places):
                    here = pl.ds((level * PAD + k) * TALL, 2 * PAD)
                    q_tall[here, 0 : tiles[k]] = q_buf[level, pl.ds(start, 2 * PAD), place]
                    c_tall[here, 0 : tiles[k]] = c_buf[level, pl.ds(start, 2 * PAD), place]
            for level in range(levels):
                base = level * PAD * TALL + first
                values = rim_section(
                    lambda row: q_tall[pl.ds(base + row, PAD, stride=TALL), :],
                    lambda row: c_tall[pl.ds(base + row, PAD, stride=TALL), :],
                )
                for row, value in enumerate(values):
                    rim[pl.ds(level * RIM + row, PAD, stride=PAD), :] = value
            for k in range(PAD):
                value = rim[k * PAD : k * PAD + PAD, :]
                high = value.astype(jnp.bfloat16).astype(jnp.float32)
                both = jnp.concatenate([high, value - high], axis=0)
                place = pl.ds(pl.multiple_of(step * PAD * LANE + k * LANE, LANE), LANE)
                e_buf[:, place] = both.astype(jnp.bfloat16)
            return carry

        whole = lon_count // (PAD * LANE)
        lax.fori_loop(0, whole, strip, 0)
        rest = lon_count - whole * PAD * LANE
        if rest:
            strip(whole, 0, tuple(min(LANE, rest - k * LANE) for k in range(PAD)))
        rows = jnp.dot(e_buf[...], t_buf[...], preferred_element_type=jnp.float32)
        rows = rows[0:PAD] + rows[PAD:]
        swapped = pltpu.roll(rows, RIM, 0)
        at = pl.multiple_of(jnp.where(top, 0, lat_rows - PAD), 8)
        fresh = jnp.where(top, row8, PAD - 1 - row8) < RIM
        cover = 2 * (lane8 % wave_count) < keep[pl.ds(at, PAD), :]
        for level, mine in enumerate(
            (jnp.where(top, rows, swapped), jnp.where(top, swapped, rows))
        ):
            place = pl.ds(pl.multiple_of(level * lat_rows + at, 8), PAD)
            spec[place, :] = jnp.where(fresh, jnp.where(cover, mine, 0.0), spec[place, :])

    halo_step(1, "wait_recv", odd)
    halo_step(0, "wait_recv", jnp.logical_not(odd))
    edge(odd)
    halo_step(0, "wait_recv", odd & (wide < n_wide - 1))
    halo_step(1, "wait_recv", jnp.logical_not(odd) & (wide > 0))
    edge(jnp.logical_not(odd))

    high, low = split(spec[...])
    chooser = pick[...].astype(jnp.bfloat16)
    moved = lax.dot_general(chooser, high, last_dims, preferred_element_type=jnp.float32)
    moved = moved + lax.dot_general(chooser, low, last_dims, preferred_element_type=jnp.float32)
    for at in range(n_wide):
        sent[at] = moved[8 * at : 8 * at + 4, :]

    turns = [1 - 2 * ((wide // bit) % 2) for bit in bits]

    def fourier_copy(code):
        to_wide = wide
        for bit, turn in zip(bits, turns):
            if code // n_narrow & bit:
                to_wide = to_wide + bit * turn
        to_narrow = 1 - narrow if code % n_narrow else narrow
        return pltpu.make_async_remote_copy(
            src_ref=sent.at[to_wide],
            dst_ref=got.at[me],
            send_sem=four_send,
            recv_sem=four_recv,
            device_id=(to_wide, to_narrow),
            device_id_type=MESH,
        )

    for code in range(total - 1, 0, -1):
        fourier_copy(code).start()
    got[me] = sent[wide]

    others = got.at[pl.ds(0, total - 1)]
    pltpu.make_async_copy(others, others, four_recv).wait()
    for at in range(n_wide):
        values = jnp.concatenate([got[n_narrow * at + j] for j in range(n_narrow)], axis=0)
        high, low = split(values)
        xs[:, LANE * at : LANE * at + LANE] = jnp.concatenate([high, low], axis=0)
    product = lax.dot_general(xs[...], lx[...], last_dims, preferred_element_type=jnp.float32)
    product = product[0:8] + product[8:16]
    product = product + pltpu.roll(product, LANE // 2, 1)
    by_level = []
    for level in range(levels):
        moved = product if level == 0 else pltpu.roll(product, LANE - level * block, 1)
        by_level.append(jnp.where(lane8 < owned, moved, pltpu.roll(moved, 6, 0)))
    for c in range(2):
        for i in range(levels_all):
            result = jnp.zeros((1, LANE), jnp.float32)
            for n in range(n_narrow):
                for level in range(levels):
                    row = 4 * n + c
                    result = result + mix[i][levels * n + level] * by_level[level][row : row + 1]
            out[c, i, 0:1, :] = result[:, 0:owned]
            out[c, i, 1:2, :] = pltpu.roll(result, LANE - owned, 1)[:, 0:owned]

    pltpu.make_async_copy(others, others, four_send).wait()
    leg_copy.wait_send()
    halo_step(1, "wait_send", wide < n_wide - 1)
    halo_step(0, "wait_send", wide > 0)


def fused_fits(tracer, band_map, legendre, n_wide, n_narrow):
    levels, lat_rows = tracer.shape[0], tracer.shape[1]
    waves = band_map.shape[0]
    return (
        levels == 2
        and n_narrow == 2
        and lat_rows * levels == LANE
        and waves == n_wide * n_narrow
        and n_wide & (n_wide - 1) == 0
        and n_wide.bit_length() <= CHUNKS + 1
        and -(-tracer.shape[2] // LANE) % (CHUNKS * PAD) == 0
        and tracer.shape[2] > PAD * LANE
        and 4 * waves == LANE
        and legendre.shape[3] * 2 == n_wide * lat_rows
        and 2 * n_wide * 4 == LANE
    )


def fused(
    tracer, courant, nlon_counts, band_map, owner_map, legendre, modes_to, modes_from, mode_rates
):
    n_wide = lax.axis_size("wide")
    n_narrow = lax.axis_size("narrow")
    levels, lat_rows, lon_count = tracer.shape
    waves = band_map.shape[0]
    total = n_wide * n_narrow
    table = fourier_table(lon_count, waves)
    lon_pad = table.shape[0]
    tall = lat_rows + 2 * PAD
    half = legendre.shape[3]
    levels_all = levels * n_narrow
    vmem, smem, dma = pltpu.VMEM, pltpu.SMEM, pltpu.SemaphoreType.DMA
    operands = (
        tracer, courant, nlon_counts, band_map, owner_map,
        legendre.reshape(waves, half), modes_to, modes_from, mode_rates, jnp.asarray(table),
    )
    return pl.pallas_call(
        functools.partial(fused_kernel, n_wide, n_narrow, lon_count),
        out_shape=vmem((2, levels_all, 2, waves // n_narrow), jnp.float32),
        in_specs=[pl.BlockSpec(memory_space=pltpu.HBM)] * 10,
        out_specs=pl.BlockSpec(memory_space=pltpu.VMEM),
        scratch_shapes=[
            vmem((levels, tall, lon_count), jnp.float32),
            vmem((levels, tall, lon_count), jnp.float32),
            vmem((lon_pad, LANE), jnp.bfloat16),
            vmem((2 * levels * lat_rows, lon_pad), jnp.bfloat16),
            vmem((2 * PAD, lon_pad), jnp.bfloat16),
            vmem(((levels + 1) * PAD * TALL, LANE), jnp.float32),
            vmem(((levels + 1) * PAD * TALL, LANE), jnp.float32),
            vmem((PAD * PAD + PAD, LANE), jnp.float32),
            vmem((2 * levels * lat_rows, LANE), jnp.float32),
            vmem((levels * lat_rows, LANE), jnp.float32),
            vmem((n_narrow, waves, half), jnp.float32),
            smem((lat_rows,), jnp.int32),
            smem((waves,), jnp.int32),
            smem((waves,), jnp.int32),
            smem((levels_all, levels_all), jnp.float32),
            smem((levels_all, levels_all), jnp.float32),
            smem((levels_all,), jnp.float32),
            vmem((8 * n_wide, LANE), jnp.float32),
            vmem((lat_rows, LANE), jnp.int32),
            vmem((waves // n_narrow, LANE), jnp.int32),
            vmem((n_wide, 4, LANE), jnp.float32),
            vmem((total, 4, LANE), jnp.float32),
            vmem((LANE, n_wide * LANE), jnp.bfloat16),
            vmem((16, n_wide * LANE), jnp.bfloat16),
            dma((6,)),
            dma((CHUNKS, 2)),
            dma,
            dma((2, 2)),
            dma((2, 2)),
            dma,
            dma((n_narrow,)),
            dma,
            dma,
            pltpu.SemaphoreType.REGULAR((total.bit_length(),)),
        ],
        compiler_params=pltpu.CompilerParams(
            collective_id=0, has_side_effects=True
        ),
    )(*(pltpu.with_memory_space_constraint(operand, pltpu.HBM) for operand in operands))


def program(tracer, courant, nlon_counts, band_map, owner_map, legendre, *modes):
    choose = (
        fused
        if fused_fits(
            tracer, band_map, legendre, lax.axis_size("wide"), lax.axis_size("narrow")
        )
        else body
    )
    return choose(tracer, courant, nlon_counts, band_map, owner_map, legendre, *modes)


def solution(mesh):
    placed = (
        P("narrow", "wide", None),
        P("narrow", "wide", None),
        P("wide"),
        P(),
        P(),
        P(("wide", "narrow"), None, None, None),
        P(),
        P(),
        P(),
    )
    return jax.shard_map(
        program, mesh=mesh, in_specs=placed, out_specs=P(None, None, "wide", "narrow"), check_vma=False
    )
```

```python
import functools
import math

import jax
import jax.numpy as jnp
import numpy as np
from jax import lax
from jax.experimental import pallas as pl
from jax.experimental.pallas import tpu as pltpu
from jax.sharding import PartitionSpec as P

NLAT = 1024


def extended(array, sides, width):
    for axis, dim in sides:
        devices, length = (lax.axis_size(axis), array.shape[dim])
        up = [(i, (i + 1) % devices) for i in range(devices - 1)]
        down = [(j, i) for i, j in up]
        last = lax.slice_in_dim(array, length - width, length, axis=dim)
        initial = lax.slice_in_dim(array, 0, width, axis=dim)
        before = lax.ppermute(last, axis, up)
        after = lax.ppermute(initial, axis, down)
        array = jnp.concatenate([before, array, after], axis=dim)
    return array


def advect_section(field_ext, rate_ext, open_faces):
    row_total = field_ext.shape[1]
    row_below = field_ext[:, 0 : row_total - 3]
    row_here = field_ext[:, 1 : row_total - 2]
    row_above = field_ext[:, 2 : row_total - 1]
    row_beyond = field_ext[:, 3:row_total]
    face_rate = rate_ext[:, 1 : row_total - 2] * open_faces[1 : row_total - 2][:, None]
    upwind = (5.0 * row_here + 2.0 * row_above - row_below) / 6.0
    downwind = (5.0 * row_above + 2.0 * row_here - row_beyond) / 6.0
    low_bound = jnp.minimum(row_here, row_above)
    high_bound = jnp.maximum(row_here, row_above)
    face_value = jnp.clip(jnp.where(face_rate >= 0.0, upwind, downwind), low_bound, high_bound)
    face_flux = face_rate * face_value
    return field_ext[:, 2 : row_total - 2] - (face_flux[:, 1:] - face_flux[:, :-1])


def valid_rows(first_row, lat_rows, rim_width):
    row_ids = first_row + jnp.arange(lat_rows + 2 * rim_width, dtype=jnp.int32) - rim_width
    return ((row_ids >= 0) & (row_ids < NLAT - 1)).astype(jnp.float32)


def longitude_transform(advected, wave_count):
    levels_dev, lat_rows, lon_count = advected.shape
    short_len = 32
    long_len = lon_count // short_len
    block_count = wave_count // short_len
    row_count = levels_dev * lat_rows
    grid_rows = advected.reshape(row_count, short_len, long_len)
    short_ids = jnp.arange(short_len, dtype=jnp.int32)
    turn_one = short_ids[:, None] * short_ids[None, :] % short_len
    angle_one = 2.0 * math.pi / short_len * turn_one.astype(jnp.float32)
    highest = lax.Precision.HIGHEST
    inner_re = jnp.einsum("pab,ar->prb", grid_rows, jnp.cos(angle_one), precision=highest)
    inner_im = -jnp.einsum("pab,ar->prb", grid_rows, jnp.sin(angle_one), precision=highest)
    long_ids = jnp.arange(long_len, dtype=jnp.int32)
    block_ids = jnp.arange(block_count, dtype=jnp.int32)
    wave_ids = short_len * block_ids[None, None, :] + short_ids[:, None, None]
    turn_two = wave_ids * long_ids[None, :, None] % lon_count
    angle_two = 2.0 * math.pi / lon_count * turn_two.astype(jnp.float32)
    cos_two = jnp.cos(angle_two)
    sin_two = jnp.sin(angle_two)
    outer_re = jnp.einsum("prb,rbc->crp", inner_re, cos_two, precision=highest) + jnp.einsum(
        "prb,rbc->crp", inner_im, sin_two, precision=highest
    )
    outer_im = jnp.einsum("prb,rbc->crp", inner_im, cos_two, precision=highest) - jnp.einsum(
        "prb,rbc->crp", inner_re, sin_two, precision=highest
    )
    outer_re = (outer_re / math.sqrt(lon_count)).reshape(wave_count, levels_dev, lat_rows)
    outer_im = (outer_im / math.sqrt(lon_count)).reshape(wave_count, levels_dev, lat_rows)
    return jnp.stack([outer_re, outer_im], axis=1)


def body(
    tracer, courant, nlon_counts, band_map, owner_map, legendre, modes_to, modes_from, mode_rates
):
    levels_dev = tracer.shape[0]
    lat_rows = tracer.shape[1]
    n_wide = lax.axis_size("wide")
    n_narrow = lax.axis_size("narrow")
    first_row = lax.axis_index("wide") * lat_rows
    stacked = jnp.stack([tracer, courant])
    padded = extended(stacked, (("wide", 2),), 4)
    open_faces = valid_rows(first_row, lat_rows, 4)
    section_one = advect_section(padded[0], padded[1], open_faces)
    section_two = advect_section(section_one, padded[1][:, 2:-2], open_faces[2:-2])
    advected = 0.5 * tracer + 0.5 * section_two
    wave_count = band_map.shape[0]
    fourier = longitude_transform(advected, wave_count)
    wave_ids = jnp.arange(wave_count, dtype=jnp.int32)
    kept_mask = (2 * wave_ids[:, None] < nlon_counts[None, :]).astype(jnp.float32)
    fourier = fourier * kept_mask[:, None, None, :]
    slot_count = wave_count // (n_wide * n_narrow)
    fourier = jnp.einsum(
        "sm,mclj->sclj", (band_map[:, None] == wave_ids[None, :]).astype(jnp.float32), fourier,
        precision=lax.Precision.HIGHEST,
    )
    fourier = lax.all_to_all(fourier, "wide", split_axis=0, concat_axis=3, tiled=True)
    fourier = lax.all_to_all(fourier, "narrow", split_axis=0, concat_axis=2, tiled=True)
    levels_all = levels_dev * n_narrow
    half_rows = fourier.shape[3] // 2
    north_half = fourier[:, :, :, :half_rows]
    south_half = jnp.flip(fourier[:, :, :, half_rows:], axis=3)
    sym_part = north_half + south_half
    anti_part = north_half - south_half
    slot_start = (lax.axis_index("wide") * n_narrow + lax.axis_index("narrow")) * slot_count
    slot_waves = lax.dynamic_slice_in_dim(band_map, slot_start, slot_count)
    same_parity = (jnp.arange(2, dtype=jnp.int32)[None, :] - slot_waves[:, None]) % 2 == 0
    chosen = jnp.where(same_parity[:, :, None, None, None], sym_part[:, None], anti_part[:, None])
    spectral = jnp.einsum("spkj,spclj->spkcl", legendre, chosen, precision=lax.Precision.HIGHEST)
    degree_ids = (
        2 * jnp.arange(wave_count // 2, dtype=jnp.int32)[None, :]
        + jnp.arange(2, dtype=jnp.int32)[:, None]
    )
    upper_mask = (degree_ids[None] >= slot_waves[:, None, None]).astype(jnp.float32)
    spectral = spectral * upper_mask[:, :, :, None, None]
    spectral = jnp.transpose(spectral, (0, 2, 1, 3, 4)).reshape(
        slot_count, wave_count, 2, levels_all
    )
    spectral = jnp.einsum(
        "tn,sncl->stcl", (owner_map[:, None] == wave_ids[None, :]).astype(jnp.float32), spectral,
        precision=lax.Precision.HIGHEST,
    )
    gathered = lax.all_to_all(spectral, "narrow", split_axis=1, concat_axis=0, tiled=True)
    owned = gathered.shape[1]
    owned_degrees = lax.dynamic_slice_in_dim(owner_map, lax.axis_index("narrow") * owned, owned)
    degree_sq = (owned_degrees * (owned_degrees + 1)).astype(jnp.float32)
    damping = 1.0 / (1.0 + degree_sq[None, :] * mode_rates[:, None])
    modal_part = jnp.einsum("kl,stcl->kstc", modes_to, gathered, precision=lax.Precision.HIGHEST)
    scaled = modal_part * damping[:, None, :, None]
    return jnp.einsum("ik,kstc->cist", modes_from, scaled, precision=lax.Precision.HIGHEST)


MESH = pl.DeviceIdType.MESH
LANE = 128
PAD = 8
RIM = 4
CHUNKS = 4
TALL = 17
HALO = {1: (4, 3), 0: (4, 2)}


def chunk_list(lon_count, count):
    tiles = -(-lon_count // LANE)
    cuts = [min(lon_count, LANE * (tiles * cut // count)) for cut in range(count + 1)]
    return [(lo, hi - lo) for lo, hi in zip(cuts, cuts[1:])]


def fourier_table(lon_count, wave_count):
    rows = -(-lon_count // LANE) * LANE
    turns = np.outer(np.arange(lon_count), np.arange(wave_count)) % lon_count
    angle = 2.0 * np.pi / lon_count * turns
    full = np.concatenate([np.cos(angle), -np.sin(angle)], axis=1) * (0.5 / np.sqrt(lon_count))
    high = full.astype(jnp.bfloat16)
    low = (full - high.astype(np.float64)).astype(jnp.bfloat16)
    table = np.zeros((rows, LANE), jnp.bfloat16)
    table[:lon_count] = np.concatenate([high, low], axis=1)
    return table


def split(value):
    high = value.astype(jnp.bfloat16)
    low = (value - high.astype(jnp.float32)).astype(jnp.bfloat16)
    return high, low


def section(field, rate, ahead):
    rows = field.shape[0]
    above = pltpu.roll(field, rows - 1, 0)
    step = above - field
    near = jnp.where(ahead, pltpu.roll(step, 1, 0), pltpu.roll(step, rows - 1, 0))
    slope = step * (1.0 / 3.0) + near * (1.0 / 6.0)
    slope = jnp.maximum(jnp.minimum(slope, jnp.maximum(step, 0.0)), jnp.minimum(step, 0.0))
    flux = rate * jnp.where(ahead, field + slope, above - slope)
    return field - (flux - pltpu.roll(flux, 1, 0))


def rim_flux(field, step, rate, ahead, face):
    here = step[face]
    near = jnp.where(ahead[face], step[face - 1], step[face + 1])
    slope = here * (1.0 / 3.0) + near * (1.0 / 6.0)
    slope = jnp.maximum(jnp.minimum(slope, jnp.maximum(here, 0.0)), jnp.minimum(here, 0.0))
    return rate[face] * jnp.where(ahead[face], field[face] + slope, field[face + 1] - slope)


def rim_section(field_row, rate_row):
    field = {row: field_row(row) for row in range(-4, RIM + 4)}
    rate = {row: rate_row(row) for row in range(-3, RIM + 2)}
    ahead = {row: rate[row] >= 0.0 for row in rate}
    step = {row: field[row + 1] - field[row] for row in range(-4, RIM + 3)}
    flux = {row: rim_flux(field, step, rate, ahead, row) for row in range(-3, RIM + 2)}
    once = {row: field[row] - (flux[row] - flux[row - 1]) for row in range(-2, RIM + 2)}
    step = {row: once[row + 1] - once[row] for row in range(-2, RIM + 1)}
    flux = {row: rim_flux(once, step, rate, ahead, row) for row in range(-1, RIM)}
    return [field[row] + (once[row] - (flux[row] - flux[row - 1])) for row in range(RIM)]


def ids(shape, dim):
    return lax.broadcasted_iota(jnp.int32, shape, dim)


def fused_kernel(
    n_wide, n_narrow, lon_count,
    tracer, courant, nlon, band, owner, legendre, modes_to, modes_from, rates, table,
    out,
    q_buf, c_buf, t_buf, a_buf, e_buf, q_tall, c_tall, rim, spec, leg, nlon_s, band_s, owner_s, to_s, from_s, rate_s,
    pick, keep, degree, sent, got, lx, xs,
    small_sem, load_sem, table_sem, halo_send, halo_recv, leg_send, leg_recv, four_send, four_recv,
    entered,
):
    wide, narrow = lax.axis_index("wide"), lax.axis_index("narrow")
    total = n_wide * n_narrow
    me = wide * n_narrow + narrow
    levels, lat_rows = tracer.shape[0], tracer.shape[1]
    wave_count = band_s.shape[0]
    lon_pad = t_buf.shape[0]
    chunks = chunk_list(lon_count, CHUNKS)
    owned = wave_count // n_narrow
    half_waves = wave_count // 2
    row_total = levels * lat_rows

    barrier = pltpu.get_barrier_semaphore()

    bits = [2**k for k in range(n_wide.bit_length() - 1)]
    low = 2 ** (len(bits) // 2)
    high = n_wide // low
    far_at, near_at = wide // low, wide % low
    near = [
        (far_at * low + (near_at + a) % low, (narrow + b) % n_narrow)
        for a in range(low)
        for b in range(n_narrow)
        if a or b
    ]
    far = [(((far_at + a) % high) * low + near_at, narrow) for a in range(1, high)]
    last_near, first_near = near_at == low - 1, near_at == 0
    crosses = (last_near & (far_at < high - 1)) | (first_near & (far_at > 0))

    @pl.when(crosses)
    def _():
        pl.semaphore_signal(
            barrier,
            inc=1,
            device_id=(jnp.where(last_near, wide + 1, wide - 1), narrow),
            device_id_type=MESH,
        )

    for other in near + far:
        pl.semaphore_signal(barrier, inc=1, device_id=other, device_id_type=MESH)

    smalls = []
    for at, (here, there) in enumerate(
        ((nlon, nlon_s), (band, band_s), (owner, owner_s), (modes_to, to_s), (modes_from, from_s), (rates, rate_s))
    ):
        smalls.append(pltpu.make_async_copy(here, there, small_sem.at[at]))
    for copy in smalls:
        copy.start()
    loads = []
    for at, (lo, size) in enumerate(chunks):
        pair = []
        for which, (here, there) in enumerate(((tracer, q_buf), (courant, c_buf))):
            copy = pltpu.make_async_copy(
                here.at[:, :, pl.ds(lo, size)],
                there.at[:, pl.ds(PAD, lat_rows), pl.ds(lo, size)],
                load_sem.at[at, which],
            )
            copy.start()
            pair.append(copy)
        loads.append(pair)
    table_copy = pltpu.make_async_copy(table, t_buf, table_sem)
    table_copy.start()
    own_leg = pltpu.make_async_copy(legendre, leg.at[narrow], leg_recv.at[narrow])
    own_leg.start()

    @pl.when(wide == 0)
    def _():
        q_buf[:, 0:PAD, :] = jnp.zeros((levels, PAD, lon_count), jnp.float32)
        c_buf[:, 0:PAD, :] = jnp.zeros((levels, PAD, lon_count), jnp.float32)

    @pl.when(wide == n_wide - 1)
    def _():
        q_buf[:, PAD + lat_rows :, :] = jnp.zeros((levels, PAD, lon_count), jnp.float32)
        c_buf[:, PAD + lat_rows :, :] = jnp.zeros((levels, PAD, lon_count), jnp.float32)

    greeted = len(near) + len(far)

    @pl.when(crosses)
    def _():
        pl.semaphore_wait(barrier, greeted + 1)

    @pl.when(jnp.logical_not(crosses))
    def _():
        pl.semaphore_wait(barrier, greeted)

    for other in far:
        pl.semaphore_signal(entered, inc=1, device_id=other, device_id_type=MESH)

    def halo(up, which):
        here, there = ((tracer, q_buf), (courant, c_buf))[which]
        count = HALO[up][which]
        first = lat_rows - count if up else 0
        land = PAD - count if up else PAD + lat_rows
        return pltpu.make_async_remote_copy(
            src_ref=here.at[:, pl.ds(first, count), :],
            dst_ref=there.at[:, pl.ds(land, count), :],
            send_sem=halo_send.at[up, which],
            recv_sem=halo_recv.at[up, which],
            device_id=(wide + 1 if up else wide - 1, narrow),
            device_id_type=MESH,
        )

    odd = wide % 2 == 1

    def halo_step(up, what, cond):
        @pl.when(cond)
        def _():
            for which in range(2):
                getattr(halo(up, which), what)()

    halo_step(1, "start", odd & (wide < n_wide - 1))
    halo_step(0, "start", jnp.logical_not(odd) & (wide > 0))
    halo_step(0, "start", odd)
    halo_step(1, "start", jnp.logical_not(odd))

    leg_copy = pltpu.make_async_remote_copy(
        src_ref=legendre,
        dst_ref=leg.at[narrow],
        send_sem=leg_send,
        recv_sem=leg_recv.at[narrow],
        device_id=(wide, 1 - narrow),
        device_id_type=MESH,
    )
    leg_copy.start()

    for copy in smalls:
        copy.wait()
    row8, lane8 = ids((8, LANE), 0), ids((8, LANE), 1)
    for at in range(n_wide):
        wave = jnp.where(row8 < 2, band_s[2 * at], band_s[2 * at + 1])
        column = (row8 % 2) * wave_count + wave
        hit = (row8 < 4) & (lane8 % (2 * wave_count) == column)
        pick[8 * at : 8 * at + 8, :] = jnp.where(hit, 1.0, 0.0)
    for row in range(lat_rows):
        keep[row : row + 1, :] = jnp.full((1, LANE), nlon_s[row], jnp.int32)
    for row in range(owned):
        degree[row : row + 1, :] = jnp.full((1, LANE), owner_s[narrow * owned + row], jnp.int32)

    lane1 = ids((1, LANE), 1)
    number = jnp.zeros((1, LANE), jnp.int32)
    for at in range(owned):
        number = jnp.where(lane1 % owned == at, owner_s[narrow * owned + at], number)
    squared = (number * (number + 1)).astype(jnp.float32)
    levels_all = levels * n_narrow
    damping = [1.0 / (1.0 + squared * rate_s[k]) for k in range(levels_all)]
    mix = [
        [
            sum((from_s[i, k] * to_s[k, l]) * damping[k] for k in range(levels_all))
            for l in range(levels_all)
        ]
        for i in range(levels_all)
    ]

    weights = [
        [
            jnp.where(row8 < 4, mix[i][level], mix[i][levels + level])
            for level in range(levels)
        ]
        for i in range(levels_all)
    ]
    a_buf[:, lon_pad - LANE :] = jnp.zeros((2 * row_total, LANE), jnp.bfloat16)
    width = lon_pad // CHUNKS
    for at in range(CHUNKS):
        loads[at][0].wait()
        loads[at][1].wait()

        def tile(step, carry, lo=at * width, lanes=LANE):
            columns = pl.ds(pl.multiple_of(lo + step * LANE, LANE), lanes)
            for level in range(levels):
                field = q_buf[level, PAD : PAD + lat_rows, columns]
                rate = c_buf[level, PAD : PAD + lat_rows, columns]
                ahead = rate >= 0.0
                twice = section(section(field, rate, ahead), rate, ahead)
                high, low = split(field + twice)
                first = level * lat_rows
                a_buf[first : first + lat_rows, columns] = high
                a_buf[row_total + first : row_total + first + lat_rows, columns] = low
            return carry

        whole, rest = divmod(chunks[at][1], LANE)
        lax.fori_loop(0, whole, tile, 0)
        if rest:
            tile(whole, 0, lanes=rest)
    table_copy.wait()
    spectrum = jnp.dot(a_buf[...], t_buf[...], preferred_element_type=jnp.float32)
    spectrum = spectrum[0:row_total] + spectrum[row_total:]
    kept = 2 * (ids((lat_rows, LANE), 1) % wave_count) < keep[...]
    spec[...] = jnp.where(jnp.concatenate([kept] * levels, axis=0), spectrum, 0.0)

    @pl.when(wide == n_wide - 1)
    def _():
        last = PAD + lat_rows - 1
        c_buf[:, last : last + 1, :] = jnp.zeros((levels, 1, lon_count), jnp.float32)

    own_leg.wait()
    pltpu.make_async_remote_copy(
        src_ref=legendre,
        dst_ref=leg.at[1 - narrow],
        send_sem=leg_send,
        recv_sem=leg_recv.at[1 - narrow],
        device_id=(wide, 1 - narrow),
        device_id_type=MESH,
    ).wait_recv()

    degrees = degree[:, 0:wave_count]
    flat = ids((owned, wave_count), 1)
    held = 2 * (flat % half_waves) + flat // half_waves
    north, south = [], []
    for slot in range(n_narrow):
        wave = band_s[wide * n_narrow + slot]
        chosen = jnp.where((held == degrees) & (degrees >= wave), 1.0, 0.0)
        even = ((degrees + wave) % 2) == 0
        north.append(chosen.astype(jnp.bfloat16))
        south.append(jnp.where(even, chosen, -chosen).astype(jnp.bfloat16))
    leg_parts = [split(leg[slot]) for slot in range(n_narrow)]
    block = n_narrow * owned

    def rows_of(picks):
        return jnp.concatenate(
            [
                jnp.dot(picks[slot], leg_parts[slot][half], preferred_element_type=jnp.float32)
                for half in range(2)
                for slot in range(n_narrow)
            ],
            axis=0,
        )

    source, lane = ids((LANE, LANE), 0), ids((LANE, LANE), 1)
    lane_rows = ids((block, LANE), 1)
    tiles = leg.shape[2] // LANE
    for southern, picks in ((False, north), (True, south)):
        rows = rows_of(picks).astype(jnp.bfloat16)
        tall = jnp.concatenate([rows[:, LANE * a : LANE * a + LANE] for a in range(tiles)], axis=0)
        for half in range(2):
            within = lane % lat_rows
            if southern:
                within = lat_rows - 1 - within
            spread = jnp.where(source == half * lat_rows + within, 1.0, 0.0).astype(jnp.bfloat16)
            wide_rows = jnp.dot(tall, spread, preferred_element_type=jnp.float32)
            for a in range(tiles):
                lat_block = 2 * a + half
                if southern:
                    lat_block = n_wide - 1 - lat_block
                for part in range(2):
                    piece = wide_rows[(a * 2 + part) * block : (a * 2 + part + 1) * block]
                    for level in range(levels):
                        kept_piece = jnp.where(lane_rows // lat_rows == level, piece, 0.0)
                        first = (part * levels + level) * block
                        lx[first : first + block, LANE * lat_block : LANE * lat_block + LANE] = (
                            kept_piece.astype(jnp.bfloat16)
                        )

    last_dims = (((1,), (1,)), ((), ()))

    def edge(top):
        start = pl.multiple_of(jnp.where(top, 0, lat_rows), 8)
        first = jnp.where(top, PAD, PAD - RIM)

        def strip(step, carry, tiles=(LANE,) * PAD):
            places = [
                pl.ds(pl.multiple_of(step * PAD * LANE + k * LANE, LANE), lanes)
                for k, lanes in enumerate(tiles)
            ]
            for level in range(levels):
                for k, place in enumerate(places):
                    here = pl.ds((level * PAD + k) * TALL, 2 * PAD)
                    q_tall[here, 0 : tiles[k]] = q_buf[level, pl.ds(start, 2 * PAD), place]
                    c_tall[here, 0 : tiles[k]] = c_buf[level, pl.ds(start, 2 * PAD), place]
            for level in range(levels):
                base = level * PAD * TALL + first
                values = rim_section(
                    lambda row: q_tall[pl.ds(base + row, PAD, stride=TALL), :],
                    lambda row: c_tall[pl.ds(base + row, PAD, stride=TALL), :],
                )
                for row, value in enumerate(values):
                    rim[pl.ds(level * RIM + row, PAD, stride=PAD), :] = value
            for k in range(PAD):
                value = rim[k * PAD : k * PAD + PAD, :]
                high = value.astype(jnp.bfloat16).astype(jnp.float32)
                both = jnp.concatenate([high, value - high], axis=0)
                place = pl.ds(pl.multiple_of(step * PAD * LANE + k * LANE, LANE), LANE)
                e_buf[:, place] = both.astype(jnp.bfloat16)
            return carry

        whole = lon_count // (PAD * LANE)
        lax.fori_loop(0, whole, strip, 0)
        rest = lon_count - whole * PAD * LANE
        if rest:
            strip(whole, 0, tuple(min(LANE, rest - k * LANE) for k in range(PAD)))
        rows = jnp.dot(e_buf[...], t_buf[...], preferred_element_type=jnp.float32)
        rows = rows[0:PAD] + rows[PAD:]
        swapped = pltpu.roll(rows, RIM, 0)
        at = pl.multiple_of(jnp.where(top, 0, lat_rows - PAD), 8)
        fresh = jnp.where(top, row8, PAD - 1 - row8) < RIM
        cover = 2 * (lane8 % wave_count) < keep[pl.ds(at, PAD), :]
        for level, mine in enumerate(
            (jnp.where(top, rows, swapped), jnp.where(top, swapped, rows))
        ):
            place = pl.ds(pl.multiple_of(level * lat_rows + at, 8), PAD)
            spec[place, :] = jnp.where(fresh, jnp.where(cover, mine, 0.0), spec[place, :])

    halo_step(1, "wait_recv", odd)
    halo_step(0, "wait_recv", jnp.logical_not(odd))
    edge(odd)
    halo_step(0, "wait_recv", odd & (wide < n_wide - 1))
    halo_step(1, "wait_recv", jnp.logical_not(odd) & (wide > 0))
    edge(jnp.logical_not(odd))

    high, low = split(spec[...])
    chooser = pick[...].astype(jnp.bfloat16)
    moved = lax.dot_general(chooser, high, last_dims, preferred_element_type=jnp.float32)
    moved = moved + lax.dot_general(chooser, low, last_dims, preferred_element_type=jnp.float32)
    for at in range(n_wide):
        sent[at] = moved[8 * at : 8 * at + 4, :]

    turns = [1 - 2 * ((wide // bit) % 2) for bit in bits]

    def fourier_copy(code):
        to_wide = wide
        for bit, turn in zip(bits, turns):
            if code // n_narrow & bit:
                to_wide = to_wide + bit * turn
        to_narrow = 1 - narrow if code % n_narrow else narrow
        return pltpu.make_async_remote_copy(
            src_ref=sent.at[to_wide],
            dst_ref=got.at[me],
            send_sem=four_send,
            recv_sem=four_recv,
            device_id=(to_wide, to_narrow),
            device_id_type=MESH,
        )

    pl.semaphore_wait(entered, len(far))
    for code in range(total - 1, 0, -1):
        fourier_copy(code).start()
    got[me] = sent[wide]

    others = got.at[pl.ds(0, total - 1)]
    pltpu.make_async_copy(others, others, four_recv).wait()
    for at in range(n_wide):
        values = jnp.concatenate([got[n_narrow * at + j] for j in range(n_narrow)], axis=0)
        high, low = split(values)
        xs[:, LANE * at : LANE * at + LANE] = jnp.concatenate([high, low], axis=0)
    product = lax.dot_general(xs[...], lx[...], last_dims, preferred_element_type=jnp.float32)
    product = product[0:8] + product[8:16]
    product = product + pltpu.roll(product, LANE // 2, 1)
    by_level = []
    for level in range(levels):
        moved = product if level == 0 else pltpu.roll(product, LANE - level * block, 1)
        by_level.append(jnp.where(lane8 < owned, moved, pltpu.roll(moved, 6, 0)))
    for i in range(levels_all):
        result = sum(weights[i][level] * by_level[level] for level in range(levels))
        result = result + pltpu.roll(result, 4, 0)
        second = pltpu.roll(result, LANE - owned, 1)
        for c in range(2):
            out[c, i, 0:1, :] = result[c : c + 1, 0:owned]
            out[c, i, 1:2, :] = second[c : c + 1, 0:owned]
    pltpu.make_async_copy(others, others, four_send).wait()
    leg_copy.wait_send()
    halo_step(1, "wait_send", wide < n_wide - 1)
    halo_step(0, "wait_send", wide > 0)


def fused_fits(tracer, band_map, legendre, n_wide, n_narrow):
    levels, lat_rows = tracer.shape[0], tracer.shape[1]
    waves = band_map.shape[0]
    return (
        levels == 2
        and n_narrow == 2
        and lat_rows * levels == LANE
        and waves == n_wide * n_narrow
        and n_wide & (n_wide - 1) == 0
        and -(-tracer.shape[2] // LANE) % (CHUNKS * PAD) == 0
        and tracer.shape[2] > PAD * LANE
        and 4 * waves == LANE
        and legendre.shape[3] * 2 == n_wide * lat_rows
        and 2 * n_wide * 4 == LANE
    )


def fused(
    tracer, courant, nlon_counts, band_map, owner_map, legendre, modes_to, modes_from, mode_rates
):
    n_wide = lax.axis_size("wide")
    n_narrow = lax.axis_size("narrow")
    levels, lat_rows, lon_count = tracer.shape
    waves = band_map.shape[0]
    total = n_wide * n_narrow
    table = fourier_table(lon_count, waves)
    lon_pad = table.shape[0]
    tall = lat_rows + 2 * PAD
    half = legendre.shape[3]
    levels_all = levels * n_narrow
    vmem, smem, dma = pltpu.VMEM, pltpu.SMEM, pltpu.SemaphoreType.DMA
    operands = (
        tracer, courant, nlon_counts, band_map, owner_map,
        legendre.reshape(waves, half), modes_to, modes_from, mode_rates, jnp.asarray(table),
    )
    return pl.pallas_call(
        functools.partial(fused_kernel, n_wide, n_narrow, lon_count),
        out_shape=vmem((2, levels_all, 2, waves // n_narrow), jnp.float32),
        in_specs=[pl.BlockSpec(memory_space=pltpu.HBM)] * 10,
        out_specs=pl.BlockSpec(memory_space=pltpu.VMEM),
        scratch_shapes=[
            vmem((levels, tall, lon_count), jnp.float32),
            vmem((levels, tall, lon_count), jnp.float32),
            vmem((lon_pad, LANE), jnp.bfloat16),
            vmem((2 * levels * lat_rows, lon_pad), jnp.bfloat16),
            vmem((2 * PAD, lon_pad), jnp.bfloat16),
            vmem(((levels + 1) * PAD * TALL, LANE), jnp.float32),
            vmem(((levels + 1) * PAD * TALL, LANE), jnp.float32),
            vmem((PAD * PAD + PAD, LANE), jnp.float32),
            vmem((levels * lat_rows, LANE), jnp.float32),
            vmem((n_narrow, waves, half), jnp.float32),
            smem((lat_rows,), jnp.int32),
            smem((waves,), jnp.int32),
            smem((waves,), jnp.int32),
            smem((levels_all, levels_all), jnp.float32),
            smem((levels_all, levels_all), jnp.float32),
            smem((levels_all,), jnp.float32),
            vmem((8 * n_wide, LANE), jnp.float32),
            vmem((lat_rows, LANE), jnp.int32),
            vmem((waves // n_narrow, LANE), jnp.int32),
            vmem((n_wide, 4, LANE), jnp.float32),
            vmem((total, 4, LANE), jnp.float32),
            vmem((LANE, n_wide * LANE), jnp.bfloat16),
            vmem((16, n_wide * LANE), jnp.bfloat16),
            dma((6,)),
            dma((CHUNKS, 2)),
            dma,
            dma((2, 2)),
            dma((2, 2)),
            dma,
            dma((n_narrow,)),
            dma,
            dma,
            pltpu.SemaphoreType.REGULAR,
        ],
        compiler_params=pltpu.CompilerParams(
            collective_id=0, has_side_effects=True
        ),
    )(*(pltpu.with_memory_space_constraint(operand, pltpu.HBM) for operand in operands))


def program(tracer, courant, nlon_counts, band_map, owner_map, legendre, *modes):
    choose = (
        fused
        if fused_fits(
            tracer, band_map, legendre, lax.axis_size("wide"), lax.axis_size("narrow")
        )
        else body
    )
    return choose(tracer, courant, nlon_counts, band_map, owner_map, legendre, *modes)


def solution(mesh):
    placed = (
        P("narrow", "wide", None),
        P("narrow", "wide", None),
        P("wide"),
        P(),
        P(),
        P(("wide", "narrow"), None, None, None),
        P(),
        P(),
        P(),
    )
    return jax.shard_map(
        program, mesh=mesh, in_specs=placed, out_specs=P(None, None, "wide", "narrow"), check_vma=False
    )
```

```python
import functools
import math

import jax
import jax.numpy as jnp
import numpy as np
from jax import lax
from jax.experimental import pallas as pl
from jax.experimental.pallas import tpu as pltpu
from jax.sharding import PartitionSpec as P

NLAT = 1024


def extended(array, sides, width):
    for axis, dim in sides:
        devices, length = (lax.axis_size(axis), array.shape[dim])
        up = [(i, (i + 1) % devices) for i in range(devices - 1)]
        down = [(j, i) for i, j in up]
        last = lax.slice_in_dim(array, length - width, length, axis=dim)
        initial = lax.slice_in_dim(array, 0, width, axis=dim)
        before = lax.ppermute(last, axis, up)
        after = lax.ppermute(initial, axis, down)
        array = jnp.concatenate([before, array, after], axis=dim)
    return array


def advect_section(field_ext, rate_ext, open_faces):
    row_total = field_ext.shape[1]
    row_below = field_ext[:, 0 : row_total - 3]
    row_here = field_ext[:, 1 : row_total - 2]
    row_above = field_ext[:, 2 : row_total - 1]
    row_beyond = field_ext[:, 3:row_total]
    face_rate = rate_ext[:, 1 : row_total - 2] * open_faces[1 : row_total - 2][:, None]
    upwind = (5.0 * row_here + 2.0 * row_above - row_below) / 6.0
    downwind = (5.0 * row_above + 2.0 * row_here - row_beyond) / 6.0
    low_bound = jnp.minimum(row_here, row_above)
    high_bound = jnp.maximum(row_here, row_above)
    face_value = jnp.clip(jnp.where(face_rate >= 0.0, upwind, downwind), low_bound, high_bound)
    face_flux = face_rate * face_value
    return field_ext[:, 2 : row_total - 2] - (face_flux[:, 1:] - face_flux[:, :-1])


def valid_rows(first_row, lat_rows, rim_width):
    row_ids = first_row + jnp.arange(lat_rows + 2 * rim_width, dtype=jnp.int32) - rim_width
    return ((row_ids >= 0) & (row_ids < NLAT - 1)).astype(jnp.float32)


def longitude_transform(advected, wave_count):
    levels_dev, lat_rows, lon_count = advected.shape
    short_len = 32
    long_len = lon_count // short_len
    block_count = wave_count // short_len
    row_count = levels_dev * lat_rows
    grid_rows = advected.reshape(row_count, short_len, long_len)
    short_ids = jnp.arange(short_len, dtype=jnp.int32)
    turn_one = short_ids[:, None] * short_ids[None, :] % short_len
    angle_one = 2.0 * math.pi / short_len * turn_one.astype(jnp.float32)
    highest = lax.Precision.HIGHEST
    inner_re = jnp.einsum("pab,ar->prb", grid_rows, jnp.cos(angle_one), precision=highest)
    inner_im = -jnp.einsum("pab,ar->prb", grid_rows, jnp.sin(angle_one), precision=highest)
    long_ids = jnp.arange(long_len, dtype=jnp.int32)
    block_ids = jnp.arange(block_count, dtype=jnp.int32)
    wave_ids = short_len * block_ids[None, None, :] + short_ids[:, None, None]
    turn_two = wave_ids * long_ids[None, :, None] % lon_count
    angle_two = 2.0 * math.pi / lon_count * turn_two.astype(jnp.float32)
    cos_two = jnp.cos(angle_two)
    sin_two = jnp.sin(angle_two)
    outer_re = jnp.einsum("prb,rbc->crp", inner_re, cos_two, precision=highest) + jnp.einsum(
        "prb,rbc->crp", inner_im, sin_two, precision=highest
    )
    outer_im = jnp.einsum("prb,rbc->crp", inner_im, cos_two, precision=highest) - jnp.einsum(
        "prb,rbc->crp", inner_re, sin_two, precision=highest
    )
    outer_re = (outer_re / math.sqrt(lon_count)).reshape(wave_count, levels_dev, lat_rows)
    outer_im = (outer_im / math.sqrt(lon_count)).reshape(wave_count, levels_dev, lat_rows)
    return jnp.stack([outer_re, outer_im], axis=1)


def body(
    tracer, courant, nlon_counts, band_map, owner_map, legendre, modes_to, modes_from, mode_rates
):
    levels_dev = tracer.shape[0]
    lat_rows = tracer.shape[1]
    n_wide = lax.axis_size("wide")
    n_narrow = lax.axis_size("narrow")
    first_row = lax.axis_index("wide") * lat_rows
    stacked = jnp.stack([tracer, courant])
    padded = extended(stacked, (("wide", 2),), 4)
    open_faces = valid_rows(first_row, lat_rows, 4)
    section_one = advect_section(padded[0], padded[1], open_faces)
    section_two = advect_section(section_one, padded[1][:, 2:-2], open_faces[2:-2])
    advected = 0.5 * tracer + 0.5 * section_two
    wave_count = band_map.shape[0]
    fourier = longitude_transform(advected, wave_count)
    wave_ids = jnp.arange(wave_count, dtype=jnp.int32)
    kept_mask = (2 * wave_ids[:, None] < nlon_counts[None, :]).astype(jnp.float32)
    fourier = fourier * kept_mask[:, None, None, :]
    slot_count = wave_count // (n_wide * n_narrow)
    fourier = jnp.einsum(
        "sm,mclj->sclj", (band_map[:, None] == wave_ids[None, :]).astype(jnp.float32), fourier,
        precision=lax.Precision.HIGHEST,
    )
    fourier = lax.all_to_all(fourier, "wide", split_axis=0, concat_axis=3, tiled=True)
    fourier = lax.all_to_all(fourier, "narrow", split_axis=0, concat_axis=2, tiled=True)
    levels_all = levels_dev * n_narrow
    half_rows = fourier.shape[3] // 2
    north_half = fourier[:, :, :, :half_rows]
    south_half = jnp.flip(fourier[:, :, :, half_rows:], axis=3)
    sym_part = north_half + south_half
    anti_part = north_half - south_half
    slot_start = (lax.axis_index("wide") * n_narrow + lax.axis_index("narrow")) * slot_count
    slot_waves = lax.dynamic_slice_in_dim(band_map, slot_start, slot_count)
    same_parity = (jnp.arange(2, dtype=jnp.int32)[None, :] - slot_waves[:, None]) % 2 == 0
    chosen = jnp.where(same_parity[:, :, None, None, None], sym_part[:, None], anti_part[:, None])
    spectral = jnp.einsum("spkj,spclj->spkcl", legendre, chosen, precision=lax.Precision.HIGHEST)
    degree_ids = (
        2 * jnp.arange(wave_count // 2, dtype=jnp.int32)[None, :]
        + jnp.arange(2, dtype=jnp.int32)[:, None]
    )
    upper_mask = (degree_ids[None] >= slot_waves[:, None, None]).astype(jnp.float32)
    spectral = spectral * upper_mask[:, :, :, None, None]
    spectral = jnp.transpose(spectral, (0, 2, 1, 3, 4)).reshape(
        slot_count, wave_count, 2, levels_all
    )
    spectral = jnp.einsum(
        "tn,sncl->stcl", (owner_map[:, None] == wave_ids[None, :]).astype(jnp.float32), spectral,
        precision=lax.Precision.HIGHEST,
    )
    gathered = lax.all_to_all(spectral, "narrow", split_axis=1, concat_axis=0, tiled=True)
    owned = gathered.shape[1]
    owned_degrees = lax.dynamic_slice_in_dim(owner_map, lax.axis_index("narrow") * owned, owned)
    degree_sq = (owned_degrees * (owned_degrees + 1)).astype(jnp.float32)
    damping = 1.0 / (1.0 + degree_sq[None, :] * mode_rates[:, None])
    modal_part = jnp.einsum("kl,stcl->kstc", modes_to, gathered, precision=lax.Precision.HIGHEST)
    scaled = modal_part * damping[:, None, :, None]
    return jnp.einsum("ik,kstc->cist", modes_from, scaled, precision=lax.Precision.HIGHEST)


MESH = pl.DeviceIdType.MESH
LANE = 128
PAD = 8
RIM = 4
CHUNKS = 4
STRIP = 512
TALL = 17
HALO = {1: (3, 2), 0: (3, 1)}


def chunk_list(lon_count, count):
    tiles = -(-lon_count // LANE)
    cuts = [min(lon_count, LANE * (tiles * cut // count)) for cut in range(count + 1)]
    return [(lo, hi - lo) for lo, hi in zip(cuts, cuts[1:])]


def fourier_table(lon_count, wave_count):
    rows = -(-lon_count // LANE) * LANE
    turns = np.outer(np.arange(lon_count), np.arange(wave_count)) % lon_count
    angle = 2.0 * np.pi / lon_count * turns
    full = np.concatenate([np.cos(angle), -np.sin(angle)], axis=1) * (0.5 / np.sqrt(lon_count))
    high = full.astype(jnp.bfloat16)
    low = (full - high.astype(np.float64)).astype(jnp.bfloat16)
    table = np.zeros((rows, LANE), jnp.bfloat16)
    table[:lon_count] = np.concatenate([high, low], axis=1)
    return table


def split(value):
    high = value.astype(jnp.bfloat16)
    low = (value - high.astype(jnp.float32)).astype(jnp.bfloat16)
    return high, low


def face_flux(field, rate, ahead):
    rows = field.shape[0]
    above = pltpu.roll(field, rows - 1, 0)
    step = above - field
    near = jnp.where(ahead, pltpu.roll(step, 1, 0), pltpu.roll(step, rows - 1, 0))
    slope = step * (1.0 / 3.0) + near * (1.0 / 6.0)
    slope = jnp.maximum(jnp.minimum(slope, jnp.maximum(step, 0.0)), jnp.minimum(step, 0.0))
    return rate * jnp.where(ahead, field + slope, above - slope)


def section(field, rate, ahead):
    flux = face_flux(field, rate, ahead)
    return field - (flux - pltpu.roll(flux, 1, 0))


def rim_flux(field, step, rate, ahead, face):
    here = step[face]
    near = jnp.where(ahead[face], step[face - 1], step[face + 1])
    slope = here * (1.0 / 3.0) + near * (1.0 / 6.0)
    slope = jnp.maximum(jnp.minimum(slope, jnp.maximum(here, 0.0)), jnp.minimum(here, 0.0))
    return rate[face] * jnp.where(ahead[face], field[face] + slope, field[face + 1] - slope)


def rim_section(field_row, rate_row, top):
    field = {row: field_row(row) for row in range(-4, RIM + 4)}
    rate = {row: rate_row(row) for row in range(-3, RIM + 2)}
    ahead = {row: rate[row] >= 0.0 for row in rate}
    step = {row: field[row + 1] - field[row] for row in range(-4, RIM + 3)}
    flux = {row: rim_flux(field, step, rate, ahead, row) for row in range(-3, RIM + 2)}
    flux[-3] = jnp.where(top, field[-4], flux[-3])
    flux[RIM + 1] = jnp.where(top, flux[RIM + 1], field[RIM + 3])
    once = {row: field[row] - (flux[row] - flux[row - 1]) for row in range(-2, RIM + 2)}
    step = {row: once[row + 1] - once[row] for row in range(-2, RIM + 1)}
    flux = {row: rim_flux(once, step, rate, ahead, row) for row in range(-1, RIM)}
    return [field[row] + (once[row] - (flux[row] - flux[row - 1])) for row in range(RIM)]


def ids(shape, dim):
    return lax.broadcasted_iota(jnp.int32, shape, dim)


def fused_kernel(
    n_wide, n_narrow, lon_count,
    tracer, courant, nlon, band, owner, legendre, modes_to, modes_from, rates, table,
    out,
    q_buf, c_buf, t_buf, a_buf, e_buf, f_buf, q_tall, c_tall, rim, spec, leg, nlon_s, band_s, owner_s, to_s, from_s, rate_s,
    pick, keep, degree, sent, got, lx, xs,
    small_sem, load_sem, table_sem, halo_send, halo_recv, leg_send, leg_recv, four_send, four_recv,
    entered,
):
    wide, narrow = lax.axis_index("wide"), lax.axis_index("narrow")
    total = n_wide * n_narrow
    me = wide * n_narrow + narrow
    levels, lat_rows = tracer.shape[0], tracer.shape[1]
    wave_count = band_s.shape[0]
    lon_pad = t_buf.shape[0]
    chunks = chunk_list(lon_count, CHUNKS)
    owned = wave_count // n_narrow
    half_waves = wave_count // 2
    row_total = levels * lat_rows

    barrier = pltpu.get_barrier_semaphore()

    bits = [2**k for k in range(n_wide.bit_length() - 1)]
    low = 2 ** (len(bits) // 2)
    high = n_wide // low
    far_at, near_at = wide // low, wide % low
    near = [
        (far_at * low + (near_at + a) % low, (narrow + b) % n_narrow)
        for a in range(low)
        for b in range(n_narrow)
        if a or b
    ]
    far = [(((far_at + a) % high) * low + near_at, narrow) for a in range(1, high)]
    last_near, first_near = near_at == low - 1, near_at == 0
    crosses = (last_near & (far_at < high - 1)) | (first_near & (far_at > 0))

    @pl.when(crosses)
    def _():
        pl.semaphore_signal(
            barrier,
            inc=1,
            device_id=(jnp.where(last_near, wide + 1, wide - 1), narrow),
            device_id_type=MESH,
        )

    for other in near + far:
        pl.semaphore_signal(barrier, inc=1, device_id=other, device_id_type=MESH)

    smalls = []
    for at, (here, there) in enumerate(
        ((nlon, nlon_s), (band, band_s), (owner, owner_s), (modes_to, to_s), (modes_from, from_s), (rates, rate_s))
    ):
        smalls.append(pltpu.make_async_copy(here, there, small_sem.at[at]))
    for copy in smalls:
        copy.start()
    loads = []
    for at, (lo, size) in enumerate(chunks):
        pair = []
        for which, (here, there) in enumerate(((tracer, q_buf), (courant, c_buf))):
            copy = pltpu.make_async_copy(
                here.at[:, :, pl.ds(lo, size)],
                there.at[:, pl.ds(PAD, lat_rows), pl.ds(lo, size)],
                load_sem.at[at, which],
            )
            copy.start()
            pair.append(copy)
        loads.append(pair)
    table_copy = pltpu.make_async_copy(table, t_buf, table_sem)
    table_copy.start()
    own_leg = pltpu.make_async_copy(legendre, leg.at[narrow], leg_recv.at[narrow])
    own_leg.start()

    @pl.when(wide == 0)
    def _():
        q_buf[:, 0:PAD, :] = jnp.zeros((levels, PAD, lon_count), jnp.float32)
        c_buf[:, 0:PAD, :] = jnp.zeros((levels, PAD, lon_count), jnp.float32)

    @pl.when(wide == n_wide - 1)
    def _():
        q_buf[:, PAD + lat_rows :, :] = jnp.zeros((levels, PAD, lon_count), jnp.float32)
        c_buf[:, PAD + lat_rows :, :] = jnp.zeros((levels, PAD, lon_count), jnp.float32)

    greeted = len(near) + len(far)

    @pl.when(crosses)
    def _():
        pl.semaphore_wait(barrier, greeted + 1)

    @pl.when(jnp.logical_not(crosses))
    def _():
        pl.semaphore_wait(barrier, greeted)

    for other in far:
        pl.semaphore_signal(entered, inc=1, device_id=other, device_id_type=MESH)

    def halo(up, which):
        here, there = ((tracer, q_buf), (courant, c_buf), (f_buf, q_buf))[which]
        if which == 2:
            count = 1
            first = PAD - RIM + 1 if up else 1
            land = PAD - RIM if up else PAD + lat_rows + RIM - 1
        else:
            count = HALO[up][which]
            first = lat_rows - count if up else 0
            land = PAD - count if up else PAD + lat_rows
        return pltpu.make_async_remote_copy(
            src_ref=here.at[:, pl.ds(first, count), :],
            dst_ref=there.at[:, pl.ds(land, count), :],
            send_sem=halo_send.at[up, which],
            recv_sem=halo_recv.at[up, which],
            device_id=(wide + 1 if up else wide - 1, narrow),
            device_id_type=MESH,
        )

    odd = wide % 2 == 1

    def halo_step(up, what, cond, parts=(0, 1, 2)):
        @pl.when(cond)
        def _():
            for which in parts:
                getattr(halo(up, which), what)()

    def send_halos(parts):
        halo_step(1, "start", odd & (wide < n_wide - 1), parts)
        halo_step(0, "start", jnp.logical_not(odd) & (wide > 0), parts)
        halo_step(0, "start", odd, parts)
        halo_step(1, "start", jnp.logical_not(odd), parts)

    send_halos((0, 1))

    leg_copy = pltpu.make_async_remote_copy(
        src_ref=legendre,
        dst_ref=leg.at[narrow],
        send_sem=leg_send,
        recv_sem=leg_recv.at[narrow],
        device_id=(wide, 1 - narrow),
        device_id_type=MESH,
    )
    leg_copy.start()

    for copy in smalls:
        copy.wait()
    row8, lane8 = ids((8, LANE), 0), ids((8, LANE), 1)
    for at in range(n_wide):
        wave = jnp.where(row8 < 2, band_s[2 * at], band_s[2 * at + 1])
        column = (row8 % 2) * wave_count + wave
        hit = (row8 < 4) & (lane8 % (2 * wave_count) == column)
        pick[8 * at : 8 * at + 8, :] = jnp.where(hit, 1.0, 0.0)
    for row in range(lat_rows):
        keep[row : row + 1, :] = jnp.full((1, LANE), nlon_s[row], jnp.int32)
    for row in range(owned):
        degree[row : row + 1, :] = jnp.full((1, LANE), owner_s[narrow * owned + row], jnp.int32)

    lane1 = ids((1, LANE), 1)
    number = jnp.zeros((1, LANE), jnp.int32)
    for at in range(owned):
        number = jnp.where(lane1 % owned == at, owner_s[narrow * owned + at], number)
    squared = (number * (number + 1)).astype(jnp.float32)
    levels_all = levels * n_narrow
    damping = [1.0 / (1.0 + squared * rate_s[k]) for k in range(levels_all)]
    mix = [
        [
            sum((from_s[i, k] * to_s[k, l]) * damping[k] for k in range(levels_all))
            for l in range(levels_all)
        ]
        for i in range(levels_all)
    ]

    weights = [
        [
            jnp.where(row8 < 4, mix[i][level], mix[i][levels + level])
            for level in range(levels)
        ]
        for i in range(levels_all)
    ]
    a_buf[:, lon_pad - LANE :] = jnp.zeros((2 * row_total, LANE), jnp.bfloat16)

    def outer_flux(step, carry, lanes=STRIP):
        place = pl.ds(pl.multiple_of(step * STRIP, STRIP), lanes)
        lower = ids((PAD, lanes), 0) < RIM
        for level in range(levels):
            field, rate = (
                jnp.where(
                    lower,
                    buf[level, PAD : 2 * PAD, place],
                    buf[level, lat_rows : PAD + lat_rows, place],
                )
                for buf in (q_buf, c_buf)
            )
            f_buf[level, :, place] = face_flux(field, rate, rate >= 0.0)
        return carry

    width = lon_pad // CHUNKS
    for at in range(CHUNKS):
        for pair in loads[0:1] if at == 0 else loads[1:] if at == 1 else ():
            pair[0].wait()
            pair[1].wait()
        if at == 1:
            strips, extra = divmod(lon_count, STRIP)
            lax.fori_loop(0, strips, outer_flux, 0)
            if extra:
                outer_flux(strips, 0, extra)
            send_halos((2,))

        def tile(step, carry, lo=at * width, lanes=LANE):
            columns = pl.ds(pl.multiple_of(lo + step * LANE, LANE), lanes)
            for level in range(levels):
                field = q_buf[level, PAD : PAD + lat_rows, columns]
                rate = c_buf[level, PAD : PAD + lat_rows, columns]
                ahead = rate >= 0.0
                twice = section(section(field, rate, ahead), rate, ahead)
                high, low = split(field + twice)
                first = level * lat_rows
                a_buf[first : first + lat_rows, columns] = high
                a_buf[row_total + first : row_total + first + lat_rows, columns] = low
            return carry

        whole, rest = divmod(chunks[at][1], LANE)
        lax.fori_loop(0, whole, tile, 0)
        if rest:
            tile(whole, 0, lanes=rest)
    table_copy.wait()
    spectrum = jnp.dot(a_buf[...], t_buf[...], preferred_element_type=jnp.float32)
    spectrum = spectrum[0:row_total] + spectrum[row_total:]
    kept = 2 * (ids((lat_rows, LANE), 1) % wave_count) < keep[...]
    spec[...] = jnp.where(jnp.concatenate([kept] * levels, axis=0), spectrum, 0.0)

    @pl.when(wide == n_wide - 1)
    def _():
        last = PAD + lat_rows - 1
        c_buf[:, last : last + 1, :] = jnp.zeros((levels, 1, lon_count), jnp.float32)

    last_dims = (((1,), (1,)), ((), ()))

    def edge(top, slab):
        start = pl.multiple_of(jnp.where(top, 0, lat_rows), 8)
        first = jnp.where(top, PAD, PAD - RIM)

        def strip(step, carry, tiles=(LANE,) * PAD):
            places = [
                pl.ds(pl.multiple_of(step * PAD * LANE + k * LANE, LANE), lanes)
                for k, lanes in enumerate(tiles)
            ]
            for level in range(levels):
                for k, place in enumerate(places):
                    here = pl.ds((level * PAD + k) * TALL, 2 * PAD)
                    q_tall[here, 0 : tiles[k]] = q_buf[level, pl.ds(start, 2 * PAD), place]
                    c_tall[here, 0 : tiles[k]] = c_buf[level, pl.ds(start, 2 * PAD), place]
            for level in range(levels):
                base = level * PAD * TALL + first
                values = rim_section(
                    lambda row: q_tall[pl.ds(base + row, PAD, stride=TALL), :],
                    lambda row: c_tall[pl.ds(base + row, PAD, stride=TALL), :],
                    top,
                )
                for row, value in enumerate(values):
                    rim[pl.ds(level * RIM + row, PAD, stride=PAD), :] = value
            for k in range(PAD):
                value = rim[k * PAD : k * PAD + PAD, :]
                high = value.astype(jnp.bfloat16).astype(jnp.float32)
                both = jnp.concatenate([high, value - high], axis=0)
                place = pl.ds(pl.multiple_of(step * PAD * LANE + k * LANE, LANE), LANE)
                e_buf[pl.ds(slab, 2 * PAD), place] = both.astype(jnp.bfloat16)
            return carry

        whole = lon_count // (PAD * LANE)
        lax.fori_loop(0, whole, strip, 0)
        rest = lon_count - whole * PAD * LANE
        if rest:
            strip(whole, 0, tuple(min(LANE, rest - k * LANE) for k in range(PAD)))
    def replace(top, rows):
        rows = rows[0:PAD] + rows[PAD:]
        swapped = pltpu.roll(rows, RIM, 0)
        at = pl.multiple_of(jnp.where(top, 0, lat_rows - PAD), 8)
        fresh = jnp.where(top, row8, PAD - 1 - row8) < RIM
        cover = 2 * (lane8 % wave_count) < keep[pl.ds(at, PAD), :]
        for level, mine in enumerate(
            (jnp.where(top, rows, swapped), jnp.where(top, swapped, rows))
        ):
            place = pl.ds(pl.multiple_of(level * lat_rows + at, 8), PAD)
            spec[place, :] = jnp.where(fresh, jnp.where(cover, mine, 0.0), spec[place, :])

    halo_step(1, "wait_recv", odd)
    halo_step(0, "wait_recv", jnp.logical_not(odd))
    edge(odd, 0)
    halo_step(0, "wait_recv", odd & (wide < n_wide - 1))
    halo_step(1, "wait_recv", jnp.logical_not(odd) & (wide > 0))
    edge(jnp.logical_not(odd), 2 * PAD)
    rows = jnp.dot(e_buf[...], t_buf[...], preferred_element_type=jnp.float32)
    replace(odd, rows[0 : 2 * PAD])
    replace(jnp.logical_not(odd), rows[2 * PAD :])

    high, low = split(spec[...])
    chooser = pick[...].astype(jnp.bfloat16)
    moved = lax.dot_general(chooser, high, last_dims, preferred_element_type=jnp.float32)
    moved = moved + lax.dot_general(chooser, low, last_dims, preferred_element_type=jnp.float32)
    for at in range(n_wide):
        sent[at] = moved[8 * at : 8 * at + 4, :]

    turns = [1 - 2 * ((wide // bit) % 2) for bit in bits]

    def fourier_copy(code):
        to_wide = wide
        for bit, turn in zip(bits, turns):
            if code // n_narrow & bit:
                to_wide = to_wide + bit * turn
        to_narrow = 1 - narrow if code % n_narrow else narrow
        return pltpu.make_async_remote_copy(
            src_ref=sent.at[to_wide],
            dst_ref=got.at[me],
            send_sem=four_send,
            recv_sem=four_recv,
            device_id=(to_wide, to_narrow),
            device_id_type=MESH,
        )

    pl.semaphore_wait(entered, len(far))
    for code in range(total - 1, 0, -1):
        fourier_copy(code).start()
    got[me] = sent[wide]

    own_leg.wait()
    pltpu.make_async_remote_copy(
        src_ref=legendre,
        dst_ref=leg.at[1 - narrow],
        send_sem=leg_send,
        recv_sem=leg_recv.at[1 - narrow],
        device_id=(wide, 1 - narrow),
        device_id_type=MESH,
    ).wait_recv()

    degrees = degree[:, 0:wave_count]
    flat = ids((owned, wave_count), 1)
    held = 2 * (flat % half_waves) + flat // half_waves
    north, south = [], []
    for slot in range(n_narrow):
        wave = band_s[wide * n_narrow + slot]
        chosen = jnp.where((held == degrees) & (degrees >= wave), 1.0, 0.0)
        even = ((degrees + wave) % 2) == 0
        north.append(chosen.astype(jnp.bfloat16))
        south.append(jnp.where(even, chosen, -chosen).astype(jnp.bfloat16))
    leg_parts = [split(leg[slot]) for slot in range(n_narrow)]
    block = n_narrow * owned

    def rows_of(picks):
        return jnp.concatenate(
            [
                jnp.dot(picks[slot], leg_parts[slot][half], preferred_element_type=jnp.float32)
                for half in range(2)
                for slot in range(n_narrow)
            ],
            axis=0,
        )

    source, lane = ids((LANE, LANE), 0), ids((LANE, LANE), 1)
    lane_rows = ids((block, LANE), 1)
    tiles = leg.shape[2] // LANE
    for southern, picks in ((False, north), (True, south)):
        rows = rows_of(picks).astype(jnp.bfloat16)
        tall = jnp.concatenate([rows[:, LANE * a : LANE * a + LANE] for a in range(tiles)], axis=0)
        for half in range(2):
            within = lane % lat_rows
            if southern:
                within = lat_rows - 1 - within
            spread = jnp.where(source == half * lat_rows + within, 1.0, 0.0).astype(jnp.bfloat16)
            wide_rows = jnp.dot(tall, spread, preferred_element_type=jnp.float32)
            for a in range(tiles):
                lat_block = 2 * a + half
                if southern:
                    lat_block = n_wide - 1 - lat_block
                for part in range(2):
                    piece = wide_rows[(a * 2 + part) * block : (a * 2 + part + 1) * block]
                    for level in range(levels):
                        kept_piece = jnp.where(lane_rows // lat_rows == level, piece, 0.0)
                        first = (part * levels + level) * block
                        lx[first : first + block, LANE * lat_block : LANE * lat_block + LANE] = (
                            kept_piece.astype(jnp.bfloat16)
                        )

    others = got.at[pl.ds(0, total - 1)]
    pltpu.make_async_copy(others, others, four_recv).wait()
    for at in range(n_wide):
        values = jnp.concatenate([got[n_narrow * at + j] for j in range(n_narrow)], axis=0)
        high, low = split(values)
        xs[:, LANE * at : LANE * at + LANE] = jnp.concatenate([high, low], axis=0)
    product = lax.dot_general(xs[...], lx[...], last_dims, preferred_element_type=jnp.float32)
    product = product[0:8] + product[8:16]
    product = product + pltpu.roll(product, LANE // 2, 1)
    by_level = []
    for level in range(levels):
        moved = product if level == 0 else pltpu.roll(product, LANE - level * block, 1)
        by_level.append(jnp.where(lane8 < owned, moved, pltpu.roll(moved, 6, 0)))
    for i in range(levels_all):
        result = sum(weights[i][level] * by_level[level] for level in range(levels))
        result = result + pltpu.roll(result, 4, 0)
        second = pltpu.roll(result, LANE - owned, 1)
        for c in range(2):
            out[c, i, 0:1, :] = result[c : c + 1, 0:owned]
            out[c, i, 1:2, :] = second[c : c + 1, 0:owned]
    pltpu.make_async_copy(others, others, four_send).wait()
    leg_copy.wait_send()
    halo_step(1, "wait_send", wide < n_wide - 1)
    halo_step(0, "wait_send", wide > 0)


def fused_fits(tracer, band_map, legendre, n_wide, n_narrow):
    levels, lat_rows = tracer.shape[0], tracer.shape[1]
    waves = band_map.shape[0]
    return (
        levels == 2
        and n_narrow == 2
        and lat_rows * levels == LANE
        and waves == n_wide * n_narrow
        and n_wide & (n_wide - 1) == 0
        and -(-tracer.shape[2] // LANE) % CHUNKS == 0
        and -(-tracer.shape[2] // LANE) % PAD == 0
        and tracer.shape[2] > PAD * LANE
        and 4 * waves == LANE
        and legendre.shape[3] * 2 == n_wide * lat_rows
        and 2 * n_wide * 4 == LANE
    )


def fused(
    tracer, courant, nlon_counts, band_map, owner_map, legendre, modes_to, modes_from, mode_rates
):
    n_wide = lax.axis_size("wide")
    n_narrow = lax.axis_size("narrow")
    levels, lat_rows, lon_count = tracer.shape
    waves = band_map.shape[0]
    total = n_wide * n_narrow
    table = fourier_table(lon_count, waves)
    lon_pad = table.shape[0]
    tall = lat_rows + 2 * PAD
    half = legendre.shape[3]
    levels_all = levels * n_narrow
    vmem, smem, dma = pltpu.VMEM, pltpu.SMEM, pltpu.SemaphoreType.DMA
    operands = (
        tracer, courant, nlon_counts, band_map, owner_map,
        legendre.reshape(waves, half), modes_to, modes_from, mode_rates, jnp.asarray(table),
    )
    return pl.pallas_call(
        functools.partial(fused_kernel, n_wide, n_narrow, lon_count),
        out_shape=vmem((2, levels_all, 2, waves // n_narrow), jnp.float32),
        in_specs=[pl.BlockSpec(memory_space=pltpu.HBM)] * 10,
        out_specs=pl.BlockSpec(memory_space=pltpu.VMEM),
        scratch_shapes=[
            vmem((levels, tall, lon_count), jnp.float32),
            vmem((levels, tall, lon_count), jnp.float32),
            vmem((lon_pad, LANE), jnp.bfloat16),
            vmem((2 * levels * lat_rows, lon_pad), jnp.bfloat16),
            vmem((4 * PAD, lon_pad), jnp.bfloat16),
            vmem((levels, PAD, lon_count), jnp.float32),
            vmem(((levels + 1) * PAD * TALL, LANE), jnp.float32),
            vmem(((levels + 1) * PAD * TALL, LANE), jnp.float32),
            vmem((PAD * PAD + PAD, LANE), jnp.float32),
            vmem((levels * lat_rows, LANE), jnp.float32),
            vmem((n_narrow, waves, half), jnp.float32),
            smem((lat_rows,), jnp.int32),
            smem((waves,), jnp.int32),
            smem((waves,), jnp.int32),
            smem((levels_all, levels_all), jnp.float32),
            smem((levels_all, levels_all), jnp.float32),
            smem((levels_all,), jnp.float32),
            vmem((8 * n_wide, LANE), jnp.float32),
            vmem((lat_rows, LANE), jnp.int32),
            vmem((waves // n_narrow, LANE), jnp.int32),
            vmem((n_wide, 4, LANE), jnp.float32),
            vmem((total, 4, LANE), jnp.float32),
            vmem((LANE, n_wide * LANE), jnp.bfloat16),
            vmem((16, n_wide * LANE), jnp.bfloat16),
            dma((6,)),
            dma((CHUNKS, 2)),
            dma,
            dma((2, 3)),
            dma((2, 3)),
            dma,
            dma((n_narrow,)),
            dma,
            dma,
            pltpu.SemaphoreType.REGULAR,
        ],
        compiler_params=pltpu.CompilerParams(
            collective_id=0, has_side_effects=True
        ),
    )(*(pltpu.with_memory_space_constraint(operand, pltpu.HBM) for operand in operands))


def program(tracer, courant, nlon_counts, band_map, owner_map, legendre, *modes):
    choose = (
        fused
        if fused_fits(
            tracer, band_map, legendre, lax.axis_size("wide"), lax.axis_size("narrow")
        )
        else body
    )
    return choose(tracer, courant, nlon_counts, band_map, owner_map, legendre, *modes)


def solution(mesh):
    placed = (
        P("narrow", "wide", None),
        P("narrow", "wide", None),
        P("wide"),
        P(),
        P(),
        P(("wide", "narrow"), None, None, None),
        P(),
        P(),
        P(),
    )
    return jax.shard_map(
        program, mesh=mesh, in_specs=placed, out_specs=P(None, None, "wide", "narrow"), check_vma=False
    )
```

```python
import functools
import math

import jax
import jax.numpy as jnp
import numpy as np
from jax import lax
from jax.experimental import pallas as pl
from jax.experimental.pallas import tpu as pltpu
from jax.sharding import PartitionSpec as P

NLAT = 1024


def extended(array, sides, width):
    for axis, dim in sides:
        devices, length = (lax.axis_size(axis), array.shape[dim])
        up = [(i, (i + 1) % devices) for i in range(devices - 1)]
        down = [(j, i) for i, j in up]
        last = lax.slice_in_dim(array, length - width, length, axis=dim)
        initial = lax.slice_in_dim(array, 0, width, axis=dim)
        before = lax.ppermute(last, axis, up)
        after = lax.ppermute(initial, axis, down)
        array = jnp.concatenate([before, array, after], axis=dim)
    return array


def advect_section(field_ext, rate_ext, open_faces):
    row_total = field_ext.shape[1]
    row_below = field_ext[:, 0 : row_total - 3]
    row_here = field_ext[:, 1 : row_total - 2]
    row_above = field_ext[:, 2 : row_total - 1]
    row_beyond = field_ext[:, 3:row_total]
    face_rate = rate_ext[:, 1 : row_total - 2] * open_faces[1 : row_total - 2][:, None]
    upwind = (5.0 * row_here + 2.0 * row_above - row_below) / 6.0
    downwind = (5.0 * row_above + 2.0 * row_here - row_beyond) / 6.0
    low_bound = jnp.minimum(row_here, row_above)
    high_bound = jnp.maximum(row_here, row_above)
    face_value = jnp.clip(jnp.where(face_rate >= 0.0, upwind, downwind), low_bound, high_bound)
    face_flux = face_rate * face_value
    return field_ext[:, 2 : row_total - 2] - (face_flux[:, 1:] - face_flux[:, :-1])


def valid_rows(first_row, lat_rows, rim_width):
    row_ids = first_row + jnp.arange(lat_rows + 2 * rim_width, dtype=jnp.int32) - rim_width
    return ((row_ids >= 0) & (row_ids < NLAT - 1)).astype(jnp.float32)


def longitude_transform(advected, wave_count):
    levels_dev, lat_rows, lon_count = advected.shape
    short_len = 32
    long_len = lon_count // short_len
    block_count = wave_count // short_len
    row_count = levels_dev * lat_rows
    grid_rows = advected.reshape(row_count, short_len, long_len)
    short_ids = jnp.arange(short_len, dtype=jnp.int32)
    turn_one = short_ids[:, None] * short_ids[None, :] % short_len
    angle_one = 2.0 * math.pi / short_len * turn_one.astype(jnp.float32)
    highest = lax.Precision.HIGHEST
    inner_re = jnp.einsum("pab,ar->prb", grid_rows, jnp.cos(angle_one), precision=highest)
    inner_im = -jnp.einsum("pab,ar->prb", grid_rows, jnp.sin(angle_one), precision=highest)
    long_ids = jnp.arange(long_len, dtype=jnp.int32)
    block_ids = jnp.arange(block_count, dtype=jnp.int32)
    wave_ids = short_len * block_ids[None, None, :] + short_ids[:, None, None]
    turn_two = wave_ids * long_ids[None, :, None] % lon_count
    angle_two = 2.0 * math.pi / lon_count * turn_two.astype(jnp.float32)
    cos_two = jnp.cos(angle_two)
    sin_two = jnp.sin(angle_two)
    outer_re = jnp.einsum("prb,rbc->crp", inner_re, cos_two, precision=highest) + jnp.einsum(
        "prb,rbc->crp", inner_im, sin_two, precision=highest
    )
    outer_im = jnp.einsum("prb,rbc->crp", inner_im, cos_two, precision=highest) - jnp.einsum(
        "prb,rbc->crp", inner_re, sin_two, precision=highest
    )
    outer_re = (outer_re / math.sqrt(lon_count)).reshape(wave_count, levels_dev, lat_rows)
    outer_im = (outer_im / math.sqrt(lon_count)).reshape(wave_count, levels_dev, lat_rows)
    return jnp.stack([outer_re, outer_im], axis=1)


def body(
    tracer, courant, nlon_counts, band_map, owner_map, legendre, modes_to, modes_from, mode_rates
):
    levels_dev = tracer.shape[0]
    lat_rows = tracer.shape[1]
    n_wide = lax.axis_size("wide")
    n_narrow = lax.axis_size("narrow")
    first_row = lax.axis_index("wide") * lat_rows
    stacked = jnp.stack([tracer, courant])
    padded = extended(stacked, (("wide", 2),), 4)
    open_faces = valid_rows(first_row, lat_rows, 4)
    section_one = advect_section(padded[0], padded[1], open_faces)
    section_two = advect_section(section_one, padded[1][:, 2:-2], open_faces[2:-2])
    advected = 0.5 * tracer + 0.5 * section_two
    wave_count = band_map.shape[0]
    fourier = longitude_transform(advected, wave_count)
    wave_ids = jnp.arange(wave_count, dtype=jnp.int32)
    kept_mask = (2 * wave_ids[:, None] < nlon_counts[None, :]).astype(jnp.float32)
    fourier = fourier * kept_mask[:, None, None, :]
    slot_count = wave_count // (n_wide * n_narrow)
    fourier = jnp.einsum(
        "sm,mclj->sclj", (band_map[:, None] == wave_ids[None, :]).astype(jnp.float32), fourier,
        precision=lax.Precision.HIGHEST,
    )
    fourier = lax.all_to_all(fourier, "wide", split_axis=0, concat_axis=3, tiled=True)
    fourier = lax.all_to_all(fourier, "narrow", split_axis=0, concat_axis=2, tiled=True)
    levels_all = levels_dev * n_narrow
    half_rows = fourier.shape[3] // 2
    north_half = fourier[:, :, :, :half_rows]
    south_half = jnp.flip(fourier[:, :, :, half_rows:], axis=3)
    sym_part = north_half + south_half
    anti_part = north_half - south_half
    slot_start = (lax.axis_index("wide") * n_narrow + lax.axis_index("narrow")) * slot_count
    slot_waves = lax.dynamic_slice_in_dim(band_map, slot_start, slot_count)
    same_parity = (jnp.arange(2, dtype=jnp.int32)[None, :] - slot_waves[:, None]) % 2 == 0
    chosen = jnp.where(same_parity[:, :, None, None, None], sym_part[:, None], anti_part[:, None])
    spectral = jnp.einsum("spkj,spclj->spkcl", legendre, chosen, precision=lax.Precision.HIGHEST)
    degree_ids = (
        2 * jnp.arange(wave_count // 2, dtype=jnp.int32)[None, :]
        + jnp.arange(2, dtype=jnp.int32)[:, None]
    )
    upper_mask = (degree_ids[None] >= slot_waves[:, None, None]).astype(jnp.float32)
    spectral = spectral * upper_mask[:, :, :, None, None]
    spectral = jnp.transpose(spectral, (0, 2, 1, 3, 4)).reshape(
        slot_count, wave_count, 2, levels_all
    )
    spectral = jnp.einsum(
        "tn,sncl->stcl", (owner_map[:, None] == wave_ids[None, :]).astype(jnp.float32), spectral,
        precision=lax.Precision.HIGHEST,
    )
    gathered = lax.all_to_all(spectral, "narrow", split_axis=1, concat_axis=0, tiled=True)
    owned = gathered.shape[1]
    owned_degrees = lax.dynamic_slice_in_dim(owner_map, lax.axis_index("narrow") * owned, owned)
    degree_sq = (owned_degrees * (owned_degrees + 1)).astype(jnp.float32)
    damping = 1.0 / (1.0 + degree_sq[None, :] * mode_rates[:, None])
    modal_part = jnp.einsum("kl,stcl->kstc", modes_to, gathered, precision=lax.Precision.HIGHEST)
    scaled = modal_part * damping[:, None, :, None]
    return jnp.einsum("ik,kstc->cist", modes_from, scaled, precision=lax.Precision.HIGHEST)


MESH = pl.DeviceIdType.MESH
LANE = 128
PAD = 8
RIM = 4
CHUNKS = 4
STRIP = 512
TALL = 17
HALO = {1: (3, 2), 0: (3, 1)}


def chunk_list(lon_count, count):
    tiles = -(-lon_count // LANE)
    cuts = [min(lon_count, LANE * (tiles * cut // count)) for cut in range(count + 1)]
    return [(lo, hi - lo) for lo, hi in zip(cuts, cuts[1:])]


def fourier_table(lon_count, wave_count):
    rows = -(-lon_count // LANE) * LANE
    turns = np.outer(np.arange(lon_count), np.arange(wave_count)) % lon_count
    angle = 2.0 * np.pi / lon_count * turns
    full = np.concatenate([np.cos(angle), -np.sin(angle)], axis=1) * (0.5 / np.sqrt(lon_count))
    high = full.astype(jnp.bfloat16)
    low = (full - high.astype(np.float64)).astype(jnp.bfloat16)
    table = np.zeros((rows, LANE), jnp.bfloat16)
    table[:lon_count] = np.concatenate([high, low], axis=1)
    return table


def split(value):
    high = value.astype(jnp.bfloat16)
    low = (value - high.astype(jnp.float32)).astype(jnp.bfloat16)
    return high, low


def face_flux(field, rate, ahead):
    rows = field.shape[0]
    above = pltpu.roll(field, rows - 1, 0)
    step = above - field
    near = jnp.where(ahead, pltpu.roll(step, 1, 0), pltpu.roll(step, rows - 1, 0))
    slope = step * (1.0 / 3.0) + near * (1.0 / 6.0)
    slope = jnp.maximum(jnp.minimum(slope, jnp.maximum(step, 0.0)), jnp.minimum(step, 0.0))
    return rate * jnp.where(ahead, field + slope, above - slope)


def section(field, rate, ahead):
    flux = face_flux(field, rate, ahead)
    return field - (flux - pltpu.roll(flux, 1, 0))


def rim_flux(field, step, rate, ahead, face):
    here = step[face]
    near = jnp.where(ahead[face], step[face - 1], step[face + 1])
    slope = here * (1.0 / 3.0) + near * (1.0 / 6.0)
    slope = jnp.maximum(jnp.minimum(slope, jnp.maximum(here, 0.0)), jnp.minimum(here, 0.0))
    return rate[face] * jnp.where(ahead[face], field[face] + slope, field[face + 1] - slope)


def rim_section(field_row, rate_row, top):
    field = {row: field_row(row) for row in range(-4, RIM + 4)}
    rate = {row: rate_row(row) for row in range(-3, RIM + 2)}
    ahead = {row: rate[row] >= 0.0 for row in rate}
    step = {row: field[row + 1] - field[row] for row in range(-4, RIM + 3)}
    flux = {row: rim_flux(field, step, rate, ahead, row) for row in range(-3, RIM + 2)}
    flux[-3] = jnp.where(top, field[-4], flux[-3])
    flux[RIM + 1] = jnp.where(top, flux[RIM + 1], field[RIM + 3])
    once = {row: field[row] - (flux[row] - flux[row - 1]) for row in range(-2, RIM + 2)}
    step = {row: once[row + 1] - once[row] for row in range(-2, RIM + 1)}
    flux = {row: rim_flux(once, step, rate, ahead, row) for row in range(-1, RIM)}
    return [field[row] + (once[row] - (flux[row] - flux[row - 1])) for row in range(RIM)]


def ids(shape, dim):
    return lax.broadcasted_iota(jnp.int32, shape, dim)


def fused_kernel(
    n_wide, n_narrow, lon_count,
    tracer, courant, nlon, band, owner, legendre, modes_to, modes_from, rates, table,
    out,
    q_buf, c_buf, t_buf, a_buf, e_buf, f_buf, q_tall, c_tall, rim, spec, leg, nlon_s, band_s, owner_s, to_s, from_s, rate_s,
    pick, keep, degree, sent, got, lx,
    small_sem, load_sem, table_sem, halo_send, halo_recv, leg_send, leg_recv, four_send, four_recv,
    entered,
):
    wide, narrow = lax.axis_index("wide"), lax.axis_index("narrow")
    total = n_wide * n_narrow
    me = wide * n_narrow + narrow
    levels, lat_rows = tracer.shape[0], tracer.shape[1]
    wave_count = band_s.shape[0]
    lon_pad = t_buf.shape[0]
    chunks = chunk_list(lon_count, CHUNKS)
    owned = wave_count // n_narrow
    half_waves = wave_count // 2
    row_total = levels * lat_rows

    barrier = pltpu.get_barrier_semaphore()

    bits = [2**k for k in range(n_wide.bit_length() - 1)]
    mates = 2 ** (len(bits) // 2)
    planes = n_wide // mates
    far_at, near_at = wide // mates, wide % mates
    near = [
        (far_at * mates + (near_at + a) % mates, (narrow + b) % n_narrow)
        for a in range(mates)
        for b in range(n_narrow)
        if a or b
    ]
    far = [(((far_at + a) % planes) * mates + near_at, narrow) for a in range(1, planes)]
    last_near, first_near = near_at == mates - 1, near_at == 0
    crosses = (last_near & (far_at < planes - 1)) | (first_near & (far_at > 0))

    @pl.when(crosses)
    def _():
        pl.semaphore_signal(
            barrier,
            inc=1,
            device_id=(jnp.where(last_near, wide + 1, wide - 1), narrow),
            device_id_type=MESH,
        )

    for other in near + far:
        pl.semaphore_signal(barrier, inc=1, device_id=other, device_id_type=MESH)

    smalls = []
    for at, (here, there) in enumerate(
        ((nlon, nlon_s), (band, band_s), (owner, owner_s), (modes_to, to_s), (modes_from, from_s), (rates, rate_s))
    ):
        smalls.append(pltpu.make_async_copy(here, there, small_sem.at[at]))
    for copy in smalls:
        copy.start()
    loads = []
    for at, (lo, size) in enumerate(chunks):
        pair = []
        for which, (here, there) in enumerate(((tracer, q_buf), (courant, c_buf))):
            copy = pltpu.make_async_copy(
                here.at[:, :, pl.ds(lo, size)],
                there.at[:, pl.ds(PAD, lat_rows), pl.ds(lo, size)],
                load_sem.at[at, which],
            )
            copy.start()
            pair.append(copy)
        loads.append(pair)
    table_copy = pltpu.make_async_copy(table, t_buf, table_sem)
    own_leg = pltpu.make_async_copy(legendre, leg.at[narrow], leg_recv.at[narrow])
    own_leg.start()

    @pl.when(wide == 0)
    def _():
        q_buf[:, 0:PAD, :] = jnp.zeros((levels, PAD, lon_count), jnp.float32)
        c_buf[:, 0:PAD, :] = jnp.zeros((levels, PAD, lon_count), jnp.float32)

    @pl.when(wide == n_wide - 1)
    def _():
        q_buf[:, PAD + lat_rows :, :] = jnp.zeros((levels, PAD, lon_count), jnp.float32)
        c_buf[:, PAD + lat_rows :, :] = jnp.zeros((levels, PAD, lon_count), jnp.float32)

    greeted = len(near) + len(far)

    @pl.when(crosses)
    def _():
        pl.semaphore_wait(barrier, greeted + 1)

    @pl.when(jnp.logical_not(crosses))
    def _():
        pl.semaphore_wait(barrier, greeted)

    for other in far:
        pl.semaphore_signal(entered, inc=1, device_id=other, device_id_type=MESH)

    def halo(up, which):
        here, there = ((tracer, q_buf), (courant, c_buf), (f_buf, q_buf))[which]
        if which == 2:
            count = 1
            first = PAD - RIM + 1 if up else 1
            land = PAD - RIM if up else PAD + lat_rows + RIM - 1
        else:
            count = HALO[up][which]
            first = lat_rows - count if up else 0
            land = PAD - count if up else PAD + lat_rows
        return pltpu.make_async_remote_copy(
            src_ref=here.at[:, pl.ds(first, count), :],
            dst_ref=there.at[:, pl.ds(land, count), :],
            send_sem=halo_send.at[up, which],
            recv_sem=halo_recv.at[up, which],
            device_id=(wide + 1 if up else wide - 1, narrow),
            device_id_type=MESH,
        )

    odd = wide % 2 == 1

    def halo_step(up, what, cond, parts=(0, 1, 2)):
        @pl.when(cond)
        def _():
            for which in parts:
                getattr(halo(up, which), what)()

    def send_halos(parts):
        halo_step(1, "start", odd & (wide < n_wide - 1), parts)
        halo_step(0, "start", jnp.logical_not(odd) & (wide > 0), parts)
        halo_step(0, "start", odd, parts)
        halo_step(1, "start", jnp.logical_not(odd), parts)

    send_halos((0, 1))

    leg_copy = pltpu.make_async_remote_copy(
        src_ref=legendre,
        dst_ref=leg.at[narrow],
        send_sem=leg_send,
        recv_sem=leg_recv.at[narrow],
        device_id=(wide, 1 - narrow),
        device_id_type=MESH,
    )
    leg_copy.start()

    for copy in smalls:
        copy.wait()
    row8, lane8 = ids((8, LANE), 0), ids((8, LANE), 1)
    for at in range(n_wide):
        wave = jnp.where(row8 < 2, band_s[2 * at], band_s[2 * at + 1])
        column = (row8 % 2) * wave_count + wave
        hit = (row8 < 4) & (lane8 % (2 * wave_count) == column)
        pick[8 * at : 8 * at + 8, :] = jnp.where(hit, 1.0, 0.0)
    for row in range(lat_rows):
        keep[row : row + 1, :] = jnp.full((1, LANE), nlon_s[row], jnp.int32)
    for row in range(owned):
        degree[row : row + 1, :] = jnp.full((1, LANE), owner_s[narrow * owned + row], jnp.int32)

    lane1 = ids((1, LANE), 1)
    number = jnp.zeros((1, LANE), jnp.int32)
    for at in range(owned):
        number = jnp.where(lane1 % owned == at, owner_s[narrow * owned + at], number)
    squared = (number * (number + 1)).astype(jnp.float32)
    levels_all = levels * n_narrow
    damping = [1.0 / (1.0 + squared * rate_s[k]) for k in range(levels_all)]
    mix = [
        [
            sum((from_s[i, k] * to_s[k, l]) * damping[k] for k in range(levels_all))
            for l in range(levels_all)
        ]
        for i in range(levels_all)
    ]

    weights = [
        [
            jnp.where(row8 < 4, mix[i][level], mix[i][levels + level])
            for level in range(levels)
        ]
        for i in range(levels_all)
    ]
    a_buf[:, lon_pad - LANE :] = jnp.zeros((2 * row_total, LANE), jnp.bfloat16)

    def outer_flux(step, carry, lanes=STRIP):
        place = pl.ds(pl.multiple_of(step * STRIP, STRIP), lanes)
        lower = ids((PAD, lanes), 0) < RIM
        for level in range(levels):
            field, rate = (
                jnp.where(
                    lower,
                    buf[level, PAD : 2 * PAD, place],
                    buf[level, lat_rows : PAD + lat_rows, place],
                )
                for buf in (q_buf, c_buf)
            )
            f_buf[level, :, place] = face_flux(field, rate, rate >= 0.0)
        return carry

    width = lon_pad // CHUNKS
    for at in range(CHUNKS):
        for pair in loads[0:1] if at == 0 else loads[1:] if at == 1 else ():
            pair[0].wait()
            pair[1].wait()
        if at == 0:
            table_copy.start()
        if at == 1:
            strips, extra = divmod(lon_count, STRIP)
            lax.fori_loop(0, strips, outer_flux, 0)
            if extra:
                outer_flux(strips, 0, extra)
            send_halos((2,))

        def tile(step, carry, lo=at * width, lanes=LANE):
            columns = pl.ds(pl.multiple_of(lo + step * LANE, LANE), lanes)
            for level in range(levels):
                field = q_buf[level, PAD : PAD + lat_rows, columns]
                rate = c_buf[level, PAD : PAD + lat_rows, columns]
                ahead = rate >= 0.0
                twice = section(section(field, rate, ahead), rate, ahead)
                high, low = split(field + twice)
                first = level * lat_rows
                a_buf[first : first + lat_rows, columns] = high
                a_buf[row_total + first : row_total + first + lat_rows, columns] = low
            return carry

        whole, rest = divmod(chunks[at][1], LANE)
        lax.fori_loop(0, whole, tile, 0, unroll=2 if whole % 2 == 0 else 1)
        if rest:
            tile(whole, 0, lanes=rest)
    table_copy.wait()
    spectrum = jnp.dot(a_buf[...], t_buf[...], preferred_element_type=jnp.float32)
    spectrum = spectrum[0:row_total] + spectrum[row_total:]
    kept = 2 * (ids((lat_rows, LANE), 1) % wave_count) < keep[...]
    spec[...] = jnp.where(jnp.concatenate([kept] * levels, axis=0), spectrum, 0.0)

    @pl.when(wide == n_wide - 1)
    def _():
        last = PAD + lat_rows - 1
        c_buf[:, last : last + 1, :] = jnp.zeros((levels, 1, lon_count), jnp.float32)

    last_dims = (((1,), (1,)), ((), ()))

    def edge(top, slab):
        start = pl.multiple_of(jnp.where(top, 0, lat_rows), 8)
        first = jnp.where(top, PAD, PAD - RIM)

        def strip(step, carry, tiles=(LANE,) * PAD):
            places = [
                pl.ds(pl.multiple_of(step * PAD * LANE + k * LANE, LANE), lanes)
                for k, lanes in enumerate(tiles)
            ]
            for level in range(levels):
                for k, place in enumerate(places):
                    here = pl.ds((level * PAD + k) * TALL, 2 * PAD)
                    q_tall[here, 0 : tiles[k]] = q_buf[level, pl.ds(start, 2 * PAD), place]
                    c_tall[here, 0 : tiles[k]] = c_buf[level, pl.ds(start, 2 * PAD), place]
            for level in range(levels):
                base = level * PAD * TALL + first
                values = rim_section(
                    lambda row: q_tall[pl.ds(base + row, PAD, stride=TALL), :],
                    lambda row: c_tall[pl.ds(base + row, PAD, stride=TALL), :],
                    top,
                )
                for row, value in enumerate(values):
                    rim[pl.ds(level * RIM + row, PAD, stride=PAD), :] = value
            for k in range(PAD):
                value = rim[k * PAD : k * PAD + PAD, :]
                high = value.astype(jnp.bfloat16).astype(jnp.float32)
                both = jnp.concatenate([high, value - high], axis=0)
                place = pl.ds(pl.multiple_of(step * PAD * LANE + k * LANE, LANE), LANE)
                e_buf[pl.ds(slab, 2 * PAD), place] = both.astype(jnp.bfloat16)
            return carry

        whole = lon_count // (PAD * LANE)
        lax.fori_loop(0, whole, strip, 0, unroll=True)
        rest = lon_count - whole * PAD * LANE
        if rest:
            strip(whole, 0, tuple(min(LANE, rest - k * LANE) for k in range(PAD)))
    def replace(top, rows):
        rows = rows[0:PAD] + rows[PAD:]
        swapped = pltpu.roll(rows, RIM, 0)
        at = pl.multiple_of(jnp.where(top, 0, lat_rows - PAD), 8)
        fresh = jnp.where(top, row8, PAD - 1 - row8) < RIM
        cover = 2 * (lane8 % wave_count) < keep[pl.ds(at, PAD), :]
        for level, mine in enumerate(
            (jnp.where(top, rows, swapped), jnp.where(top, swapped, rows))
        ):
            place = pl.ds(pl.multiple_of(level * lat_rows + at, 8), PAD)
            spec[place, :] = jnp.where(fresh, jnp.where(cover, mine, 0.0), spec[place, :])

    halo_step(1, "wait_recv", odd)
    halo_step(0, "wait_recv", jnp.logical_not(odd))
    edge(odd, 0)
    halo_step(0, "wait_recv", odd & (wide < n_wide - 1))
    halo_step(1, "wait_recv", jnp.logical_not(odd) & (wide > 0))
    edge(jnp.logical_not(odd), 2 * PAD)
    rows = jnp.dot(e_buf[...], t_buf[...], preferred_element_type=jnp.float32)
    replace(odd, rows[0 : 2 * PAD])
    replace(jnp.logical_not(odd), rows[2 * PAD :])

    high, low = split(spec[...])
    chooser = pick[...].astype(jnp.bfloat16)
    moved = lax.dot_general(chooser, high, last_dims, preferred_element_type=jnp.float32)
    moved = moved + lax.dot_general(chooser, low, last_dims, preferred_element_type=jnp.float32)
    for at in range(n_wide):
        sent[at] = moved[8 * at : 8 * at + 4, :]

    turns = [1 - 2 * ((wide // bit) % 2) for bit in bits]

    def fourier_copy(code):
        to_wide = wide
        for bit, turn in zip(bits, turns):
            if code // n_narrow & bit:
                to_wide = to_wide + bit * turn
        to_narrow = 1 - narrow if code % n_narrow else narrow
        return pltpu.make_async_remote_copy(
            src_ref=sent.at[to_wide],
            dst_ref=got.at[me],
            send_sem=four_send,
            recv_sem=four_recv.at[code // (n_narrow * mates)],
            device_id=(to_wide, to_narrow),
            device_id_type=MESH,
        )

    pl.semaphore_wait(entered, len(far))
    for code in range(total - 1, 0, -1):
        fourier_copy(code).start()
    got[me] = sent[wide]

    own_leg.wait()
    pltpu.make_async_remote_copy(
        src_ref=legendre,
        dst_ref=leg.at[1 - narrow],
        send_sem=leg_send,
        recv_sem=leg_recv.at[1 - narrow],
        device_id=(wide, 1 - narrow),
        device_id_type=MESH,
    ).wait_recv()

    degrees = degree[:, 0:wave_count]
    flat = ids((owned, wave_count), 1)
    held = 2 * (flat % half_waves) + flat // half_waves
    north, south = [], []
    for slot in range(n_narrow):
        wave = band_s[wide * n_narrow + slot]
        chosen = jnp.where((held == degrees) & (degrees >= wave), 1.0, 0.0)
        even = ((degrees + wave) % 2) == 0
        north.append(chosen.astype(jnp.bfloat16))
        south.append(jnp.where(even, chosen, -chosen).astype(jnp.bfloat16))
    leg_parts = [split(leg[slot]) for slot in range(n_narrow)]
    block = n_narrow * owned

    def rows_of(picks):
        return jnp.concatenate(
            [
                jnp.dot(picks[slot], leg_parts[slot][half], preferred_element_type=jnp.float32)
                for half in range(2)
                for slot in range(n_narrow)
            ],
            axis=0,
        )

    source, lane = ids((LANE, LANE), 0), ids((LANE, LANE), 1)
    lane_rows = ids((block, LANE), 1)
    tiles = leg.shape[2] // LANE
    for southern, picks in ((False, north), (True, south)):
        rows = rows_of(picks).astype(jnp.bfloat16)
        tall = jnp.concatenate([rows[:, LANE * a : LANE * a + LANE] for a in range(tiles)], axis=0)
        for half in range(2):
            within = lane % lat_rows
            if southern:
                within = lat_rows - 1 - within
            spread = jnp.where(source == half * lat_rows + within, 1.0, 0.0).astype(jnp.bfloat16)
            wide_rows = jnp.dot(tall, spread, preferred_element_type=jnp.float32)
            for a in range(tiles):
                lat_block = 2 * a + half
                if southern:
                    lat_block = n_wide - 1 - lat_block
                for part in range(2):
                    piece = wide_rows[(a * 2 + part) * block : (a * 2 + part + 1) * block]
                    for level in range(levels):
                        kept_piece = jnp.where(lane_rows // lat_rows == level, piece, 0.0)
                        first = (part * levels + level) * block
                        lx[first : first + block, LANE * lat_block : LANE * lat_block + LANE] = (
                            kept_piece.astype(jnp.bfloat16)
                        )

    product = jnp.zeros((16, LANE), jnp.float32)
    plane = mates * n_narrow
    for code in range(planes):
        arrived = got.at[pl.ds(0, plane - 1 if code == 0 else plane)]
        pltpu.make_async_copy(arrived, arrived, four_recv.at[code]).wait()
        from_far = far_at
        for bit in bits:
            if code * mates & bit:
                from_far = from_far + bit // mates * (1 - 2 * ((wide // bit) % 2))
        strip = []
        for at in range(mates):
            values = jnp.concatenate(
                [got[from_far * plane + n_narrow * at + j] for j in range(n_narrow)], axis=0
            )
            top_half, rest = split(values)
            strip.append(jnp.concatenate([top_half, rest], axis=0))
        columns = pl.ds(pl.multiple_of(from_far * (mates * LANE), mates * LANE), mates * LANE)
        product = product + lax.dot_general(
            jnp.concatenate(strip, axis=1), lx[:, columns], last_dims, preferred_element_type=jnp.float32
        )
    product = product[0:8] + product[8:16]
    product = product + pltpu.roll(product, LANE // 2, 1)
    by_level = []
    for level in range(levels):
        moved = product if level == 0 else pltpu.roll(product, LANE - level * block, 1)
        by_level.append(jnp.where(lane8 < owned, moved, pltpu.roll(moved, 6, 0)))
    for i in range(levels_all):
        result = sum(weights[i][level] * by_level[level] for level in range(levels))
        result = result + pltpu.roll(result, 4, 0)
        second = pltpu.roll(result, LANE - owned, 1)
        for c in range(2):
            out[c, i, 0:1, :] = result[c : c + 1, 0:owned]
            out[c, i, 1:2, :] = second[c : c + 1, 0:owned]
    others = got.at[pl.ds(0, total - 1)]
    pltpu.make_async_copy(others, others, four_send).wait()
    leg_copy.wait_send()
    halo_step(1, "wait_send", wide < n_wide - 1)
    halo_step(0, "wait_send", wide > 0)


def fused_fits(tracer, band_map, legendre, n_wide, n_narrow):
    levels, lat_rows = tracer.shape[0], tracer.shape[1]
    waves = band_map.shape[0]
    return (
        levels == 2
        and n_narrow == 2
        and lat_rows * levels == LANE
        and waves == n_wide * n_narrow
        and n_wide & (n_wide - 1) == 0
        and -(-tracer.shape[2] // LANE) % CHUNKS == 0
        and -(-tracer.shape[2] // LANE) % PAD == 0
        and tracer.shape[2] > PAD * LANE
        and 4 * waves == LANE
        and legendre.shape[3] * 2 == n_wide * lat_rows
        and 2 * n_wide * 4 == LANE
    )


def fused(
    tracer, courant, nlon_counts, band_map, owner_map, legendre, modes_to, modes_from, mode_rates
):
    n_wide = lax.axis_size("wide")
    n_narrow = lax.axis_size("narrow")
    levels, lat_rows, lon_count = tracer.shape
    waves = band_map.shape[0]
    total = n_wide * n_narrow
    table = fourier_table(lon_count, waves)
    lon_pad = table.shape[0]
    tall = lat_rows + 2 * PAD
    half = legendre.shape[3]
    levels_all = levels * n_narrow
    vmem, smem, dma = pltpu.VMEM, pltpu.SMEM, pltpu.SemaphoreType.DMA
    operands = (
        tracer, courant, nlon_counts, band_map, owner_map,
        legendre.reshape(waves, half), modes_to, modes_from, mode_rates, jnp.asarray(table),
    )
    return pl.pallas_call(
        functools.partial(fused_kernel, n_wide, n_narrow, lon_count),
        out_shape=vmem((2, levels_all, 2, waves // n_narrow), jnp.float32),
        in_specs=[pl.BlockSpec(memory_space=pltpu.HBM)] * 10,
        out_specs=pl.BlockSpec(memory_space=pltpu.VMEM),
        scratch_shapes=[
            vmem((levels, tall, lon_count), jnp.float32),
            vmem((levels, tall, lon_count), jnp.float32),
            vmem((lon_pad, LANE), jnp.bfloat16),
            vmem((2 * levels * lat_rows, lon_pad), jnp.bfloat16),
            vmem((4 * PAD, lon_pad), jnp.bfloat16),
            vmem((levels, PAD, lon_count), jnp.float32),
            vmem(((levels + 1) * PAD * TALL, LANE), jnp.float32),
            vmem(((levels + 1) * PAD * TALL, LANE), jnp.float32),
            vmem((PAD * PAD + PAD, LANE), jnp.float32),
            vmem((levels * lat_rows, LANE), jnp.float32),
            vmem((n_narrow, waves, half), jnp.float32),
            smem((lat_rows,), jnp.int32),
            smem((waves,), jnp.int32),
            smem((waves,), jnp.int32),
            smem((levels_all, levels_all), jnp.float32),
            smem((levels_all, levels_all), jnp.float32),
            smem((levels_all,), jnp.float32),
            vmem((8 * n_wide, LANE), jnp.float32),
            vmem((lat_rows, LANE), jnp.int32),
            vmem((waves // n_narrow, LANE), jnp.int32),
            vmem((n_wide, 4, LANE), jnp.float32),
            vmem((total, 4, LANE), jnp.float32),
            vmem((LANE, n_wide * LANE), jnp.bfloat16),
            dma((6,)),
            dma((CHUNKS, 2)),
            dma,
            dma((2, 3)),
            dma((2, 3)),
            dma,
            dma((n_narrow,)),
            dma,
            dma((n_wide,)),
            pltpu.SemaphoreType.REGULAR,
        ],
        compiler_params=pltpu.CompilerParams(
            collective_id=0, has_side_effects=True
        ),
    )(*(pltpu.with_memory_space_constraint(operand, pltpu.HBM) for operand in operands))


def program(tracer, courant, nlon_counts, band_map, owner_map, legendre, *modes):
    choose = (
        fused
        if fused_fits(
            tracer, band_map, legendre, lax.axis_size("wide"), lax.axis_size("narrow")
        )
        else body
    )
    return choose(tracer, courant, nlon_counts, band_map, owner_map, legendre, *modes)


def solution(mesh):
    placed = (
        P("narrow", "wide", None),
        P("narrow", "wide", None),
        P("wide"),
        P(),
        P(),
        P(("wide", "narrow"), None, None, None),
        P(),
        P(),
        P(),
    )
    return jax.shard_map(
        program, mesh=mesh, in_specs=placed, out_specs=P(None, None, "wide", "narrow"), check_vma=False
    )
```

```python
import functools
import math

import jax
import jax.numpy as jnp
import numpy as np
from jax import lax
from jax.experimental import pallas as pl
from jax.experimental.pallas import tpu as pltpu
from jax.sharding import PartitionSpec as P

NLAT = 1024


def extended(array, sides, width):
    for axis, dim in sides:
        devices, length = (lax.axis_size(axis), array.shape[dim])
        up = [(i, (i + 1) % devices) for i in range(devices - 1)]
        down = [(j, i) for i, j in up]
        last = lax.slice_in_dim(array, length - width, length, axis=dim)
        initial = lax.slice_in_dim(array, 0, width, axis=dim)
        before = lax.ppermute(last, axis, up)
        after = lax.ppermute(initial, axis, down)
        array = jnp.concatenate([before, array, after], axis=dim)
    return array


def advect_section(field_ext, rate_ext, open_faces):
    row_total = field_ext.shape[1]
    row_below = field_ext[:, 0 : row_total - 3]
    row_here = field_ext[:, 1 : row_total - 2]
    row_above = field_ext[:, 2 : row_total - 1]
    row_beyond = field_ext[:, 3:row_total]
    face_rate = rate_ext[:, 1 : row_total - 2] * open_faces[1 : row_total - 2][:, None]
    upwind = (5.0 * row_here + 2.0 * row_above - row_below) / 6.0
    downwind = (5.0 * row_above + 2.0 * row_here - row_beyond) / 6.0
    low_bound = jnp.minimum(row_here, row_above)
    high_bound = jnp.maximum(row_here, row_above)
    face_value = jnp.clip(jnp.where(face_rate >= 0.0, upwind, downwind), low_bound, high_bound)
    face_flux = face_rate * face_value
    return field_ext[:, 2 : row_total - 2] - (face_flux[:, 1:] - face_flux[:, :-1])


def valid_rows(first_row, lat_rows, rim_width):
    row_ids = first_row + jnp.arange(lat_rows + 2 * rim_width, dtype=jnp.int32) - rim_width
    return ((row_ids >= 0) & (row_ids < NLAT - 1)).astype(jnp.float32)


def longitude_transform(advected, wave_count):
    levels_dev, lat_rows, lon_count = advected.shape
    short_len = 32
    long_len = lon_count // short_len
    block_count = wave_count // short_len
    row_count = levels_dev * lat_rows
    grid_rows = advected.reshape(row_count, short_len, long_len)
    short_ids = jnp.arange(short_len, dtype=jnp.int32)
    turn_one = short_ids[:, None] * short_ids[None, :] % short_len
    angle_one = 2.0 * math.pi / short_len * turn_one.astype(jnp.float32)
    highest = lax.Precision.HIGHEST
    inner_re = jnp.einsum("pab,ar->prb", grid_rows, jnp.cos(angle_one), precision=highest)
    inner_im = -jnp.einsum("pab,ar->prb", grid_rows, jnp.sin(angle_one), precision=highest)
    long_ids = jnp.arange(long_len, dtype=jnp.int32)
    block_ids = jnp.arange(block_count, dtype=jnp.int32)
    wave_ids = short_len * block_ids[None, None, :] + short_ids[:, None, None]
    turn_two = wave_ids * long_ids[None, :, None] % lon_count
    angle_two = 2.0 * math.pi / lon_count * turn_two.astype(jnp.float32)
    cos_two = jnp.cos(angle_two)
    sin_two = jnp.sin(angle_two)
    outer_re = jnp.einsum("prb,rbc->crp", inner_re, cos_two, precision=highest) + jnp.einsum(
        "prb,rbc->crp", inner_im, sin_two, precision=highest
    )
    outer_im = jnp.einsum("prb,rbc->crp", inner_im, cos_two, precision=highest) - jnp.einsum(
        "prb,rbc->crp", inner_re, sin_two, precision=highest
    )
    outer_re = (outer_re / math.sqrt(lon_count)).reshape(wave_count, levels_dev, lat_rows)
    outer_im = (outer_im / math.sqrt(lon_count)).reshape(wave_count, levels_dev, lat_rows)
    return jnp.stack([outer_re, outer_im], axis=1)


def body(
    tracer, courant, nlon_counts, band_map, owner_map, legendre, modes_to, modes_from, mode_rates
):
    levels_dev = tracer.shape[0]
    lat_rows = tracer.shape[1]
    n_wide = lax.axis_size("wide")
    n_narrow = lax.axis_size("narrow")
    first_row = lax.axis_index("wide") * lat_rows
    stacked = jnp.stack([tracer, courant])
    padded = extended(stacked, (("wide", 2),), 4)
    open_faces = valid_rows(first_row, lat_rows, 4)
    section_one = advect_section(padded[0], padded[1], open_faces)
    section_two = advect_section(section_one, padded[1][:, 2:-2], open_faces[2:-2])
    advected = 0.5 * tracer + 0.5 * section_two
    wave_count = band_map.shape[0]
    fourier = longitude_transform(advected, wave_count)
    wave_ids = jnp.arange(wave_count, dtype=jnp.int32)
    kept_mask = (2 * wave_ids[:, None] < nlon_counts[None, :]).astype(jnp.float32)
    fourier = fourier * kept_mask[:, None, None, :]
    slot_count = wave_count // (n_wide * n_narrow)
    fourier = jnp.einsum(
        "sm,mclj->sclj", (band_map[:, None] == wave_ids[None, :]).astype(jnp.float32), fourier,
        precision=lax.Precision.HIGHEST,
    )
    fourier = lax.all_to_all(fourier, "wide", split_axis=0, concat_axis=3, tiled=True)
    fourier = lax.all_to_all(fourier, "narrow", split_axis=0, concat_axis=2, tiled=True)
    levels_all = levels_dev * n_narrow
    half_rows = fourier.shape[3] // 2
    north_half = fourier[:, :, :, :half_rows]
    south_half = jnp.flip(fourier[:, :, :, half_rows:], axis=3)
    sym_part = north_half + south_half
    anti_part = north_half - south_half
    slot_start = (lax.axis_index("wide") * n_narrow + lax.axis_index("narrow")) * slot_count
    slot_waves = lax.dynamic_slice_in_dim(band_map, slot_start, slot_count)
    same_parity = (jnp.arange(2, dtype=jnp.int32)[None, :] - slot_waves[:, None]) % 2 == 0
    chosen = jnp.where(same_parity[:, :, None, None, None], sym_part[:, None], anti_part[:, None])
    spectral = jnp.einsum("spkj,spclj->spkcl", legendre, chosen, precision=lax.Precision.HIGHEST)
    degree_ids = (
        2 * jnp.arange(wave_count // 2, dtype=jnp.int32)[None, :]
        + jnp.arange(2, dtype=jnp.int32)[:, None]
    )
    upper_mask = (degree_ids[None] >= slot_waves[:, None, None]).astype(jnp.float32)
    spectral = spectral * upper_mask[:, :, :, None, None]
    spectral = jnp.transpose(spectral, (0, 2, 1, 3, 4)).reshape(
        slot_count, wave_count, 2, levels_all
    )
    spectral = jnp.einsum(
        "tn,sncl->stcl", (owner_map[:, None] == wave_ids[None, :]).astype(jnp.float32), spectral,
        precision=lax.Precision.HIGHEST,
    )
    gathered = lax.all_to_all(spectral, "narrow", split_axis=1, concat_axis=0, tiled=True)
    owned = gathered.shape[1]
    owned_degrees = lax.dynamic_slice_in_dim(owner_map, lax.axis_index("narrow") * owned, owned)
    degree_sq = (owned_degrees * (owned_degrees + 1)).astype(jnp.float32)
    damping = 1.0 / (1.0 + degree_sq[None, :] * mode_rates[:, None])
    modal_part = jnp.einsum("kl,stcl->kstc", modes_to, gathered, precision=lax.Precision.HIGHEST)
    scaled = modal_part * damping[:, None, :, None]
    return jnp.einsum("ik,kstc->cist", modes_from, scaled, precision=lax.Precision.HIGHEST)


MESH = pl.DeviceIdType.MESH
LANE = 128
PAD = 8
RIM = 4
CHUNKS = 4
STRIP = 512
TALL = 17
HALO = {1: (3, 2), 0: (3, 1)}


def chunk_list(lon_count, count):
    tiles = -(-lon_count // LANE)
    cuts = [min(lon_count, LANE * (tiles * cut // count)) for cut in range(count + 1)]
    return [(lo, hi - lo) for lo, hi in zip(cuts, cuts[1:])]


def fourier_table(lon_count, wave_count):
    rows = -(-lon_count // LANE) * LANE
    turns = np.outer(np.arange(lon_count), np.arange(wave_count)) % lon_count
    angle = 2.0 * np.pi / lon_count * turns
    full = np.concatenate([np.cos(angle), -np.sin(angle)], axis=1) * (0.5 / np.sqrt(lon_count))
    high = full.astype(jnp.bfloat16)
    low = (full - high.astype(np.float64)).astype(jnp.bfloat16)
    table = np.zeros((rows, LANE), jnp.bfloat16)
    table[:lon_count] = np.concatenate([high, low], axis=1)
    return table


def split(value):
    high = value.astype(jnp.bfloat16)
    low = (value - high.astype(jnp.float32)).astype(jnp.bfloat16)
    return high, low


def face_flux(field, rate, ahead):
    rows = field.shape[0]
    above = pltpu.roll(field, rows - 1, 0)
    step = above - field
    near = jnp.where(ahead, pltpu.roll(step, 1, 0), pltpu.roll(step, rows - 1, 0))
    slope = step * (1.0 / 3.0) + near * (1.0 / 6.0)
    slope = jnp.maximum(jnp.minimum(slope, jnp.maximum(step, 0.0)), jnp.minimum(step, 0.0))
    return rate * jnp.where(ahead, field + slope, above - slope)


def section(field, rate, ahead):
    flux = face_flux(field, rate, ahead)
    return field - (flux - pltpu.roll(flux, 1, 0))


def rim_flux(field, step, rate, ahead, face):
    here = step[face]
    near = jnp.where(ahead[face], step[face - 1], step[face + 1])
    slope = here * (1.0 / 3.0) + near * (1.0 / 6.0)
    slope = jnp.maximum(jnp.minimum(slope, jnp.maximum(here, 0.0)), jnp.minimum(here, 0.0))
    return rate[face] * jnp.where(ahead[face], field[face] + slope, field[face + 1] - slope)


def rim_section(field_row, rate_row, top):
    field = {row: field_row(row) for row in range(-4, RIM + 4)}
    rate = {row: rate_row(row) for row in range(-3, RIM + 2)}
    ahead = {row: rate[row] >= 0.0 for row in rate}
    step = {row: field[row + 1] - field[row] for row in range(-4, RIM + 3)}
    flux = {row: rim_flux(field, step, rate, ahead, row) for row in range(-3, RIM + 2)}
    flux[-3] = jnp.where(top, field[-4], flux[-3])
    flux[RIM + 1] = jnp.where(top, flux[RIM + 1], field[RIM + 3])
    once = {row: field[row] - (flux[row] - flux[row - 1]) for row in range(-2, RIM + 2)}
    step = {row: once[row + 1] - once[row] for row in range(-2, RIM + 1)}
    flux = {row: rim_flux(once, step, rate, ahead, row) for row in range(-1, RIM)}
    return [field[row] + (once[row] - (flux[row] - flux[row - 1])) for row in range(RIM)]


def ids(shape, dim):
    return lax.broadcasted_iota(jnp.int32, shape, dim)


def fused_kernel(
    n_wide, n_narrow, lon_count,
    tracer, courant, nlon, band, owner, legendre, modes_to, modes_from, rates, table,
    out,
    q_buf, c_buf, t_buf, a_buf, e_buf, f_buf, q_tall, c_tall, rim, spec, leg, nlon_s, band_s, owner_s, to_s, from_s, rate_s,
    pick, keep, degree, sent, got, lx,
    small_sem, load_sem, table_sem, halo_send, halo_recv, leg_send, leg_recv, four_send, four_recv,
    entered,
):
    wide, narrow = lax.axis_index("wide"), lax.axis_index("narrow")
    total = n_wide * n_narrow
    me = wide * n_narrow + narrow
    levels, lat_rows = tracer.shape[0], tracer.shape[1]
    wave_count = band_s.shape[0]
    lon_pad = t_buf.shape[0]
    chunks = chunk_list(lon_count, CHUNKS)
    owned = wave_count // n_narrow
    half_waves = wave_count // 2
    row_total = levels * lat_rows

    barrier = pltpu.get_barrier_semaphore()

    bits = [2**k for k in range(n_wide.bit_length() - 1)]
    mates = 2 ** (len(bits) // 2)
    planes = n_wide // mates
    far_at, near_at = wide // mates, wide % mates
    near = [
        (far_at * mates + (near_at + a) % mates, (narrow + b) % n_narrow)
        for a in range(mates)
        for b in range(n_narrow)
        if a or b
    ]
    far = [(((far_at + a) % planes) * mates + near_at, narrow) for a in range(1, planes)]
    last_near, first_near = near_at == mates - 1, near_at == 0
    crosses = (last_near & (far_at < planes - 1)) | (first_near & (far_at > 0))

    @pl.when(crosses)
    def _():
        pl.semaphore_signal(
            barrier,
            inc=1,
            device_id=(jnp.where(last_near, wide + 1, wide - 1), narrow),
            device_id_type=MESH,
        )

    for other in near + far:
        pl.semaphore_signal(barrier, inc=1, device_id=other, device_id_type=MESH)

    smalls = []
    for at, (here, there) in enumerate(
        ((nlon, nlon_s), (band, band_s), (owner, owner_s), (modes_to, to_s), (modes_from, from_s), (rates, rate_s))
    ):
        smalls.append(pltpu.make_async_copy(here, there, small_sem.at[at]))
    for copy in smalls:
        copy.start()
    loads = []
    for at, (lo, size) in enumerate(chunks):
        pair = []
        for which, (here, there) in enumerate(((tracer, q_buf), (courant, c_buf))):
            copy = pltpu.make_async_copy(
                here.at[:, :, pl.ds(lo, size)],
                there.at[:, pl.ds(PAD, lat_rows), pl.ds(lo, size)],
                load_sem.at[at, which],
            )
            copy.start()
            pair.append(copy)
        loads.append(pair)
    table_copy = pltpu.make_async_copy(table, t_buf, table_sem)
    own_leg = pltpu.make_async_copy(legendre, leg.at[narrow], leg_recv.at[narrow])
    own_leg.start()

    @pl.when(wide == 0)
    def _():
        q_buf[:, 0:PAD, :] = jnp.zeros((levels, PAD, lon_count), jnp.float32)
        c_buf[:, 0:PAD, :] = jnp.zeros((levels, PAD, lon_count), jnp.float32)

    @pl.when(wide == n_wide - 1)
    def _():
        q_buf[:, PAD + lat_rows :, :] = jnp.zeros((levels, PAD, lon_count), jnp.float32)
        c_buf[:, PAD + lat_rows :, :] = jnp.zeros((levels, PAD, lon_count), jnp.float32)

    greeted = len(near) + len(far)

    @pl.when(crosses)
    def _():
        pl.semaphore_wait(barrier, greeted + 1)

    @pl.when(jnp.logical_not(crosses))
    def _():
        pl.semaphore_wait(barrier, greeted)

    for other in far:
        pl.semaphore_signal(entered, inc=1, device_id=other, device_id_type=MESH)

    def halo(up, which):
        here, there = ((tracer, q_buf), (courant, c_buf), (f_buf, q_buf))[which]
        if which == 2:
            count = 1
            first = PAD - RIM + 1 if up else 1
            land = PAD - RIM if up else PAD + lat_rows + RIM - 1
        else:
            count = HALO[up][which]
            first = lat_rows - count if up else 0
            land = PAD - count if up else PAD + lat_rows
        return pltpu.make_async_remote_copy(
            src_ref=here.at[:, pl.ds(first, count), :],
            dst_ref=there.at[:, pl.ds(land, count), :],
            send_sem=halo_send.at[up, which],
            recv_sem=halo_recv.at[up, which],
            device_id=(wide + 1 if up else wide - 1, narrow),
            device_id_type=MESH,
        )

    odd = wide % 2 == 1

    def halo_step(up, what, cond, parts=(0, 1, 2)):
        @pl.when(cond)
        def _():
            for which in parts:
                getattr(halo(up, which), what)()

    def send_halos(parts):
        halo_step(1, "start", odd & (wide < n_wide - 1), parts)
        halo_step(0, "start", jnp.logical_not(odd) & (wide > 0), parts)
        halo_step(0, "start", odd, parts)
        halo_step(1, "start", jnp.logical_not(odd), parts)

    send_halos((0, 1))

    leg_copy = pltpu.make_async_remote_copy(
        src_ref=legendre,
        dst_ref=leg.at[narrow],
        send_sem=leg_send,
        recv_sem=leg_recv.at[narrow],
        device_id=(wide, 1 - narrow),
        device_id_type=MESH,
    )
    leg_copy.start()

    for copy in smalls:
        copy.wait()
    row8, lane8 = ids((8, LANE), 0), ids((8, LANE), 1)
    for at in range(n_wide):
        wave = jnp.where(row8 < 2, band_s[2 * at], band_s[2 * at + 1])
        column = (row8 % 2) * wave_count + wave
        hit = (row8 < 4) & (lane8 % (2 * wave_count) == column)
        pick[8 * at : 8 * at + 8, :] = jnp.where(hit, 1.0, 0.0)
    for row in range(lat_rows):
        keep[row : row + 1, :] = jnp.full((1, LANE), nlon_s[row], jnp.int32)
    for row in range(owned):
        degree[row : row + 1, :] = jnp.full((1, LANE), owner_s[narrow * owned + row], jnp.int32)

    lane1 = ids((1, LANE), 1)
    number = jnp.zeros((1, LANE), jnp.int32)
    for at in range(owned):
        number = jnp.where(lane1 % owned == at, owner_s[narrow * owned + at], number)
    squared = (number * (number + 1)).astype(jnp.float32)
    levels_all = levels * n_narrow
    damping = [1.0 / (1.0 + squared * rate_s[k]) for k in range(levels_all)]
    mix = [
        [
            sum((from_s[i, k] * to_s[k, l]) * damping[k] for k in range(levels_all))
            for l in range(levels_all)
        ]
        for i in range(levels_all)
    ]

    weights = [
        [
            jnp.where(row8 < 4, mix[i][level], mix[i][levels + level])
            for level in range(levels)
        ]
        for i in range(levels_all)
    ]
    a_buf[:, lon_pad - LANE :] = jnp.zeros((2 * row_total, LANE), jnp.bfloat16)

    def outer_flux(step, carry, lanes=STRIP):
        place = pl.ds(pl.multiple_of(step * STRIP, STRIP), lanes)
        lower = ids((PAD, lanes), 0) < RIM
        for level in range(levels):
            field, rate = (
                jnp.where(
                    lower,
                    buf[level, PAD : 2 * PAD, place],
                    buf[level, lat_rows : PAD + lat_rows, place],
                )
                for buf in (q_buf, c_buf)
            )
            f_buf[level, :, place] = face_flux(field, rate, rate >= 0.0)
        return carry

    width = lon_pad // CHUNKS
    for at in range(CHUNKS):
        for pair in loads[0:1] if at == 0 else loads[1:] if at == 1 else ():
            pair[0].wait()
            pair[1].wait()
        if at == 0:
            table_copy.start()
        if at == 1:
            strips, extra = divmod(lon_count, STRIP)
            lax.fori_loop(0, strips, outer_flux, 0)
            if extra:
                outer_flux(strips, 0, extra)
            send_halos((2,))

        def tile(step, carry, lo=at * width, lanes=LANE):
            columns = pl.ds(pl.multiple_of(lo + step * LANE, LANE), lanes)
            for level in range(levels):
                field = q_buf[level, PAD : PAD + lat_rows, columns]
                rate = c_buf[level, PAD : PAD + lat_rows, columns]
                ahead = rate >= 0.0
                twice = section(section(field, rate, ahead), rate, ahead)
                high, low = split(field + twice)
                first = level * lat_rows
                a_buf[first : first + lat_rows, columns] = high
                a_buf[row_total + first : row_total + first + lat_rows, columns] = low
            return carry

        whole, rest = divmod(chunks[at][1], LANE)
        lax.fori_loop(0, whole, tile, 0, unroll=2 if whole % 2 == 0 else 1)
        if rest:
            tile(whole, 0, lanes=rest)
    table_copy.wait()
    spectrum = jnp.dot(a_buf[...], t_buf[...], preferred_element_type=jnp.float32)
    spectrum = spectrum[0:row_total] + spectrum[row_total:]
    kept = 2 * (ids((lat_rows, LANE), 1) % wave_count) < keep[...]
    spec[...] = jnp.where(jnp.concatenate([kept] * levels, axis=0), spectrum, 0.0)

    @pl.when(wide == n_wide - 1)
    def _():
        last = PAD + lat_rows - 1
        c_buf[:, last : last + 1, :] = jnp.zeros((levels, 1, lon_count), jnp.float32)

    last_dims = (((1,), (1,)), ((), ()))

    def edge(top, slab):
        start = pl.multiple_of(jnp.where(top, 0, lat_rows), 8)
        first = jnp.where(top, PAD, PAD - RIM)

        def strip(step, carry, tiles=(LANE,) * PAD):
            places = [
                pl.ds(pl.multiple_of(step * PAD * LANE + k * LANE, LANE), lanes)
                for k, lanes in enumerate(tiles)
            ]
            for level in range(levels):
                for k, place in enumerate(places):
                    here = pl.ds((level * PAD + k) * TALL, 2 * PAD)
                    q_tall[here, 0 : tiles[k]] = q_buf[level, pl.ds(start, 2 * PAD), place]
                    c_tall[here, 0 : tiles[k]] = c_buf[level, pl.ds(start, 2 * PAD), place]
            for level in range(levels):
                base = level * PAD * TALL + first
                values = rim_section(
                    lambda row: q_tall[pl.ds(base + row, PAD, stride=TALL), :],
                    lambda row: c_tall[pl.ds(base + row, PAD, stride=TALL), :],
                    top,
                )
                for row, value in enumerate(values):
                    rim[pl.ds(level * RIM + row, PAD, stride=PAD), :] = value
            for k in range(PAD):
                value = rim[k * PAD : k * PAD + PAD, :]
                high = value.astype(jnp.bfloat16).astype(jnp.float32)
                both = jnp.concatenate([high, value - high], axis=0)
                place = pl.ds(pl.multiple_of(step * PAD * LANE + k * LANE, LANE), LANE)
                e_buf[pl.ds(slab, 2 * PAD), place] = both.astype(jnp.bfloat16)
            return carry

        whole = lon_count // (PAD * LANE)
        lax.fori_loop(0, whole, strip, 0, unroll=True)
        rest = lon_count - whole * PAD * LANE
        if rest:
            strip(whole, 0, tuple(min(LANE, rest - k * LANE) for k in range(PAD)))
    def replace(top, rows):
        rows = rows[0:PAD] + rows[PAD:]
        swapped = pltpu.roll(rows, RIM, 0)
        at = pl.multiple_of(jnp.where(top, 0, lat_rows - PAD), 8)
        fresh = jnp.where(top, row8, PAD - 1 - row8) < RIM
        cover = 2 * (lane8 % wave_count) < keep[pl.ds(at, PAD), :]
        for level, mine in enumerate(
            (jnp.where(top, rows, swapped), jnp.where(top, swapped, rows))
        ):
            place = pl.ds(pl.multiple_of(level * lat_rows + at, 8), PAD)
            spec[place, :] = jnp.where(fresh, jnp.where(cover, mine, 0.0), spec[place, :])

    halo_step(1, "wait_recv", odd)
    halo_step(0, "wait_recv", jnp.logical_not(odd))
    edge(odd, 0)
    halo_step(0, "wait_recv", odd & (wide < n_wide - 1))
    halo_step(1, "wait_recv", jnp.logical_not(odd) & (wide > 0))
    edge(jnp.logical_not(odd), 2 * PAD)
    rows = jnp.dot(e_buf[...], t_buf[...], preferred_element_type=jnp.float32)
    replace(odd, rows[0 : 2 * PAD])
    replace(jnp.logical_not(odd), rows[2 * PAD :])

    high, low = split(spec[...])
    chooser = pick[...].astype(jnp.bfloat16)
    moved = lax.dot_general(
        jnp.concatenate([chooser, chooser], axis=1),
        jnp.concatenate([high, low], axis=1),
        last_dims,
        preferred_element_type=jnp.float32,
    )
    for at in range(n_wide):
        sent[at] = moved[8 * at : 8 * at + 4, :]

    turns = [1 - 2 * ((wide // bit) % 2) for bit in bits]

    def fourier_copy(code):
        to_wide = wide
        for bit, turn in zip(bits, turns):
            if code // n_narrow & bit:
                to_wide = to_wide + bit * turn
        to_narrow = 1 - narrow if code % n_narrow else narrow
        return pltpu.make_async_remote_copy(
            src_ref=sent.at[to_wide],
            dst_ref=got.at[me],
            send_sem=four_send,
            recv_sem=four_recv.at[code // (n_narrow * mates)],
            device_id=(to_wide, to_narrow),
            device_id_type=MESH,
        )

    pl.semaphore_wait(entered, len(far))
    for code in range(total - 1, 0, -1):
        fourier_copy(code).start()
    got[me] = sent[wide]

    own_leg.wait()
    pltpu.make_async_remote_copy(
        src_ref=legendre,
        dst_ref=leg.at[1 - narrow],
        send_sem=leg_send,
        recv_sem=leg_recv.at[1 - narrow],
        device_id=(wide, 1 - narrow),
        device_id_type=MESH,
    ).wait_recv()

    degrees = degree[:, 0:wave_count]
    flat = ids((owned, wave_count), 1)
    held = 2 * (flat % half_waves) + flat // half_waves
    north, south = [], []
    for slot in range(n_narrow):
        wave = band_s[wide * n_narrow + slot]
        chosen = jnp.where((held == degrees) & (degrees >= wave), 1.0, 0.0)
        even = ((degrees + wave) % 2) == 0
        north.append(chosen.astype(jnp.bfloat16))
        south.append(jnp.where(even, chosen, -chosen).astype(jnp.bfloat16))
    leg_parts = [split(leg[slot]) for slot in range(n_narrow)]
    block = n_narrow * owned

    def rows_of(picks):
        return jnp.concatenate(
            [
                jnp.dot(picks[slot], leg_parts[slot][half], preferred_element_type=jnp.float32)
                for half in range(2)
                for slot in range(n_narrow)
            ],
            axis=0,
        )

    source, lane = ids((LANE, LANE), 0), ids((LANE, LANE), 1)
    lane_rows = ids((block, LANE), 1)
    tiles = leg.shape[2] // LANE
    for southern, picks in ((False, north), (True, south)):
        rows = rows_of(picks).astype(jnp.bfloat16)
        tall = jnp.concatenate([rows[:, LANE * a : LANE * a + LANE] for a in range(tiles)], axis=0)
        for half in range(2):
            within = lane % lat_rows
            if southern:
                within = lat_rows - 1 - within
            spread = jnp.where(source == half * lat_rows + within, 1.0, 0.0).astype(jnp.bfloat16)
            wide_rows = jnp.dot(tall, spread, preferred_element_type=jnp.float32)
            for a in range(tiles):
                lat_block = 2 * a + half
                if southern:
                    lat_block = n_wide - 1 - lat_block
                for part in range(2):
                    piece = wide_rows[(a * 2 + part) * block : (a * 2 + part + 1) * block]
                    for level in range(levels):
                        kept_piece = jnp.where(lane_rows // lat_rows == level, piece, 0.0)
                        first = (part * levels + level) * block
                        lx[first : first + block, LANE * lat_block : LANE * lat_block + LANE] = (
                            kept_piece.astype(jnp.bfloat16)
                        )

    product = jnp.zeros((16, LANE), jnp.float32)
    plane = mates * n_narrow
    for code in range(planes):
        arrived = got.at[pl.ds(0, plane - 1 if code == 0 else plane)]
        pltpu.make_async_copy(arrived, arrived, four_recv.at[code]).wait()
        from_far = far_at
        for bit in bits:
            if code * mates & bit:
                from_far = from_far + bit // mates * (1 - 2 * ((wide // bit) % 2))
        strip = []
        for at in range(mates):
            values = jnp.concatenate(
                [got[from_far * plane + n_narrow * at + j] for j in range(n_narrow)], axis=0
            )
            top_half, rest = split(values)
            strip.append(jnp.concatenate([top_half, rest], axis=0))
        columns = pl.ds(pl.multiple_of(from_far * (mates * LANE), mates * LANE), mates * LANE)
        product = product + lax.dot_general(
            jnp.concatenate(strip, axis=1), lx[:, columns], last_dims, preferred_element_type=jnp.float32
        )
    product = product[0:8] + product[8:16]
    product = product + pltpu.roll(product, LANE // 2, 1)
    by_level = []
    for level in range(levels):
        moved = product if level == 0 else pltpu.roll(product, LANE - level * block, 1)
        by_level.append(jnp.where(lane8 < owned, moved, pltpu.roll(moved, 6, 0)))
    for i in range(levels_all):
        result = sum(weights[i][level] * by_level[level] for level in range(levels))
        result = result + pltpu.roll(result, 4, 0)
        second = pltpu.roll(result, LANE - owned, 1)
        for c in range(2):
            out[c, i, 0:1, :] = result[c : c + 1, 0:owned]
            out[c, i, 1:2, :] = second[c : c + 1, 0:owned]
    others = got.at[pl.ds(0, total - 1)]
    pltpu.make_async_copy(others, others, four_send).wait()
    leg_copy.wait_send()
    halo_step(1, "wait_send", wide < n_wide - 1)
    halo_step(0, "wait_send", wide > 0)


def fused_fits(tracer, band_map, legendre, n_wide, n_narrow):
    levels, lat_rows = tracer.shape[0], tracer.shape[1]
    waves = band_map.shape[0]
    return (
        levels == 2
        and n_narrow == 2
        and lat_rows * levels == LANE
        and waves == n_wide * n_narrow
        and n_wide & (n_wide - 1) == 0
        and -(-tracer.shape[2] // LANE) % CHUNKS == 0
        and -(-tracer.shape[2] // LANE) % PAD == 0
        and tracer.shape[2] > PAD * LANE
        and 4 * waves == LANE
        and legendre.shape[3] * 2 == n_wide * lat_rows
        and 2 * n_wide * 4 == LANE
    )


def fused(
    tracer, courant, nlon_counts, band_map, owner_map, legendre, modes_to, modes_from, mode_rates
):
    n_wide = lax.axis_size("wide")
    n_narrow = lax.axis_size("narrow")
    levels, lat_rows, lon_count = tracer.shape
    waves = band_map.shape[0]
    total = n_wide * n_narrow
    table = fourier_table(lon_count, waves)
    lon_pad = table.shape[0]
    tall = lat_rows + 2 * PAD
    half = legendre.shape[3]
    levels_all = levels * n_narrow
    vmem, smem, dma = pltpu.VMEM, pltpu.SMEM, pltpu.SemaphoreType.DMA
    operands = (
        tracer, courant, nlon_counts, band_map, owner_map,
        legendre.reshape(waves, half), modes_to, modes_from, mode_rates, jnp.asarray(table),
    )
    return pl.pallas_call(
        functools.partial(fused_kernel, n_wide, n_narrow, lon_count),
        out_shape=vmem((2, levels_all, 2, waves // n_narrow), jnp.float32),
        in_specs=[pl.BlockSpec(memory_space=pltpu.HBM)] * 10,
        out_specs=pl.BlockSpec(memory_space=pltpu.VMEM),
        scratch_shapes=[
            vmem((levels, tall, lon_count), jnp.float32),
            vmem((levels, tall, lon_count), jnp.float32),
            vmem((lon_pad, LANE), jnp.bfloat16),
            vmem((2 * levels * lat_rows, lon_pad), jnp.bfloat16),
            vmem((4 * PAD, lon_pad), jnp.bfloat16),
            vmem((levels, PAD, lon_count), jnp.float32),
            vmem(((levels + 1) * PAD * TALL, LANE), jnp.float32),
            vmem(((levels + 1) * PAD * TALL, LANE), jnp.float32),
            vmem((PAD * PAD + PAD, LANE), jnp.float32),
            vmem((levels * lat_rows, LANE), jnp.float32),
            vmem((n_narrow, waves, half), jnp.float32),
            smem((lat_rows,), jnp.int32),
            smem((waves,), jnp.int32),
            smem((waves,), jnp.int32),
            smem((levels_all, levels_all), jnp.float32),
            smem((levels_all, levels_all), jnp.float32),
            smem((levels_all,), jnp.float32),
            vmem((8 * n_wide, LANE), jnp.float32),
            vmem((lat_rows, LANE), jnp.int32),
            vmem((waves // n_narrow, LANE), jnp.int32),
            vmem((n_wide, 4, LANE), jnp.float32),
            vmem((total, 4, LANE), jnp.float32),
            vmem((LANE, n_wide * LANE), jnp.bfloat16),
            dma((6,)),
            dma((CHUNKS, 2)),
            dma,
            dma((2, 3)),
            dma((2, 3)),
            dma,
            dma((n_narrow,)),
            dma,
            dma((n_wide,)),
            pltpu.SemaphoreType.REGULAR,
        ],
        compiler_params=pltpu.CompilerParams(
            collective_id=0, has_side_effects=True
        ),
    )(*(pltpu.with_memory_space_constraint(operand, pltpu.HBM) for operand in operands))


def program(tracer, courant, nlon_counts, band_map, owner_map, legendre, *modes):
    choose = (
        fused
        if fused_fits(
            tracer, band_map, legendre, lax.axis_size("wide"), lax.axis_size("narrow")
        )
        else body
    )
    return choose(tracer, courant, nlon_counts, band_map, owner_map, legendre, *modes)


def solution(mesh):
    placed = (
        P("narrow", "wide", None),
        P("narrow", "wide", None),
        P("wide"),
        P(),
        P(),
        P(("wide", "narrow"), None, None, None),
        P(),
        P(),
        P(),
    )
    return jax.shard_map(
        program, mesh=mesh, in_specs=placed, out_specs=P(None, None, "wide", "narrow"), check_vma=False
    )
```

```python
import functools
import math

import jax
import jax.numpy as jnp
import numpy as np
from jax import lax
from jax.experimental import pallas as pl
from jax.experimental.pallas import tpu as pltpu
from jax.sharding import PartitionSpec as P

NLAT = 1024


def extended(array, sides, width):
    for axis, dim in sides:
        devices, length = (lax.axis_size(axis), array.shape[dim])
        up = [(i, (i + 1) % devices) for i in range(devices - 1)]
        down = [(j, i) for i, j in up]
        last = lax.slice_in_dim(array, length - width, length, axis=dim)
        initial = lax.slice_in_dim(array, 0, width, axis=dim)
        before = lax.ppermute(last, axis, up)
        after = lax.ppermute(initial, axis, down)
        array = jnp.concatenate([before, array, after], axis=dim)
    return array


def advect_section(field_ext, rate_ext, open_faces):
    row_total = field_ext.shape[1]
    row_below = field_ext[:, 0 : row_total - 3]
    row_here = field_ext[:, 1 : row_total - 2]
    row_above = field_ext[:, 2 : row_total - 1]
    row_beyond = field_ext[:, 3:row_total]
    face_rate = rate_ext[:, 1 : row_total - 2] * open_faces[1 : row_total - 2][:, None]
    upwind = (5.0 * row_here + 2.0 * row_above - row_below) / 6.0
    downwind = (5.0 * row_above + 2.0 * row_here - row_beyond) / 6.0
    low_bound = jnp.minimum(row_here, row_above)
    high_bound = jnp.maximum(row_here, row_above)
    face_value = jnp.clip(jnp.where(face_rate >= 0.0, upwind, downwind), low_bound, high_bound)
    face_flux = face_rate * face_value
    return field_ext[:, 2 : row_total - 2] - (face_flux[:, 1:] - face_flux[:, :-1])


def valid_rows(first_row, lat_rows, rim_width):
    row_ids = first_row + jnp.arange(lat_rows + 2 * rim_width, dtype=jnp.int32) - rim_width
    return ((row_ids >= 0) & (row_ids < NLAT - 1)).astype(jnp.float32)


def longitude_transform(advected, wave_count):
    levels_dev, lat_rows, lon_count = advected.shape
    short_len = 32
    long_len = lon_count // short_len
    block_count = wave_count // short_len
    row_count = levels_dev * lat_rows
    grid_rows = advected.reshape(row_count, short_len, long_len)
    short_ids = jnp.arange(short_len, dtype=jnp.int32)
    turn_one = short_ids[:, None] * short_ids[None, :] % short_len
    angle_one = 2.0 * math.pi / short_len * turn_one.astype(jnp.float32)
    highest = lax.Precision.HIGHEST
    inner_re = jnp.einsum("pab,ar->prb", grid_rows, jnp.cos(angle_one), precision=highest)
    inner_im = -jnp.einsum("pab,ar->prb", grid_rows, jnp.sin(angle_one), precision=highest)
    long_ids = jnp.arange(long_len, dtype=jnp.int32)
    block_ids = jnp.arange(block_count, dtype=jnp.int32)
    wave_ids = short_len * block_ids[None, None, :] + short_ids[:, None, None]
    turn_two = wave_ids * long_ids[None, :, None] % lon_count
    angle_two = 2.0 * math.pi / lon_count * turn_two.astype(jnp.float32)
    cos_two = jnp.cos(angle_two)
    sin_two = jnp.sin(angle_two)
    outer_re = jnp.einsum("prb,rbc->crp", inner_re, cos_two, precision=highest) + jnp.einsum(
        "prb,rbc->crp", inner_im, sin_two, precision=highest
    )
    outer_im = jnp.einsum("prb,rbc->crp", inner_im, cos_two, precision=highest) - jnp.einsum(
        "prb,rbc->crp", inner_re, sin_two, precision=highest
    )
    outer_re = (outer_re / math.sqrt(lon_count)).reshape(wave_count, levels_dev, lat_rows)
    outer_im = (outer_im / math.sqrt(lon_count)).reshape(wave_count, levels_dev, lat_rows)
    return jnp.stack([outer_re, outer_im], axis=1)


def body(
    tracer, courant, nlon_counts, band_map, owner_map, legendre, modes_to, modes_from, mode_rates
):
    levels_dev = tracer.shape[0]
    lat_rows = tracer.shape[1]
    n_wide = lax.axis_size("wide")
    n_narrow = lax.axis_size("narrow")
    first_row = lax.axis_index("wide") * lat_rows
    stacked = jnp.stack([tracer, courant])
    padded = extended(stacked, (("wide", 2),), 4)
    open_faces = valid_rows(first_row, lat_rows, 4)
    section_one = advect_section(padded[0], padded[1], open_faces)
    section_two = advect_section(section_one, padded[1][:, 2:-2], open_faces[2:-2])
    advected = 0.5 * tracer + 0.5 * section_two
    wave_count = band_map.shape[0]
    fourier = longitude_transform(advected, wave_count)
    wave_ids = jnp.arange(wave_count, dtype=jnp.int32)
    kept_mask = (2 * wave_ids[:, None] < nlon_counts[None, :]).astype(jnp.float32)
    fourier = fourier * kept_mask[:, None, None, :]
    slot_count = wave_count // (n_wide * n_narrow)
    fourier = jnp.einsum(
        "sm,mclj->sclj", (band_map[:, None] == wave_ids[None, :]).astype(jnp.float32), fourier,
        precision=lax.Precision.HIGHEST,
    )
    fourier = lax.all_to_all(fourier, "wide", split_axis=0, concat_axis=3, tiled=True)
    fourier = lax.all_to_all(fourier, "narrow", split_axis=0, concat_axis=2, tiled=True)
    levels_all = levels_dev * n_narrow
    half_rows = fourier.shape[3] // 2
    north_half = fourier[:, :, :, :half_rows]
    south_half = jnp.flip(fourier[:, :, :, half_rows:], axis=3)
    sym_part = north_half + south_half
    anti_part = north_half - south_half
    slot_start = (lax.axis_index("wide") * n_narrow + lax.axis_index("narrow")) * slot_count
    slot_waves = lax.dynamic_slice_in_dim(band_map, slot_start, slot_count)
    same_parity = (jnp.arange(2, dtype=jnp.int32)[None, :] - slot_waves[:, None]) % 2 == 0
    chosen = jnp.where(same_parity[:, :, None, None, None], sym_part[:, None], anti_part[:, None])
    spectral = jnp.einsum("spkj,spclj->spkcl", legendre, chosen, precision=lax.Precision.HIGHEST)
    degree_ids = (
        2 * jnp.arange(wave_count // 2, dtype=jnp.int32)[None, :]
        + jnp.arange(2, dtype=jnp.int32)[:, None]
    )
    upper_mask = (degree_ids[None] >= slot_waves[:, None, None]).astype(jnp.float32)
    spectral = spectral * upper_mask[:, :, :, None, None]
    spectral = jnp.transpose(spectral, (0, 2, 1, 3, 4)).reshape(
        slot_count, wave_count, 2, levels_all
    )
    spectral = jnp.einsum(
        "tn,sncl->stcl", (owner_map[:, None] == wave_ids[None, :]).astype(jnp.float32), spectral,
        precision=lax.Precision.HIGHEST,
    )
    gathered = lax.all_to_all(spectral, "narrow", split_axis=1, concat_axis=0, tiled=True)
    owned = gathered.shape[1]
    owned_degrees = lax.dynamic_slice_in_dim(owner_map, lax.axis_index("narrow") * owned, owned)
    degree_sq = (owned_degrees * (owned_degrees + 1)).astype(jnp.float32)
    damping = 1.0 / (1.0 + degree_sq[None, :] * mode_rates[:, None])
    modal_part = jnp.einsum("kl,stcl->kstc", modes_to, gathered, precision=lax.Precision.HIGHEST)
    scaled = modal_part * damping[:, None, :, None]
    return jnp.einsum("ik,kstc->cist", modes_from, scaled, precision=lax.Precision.HIGHEST)


MESH = pl.DeviceIdType.MESH
LANE = 128
PAD = 8
RIM = 4
CHUNKS = 4
STRIP = 512
TALL = 17
HALO = {1: (3, 2), 0: (3, 1)}


def chunk_list(lon_count, count):
    tiles = -(-lon_count // LANE)
    cuts = [min(lon_count, LANE * (tiles * cut // count)) for cut in range(count + 1)]
    return [(lo, hi - lo) for lo, hi in zip(cuts, cuts[1:])]


def fourier_table(lon_count, wave_count):
    rows = -(-lon_count // LANE) * LANE
    turns = np.outer(np.arange(lon_count), np.arange(wave_count)) % lon_count
    angle = 2.0 * np.pi / lon_count * turns
    full = np.concatenate([np.cos(angle), -np.sin(angle)], axis=1) * (0.5 / np.sqrt(lon_count))
    high = full.astype(jnp.bfloat16)
    low = (full - high.astype(np.float64)).astype(jnp.bfloat16)
    table = np.zeros((rows, LANE), jnp.bfloat16)
    table[:lon_count] = np.concatenate([high, low], axis=1)
    return table


def split(value):
    high = value.astype(jnp.bfloat16)
    low = (value - high.astype(jnp.float32)).astype(jnp.bfloat16)
    return high, low


def face_flux(field, rate, ahead):
    rows = field.shape[0]
    above = pltpu.roll(field, rows - 1, 0)
    step = above - field
    near = jnp.where(ahead, pltpu.roll(step, 1, 0), pltpu.roll(step, rows - 1, 0))
    slope = step * (1.0 / 3.0) + near * (1.0 / 6.0)
    slope = jnp.maximum(jnp.minimum(slope, jnp.maximum(step, 0.0)), jnp.minimum(step, 0.0))
    return rate * jnp.where(ahead, field + slope, above - slope)


def section(field, rate, ahead):
    flux = face_flux(field, rate, ahead)
    return field - (flux - pltpu.roll(flux, 1, 0))


def rim_flux(field, step, rate, ahead, face):
    here = step[face]
    near = jnp.where(ahead[face], step[face - 1], step[face + 1])
    slope = here * (1.0 / 3.0) + near * (1.0 / 6.0)
    slope = jnp.maximum(jnp.minimum(slope, jnp.maximum(here, 0.0)), jnp.minimum(here, 0.0))
    return rate[face] * jnp.where(ahead[face], field[face] + slope, field[face + 1] - slope)


def rim_section(field_row, rate_row, top):
    field = {row: field_row(row) for row in range(-4, RIM + 4)}
    rate = {row: rate_row(row) for row in range(-3, RIM + 2)}
    ahead = {row: rate[row] >= 0.0 for row in rate}
    step = {row: field[row + 1] - field[row] for row in range(-4, RIM + 3)}
    flux = {row: rim_flux(field, step, rate, ahead, row) for row in range(-3, RIM + 2)}
    flux[-3] = jnp.where(top, field[-4], flux[-3])
    flux[RIM + 1] = jnp.where(top, flux[RIM + 1], field[RIM + 3])
    once = {row: field[row] - (flux[row] - flux[row - 1]) for row in range(-2, RIM + 2)}
    step = {row: once[row + 1] - once[row] for row in range(-2, RIM + 1)}
    flux = {row: rim_flux(once, step, rate, ahead, row) for row in range(-1, RIM)}
    return [field[row] + (once[row] - (flux[row] - flux[row - 1])) for row in range(RIM)]


def ids(shape, dim):
    return lax.broadcasted_iota(jnp.int32, shape, dim)


def fused_kernel(
    n_wide, n_narrow, lon_count,
    tracer, courant, nlon, band, owner, legendre, modes_to, modes_from, rates, table,
    out,
    q_buf, c_buf, t_buf, a_buf, e_buf, f_buf, q_tall, c_tall, rim, spec, leg, nlon_s, band_s, owner_s, to_s, from_s, rate_s,
    pick, keep, degree, sent, got, lx,
    small_sem, load_sem, table_sem, halo_send, halo_recv, leg_send, leg_recv, four_send, four_recv,
    entered,
):
    wide, narrow = lax.axis_index("wide"), lax.axis_index("narrow")
    total = n_wide * n_narrow
    me = wide * n_narrow + narrow
    levels, lat_rows = tracer.shape[0], tracer.shape[1]
    wave_count = band_s.shape[0]
    lon_pad = t_buf.shape[0]
    chunks = chunk_list(lon_count, CHUNKS)
    owned = wave_count // n_narrow
    half_waves = wave_count // 2
    row_total = levels * lat_rows

    barrier = pltpu.get_barrier_semaphore()

    bits = [2**k for k in range(n_wide.bit_length() - 1)]
    mates = 2 ** (len(bits) // 2)
    planes = n_wide // mates
    far_at, near_at = wide // mates, wide % mates
    near = [
        (far_at * mates + (near_at + a) % mates, (narrow + b) % n_narrow)
        for a in range(mates)
        for b in range(n_narrow)
        if a or b
    ]
    far = [(((far_at + a) % planes) * mates + near_at, narrow) for a in range(1, planes)]
    last_near, first_near = near_at == mates - 1, near_at == 0
    crosses = (last_near & (far_at < planes - 1)) | (first_near & (far_at > 0))

    @pl.when(crosses)
    def _():
        pl.semaphore_signal(
            barrier,
            inc=1,
            device_id=(jnp.where(last_near, wide + 1, wide - 1), narrow),
            device_id_type=MESH,
        )

    for other in near + far:
        pl.semaphore_signal(barrier, inc=1, device_id=other, device_id_type=MESH)

    smalls = []
    for at, (here, there) in enumerate(
        ((nlon, nlon_s), (band, band_s), (owner, owner_s), (modes_to, to_s), (modes_from, from_s), (rates, rate_s))
    ):
        smalls.append(pltpu.make_async_copy(here, there, small_sem.at[at]))
    for copy in smalls:
        copy.start()
    loads = []
    for at, (lo, size) in enumerate(chunks):
        pair = []
        for which, (here, there) in enumerate(((tracer, q_buf), (courant, c_buf))):
            copy = pltpu.make_async_copy(
                here.at[:, :, pl.ds(lo, size)],
                there.at[:, pl.ds(PAD, lat_rows), pl.ds(lo, size)],
                load_sem.at[at, which],
            )
            copy.start()
            pair.append(copy)
        loads.append(pair)
    table_copy = pltpu.make_async_copy(table, t_buf, table_sem)
    own_leg = pltpu.make_async_copy(legendre, leg.at[narrow], leg_recv.at[narrow])
    own_leg.start()

    @pl.when(wide == 0)
    def _():
        q_buf[:, 0:PAD, :] = jnp.zeros((levels, PAD, lon_count), jnp.float32)
        c_buf[:, 0:PAD, :] = jnp.zeros((levels, PAD, lon_count), jnp.float32)

    @pl.when(wide == n_wide - 1)
    def _():
        q_buf[:, PAD + lat_rows :, :] = jnp.zeros((levels, PAD, lon_count), jnp.float32)
        c_buf[:, PAD + lat_rows :, :] = jnp.zeros((levels, PAD, lon_count), jnp.float32)

    greeted = len(near) + len(far)

    @pl.when(crosses)
    def _():
        pl.semaphore_wait(barrier, greeted + 1)

    @pl.when(jnp.logical_not(crosses))
    def _():
        pl.semaphore_wait(barrier, greeted)

    for other in far:
        pl.semaphore_signal(entered, inc=1, device_id=other, device_id_type=MESH)

    def halo(up, which):
        here, there = ((tracer, q_buf), (courant, c_buf), (f_buf, q_buf))[which]
        if which == 2:
            count = 1
            first = PAD - RIM + 1 if up else 1
            land = PAD - RIM if up else PAD + lat_rows + RIM - 1
        else:
            count = HALO[up][which]
            first = lat_rows - count if up else 0
            land = PAD - count if up else PAD + lat_rows
        return pltpu.make_async_remote_copy(
            src_ref=here.at[:, pl.ds(first, count), :],
            dst_ref=there.at[:, pl.ds(land, count), :],
            send_sem=halo_send.at[up, which],
            recv_sem=halo_recv.at[up, which],
            device_id=(wide + 1 if up else wide - 1, narrow),
            device_id_type=MESH,
        )

    odd = wide % 2 == 1

    def halo_step(up, what, cond, parts=(0, 1, 2)):
        @pl.when(cond)
        def _():
            for which in parts:
                getattr(halo(up, which), what)()

    def send_halos(parts):
        halo_step(1, "start", odd & (wide < n_wide - 1), parts)
        halo_step(0, "start", jnp.logical_not(odd) & (wide > 0), parts)
        halo_step(0, "start", odd, parts)
        halo_step(1, "start", jnp.logical_not(odd), parts)

    send_halos((0, 1))

    leg_copy = pltpu.make_async_remote_copy(
        src_ref=legendre,
        dst_ref=leg.at[narrow],
        send_sem=leg_send,
        recv_sem=leg_recv.at[narrow],
        device_id=(wide, 1 - narrow),
        device_id_type=MESH,
    )
    leg_copy.start()

    for copy in smalls:
        copy.wait()
    row8, lane8 = ids((8, LANE), 0), ids((8, LANE), 1)
    for at in range(n_wide):
        wave = jnp.where(row8 < 2, band_s[2 * at], band_s[2 * at + 1])
        column = (row8 % 2) * wave_count + wave
        hit = (row8 < 4) & (lane8 % (2 * wave_count) == column)
        pick[8 * at : 8 * at + 8, :] = jnp.where(hit, 1.0, 0.0)
    for row in range(lat_rows):
        keep[row : row + 1, :] = jnp.full((1, LANE), nlon_s[row], jnp.int32)
    for row in range(owned):
        degree[row : row + 1, :] = jnp.full((1, LANE), owner_s[narrow * owned + row], jnp.int32)

    lane1 = ids((1, LANE), 1)
    number = jnp.zeros((1, LANE), jnp.int32)
    for at in range(owned):
        number = jnp.where(lane1 % owned == at, owner_s[narrow * owned + at], number)
    squared = (number * (number + 1)).astype(jnp.float32)
    levels_all = levels * n_narrow
    damping = [1.0 / (1.0 + squared * rate_s[k]) for k in range(levels_all)]
    mix = [
        [
            sum((from_s[i, k] * to_s[k, l]) * damping[k] for k in range(levels_all))
            for l in range(levels_all)
        ]
        for i in range(levels_all)
    ]

    weights = [
        [
            jnp.where(row8 < 4, mix[i][level], mix[i][levels + level])
            for level in range(levels)
        ]
        for i in range(levels_all)
    ]
    a_buf[:, lon_pad - LANE :] = jnp.zeros((2 * row_total, LANE), jnp.bfloat16)

    def outer_flux(step, carry, lanes=STRIP):
        place = pl.ds(pl.multiple_of(step * STRIP, STRIP), lanes)
        lower = ids((PAD, lanes), 0) < RIM
        for level in range(levels):
            field, rate = (
                jnp.where(
                    lower,
                    buf[level, PAD : 2 * PAD, place],
                    buf[level, lat_rows : PAD + lat_rows, place],
                )
                for buf in (q_buf, c_buf)
            )
            f_buf[level, :, place] = face_flux(field, rate, rate >= 0.0)
        return carry

    width = lon_pad // CHUNKS
    for at in range(CHUNKS):
        for pair in loads[0:1] if at == 0 else loads[1:] if at == 1 else ():
            pair[0].wait()
            pair[1].wait()
        if at == 0:
            table_copy.start()
        if at == 1:
            strips, extra = divmod(lon_count, STRIP)
            lax.fori_loop(0, strips, outer_flux, 0)
            if extra:
                outer_flux(strips, 0, extra)
            send_halos((2,))

        def tile(step, carry, lo=at * width, lanes=LANE):
            columns = pl.ds(pl.multiple_of(lo + step * LANE, LANE), lanes)
            for level in range(levels):
                field = q_buf[level, PAD : PAD + lat_rows, columns]
                rate = c_buf[level, PAD : PAD + lat_rows, columns]
                ahead = rate >= 0.0
                twice = section(section(field, rate, ahead), rate, ahead)
                high, low = split(field + twice)
                first = level * lat_rows
                a_buf[first : first + lat_rows, columns] = high
                a_buf[row_total + first : row_total + first + lat_rows, columns] = low
            return carry

        whole, rest = divmod(chunks[at][1], LANE)
        lax.fori_loop(0, whole, tile, 0, unroll=2 if whole % 2 == 0 else 1)
        if rest:
            tile(whole, 0, lanes=rest)
    table_copy.wait()
    spectrum = jnp.dot(a_buf[...], t_buf[...], preferred_element_type=jnp.float32)
    spectrum = spectrum[0:row_total] + spectrum[row_total:]
    kept = 2 * (ids((lat_rows, LANE), 1) % wave_count) < keep[...]
    spec[...] = jnp.where(jnp.concatenate([kept] * levels, axis=0), spectrum, 0.0)

    @pl.when(wide == n_wide - 1)
    def _():
        last = PAD + lat_rows - 1
        c_buf[:, last : last + 1, :] = jnp.zeros((levels, 1, lon_count), jnp.float32)

    last_dims = (((1,), (1,)), ((), ()))

    def edge(top, slab):
        start = pl.multiple_of(jnp.where(top, 0, lat_rows), 8)
        first = jnp.where(top, PAD, PAD - RIM)

        def strip(step, carry, tiles=(LANE,) * PAD):
            places = [
                pl.ds(pl.multiple_of(step * PAD * LANE + k * LANE, LANE), lanes)
                for k, lanes in enumerate(tiles)
            ]
            for level in range(levels):
                for k, place in enumerate(places):
                    here = pl.ds((level * PAD + k) * TALL, 2 * PAD)
                    q_tall[here, 0 : tiles[k]] = q_buf[level, pl.ds(start, 2 * PAD), place]
                    c_tall[here, 0 : tiles[k]] = c_buf[level, pl.ds(start, 2 * PAD), place]
            for level in range(levels):
                base = level * PAD * TALL + first
                values = rim_section(
                    lambda row: q_tall[pl.ds(base + row, PAD, stride=TALL), :],
                    lambda row: c_tall[pl.ds(base + row, PAD, stride=TALL), :],
                    top,
                )
                for row, value in enumerate(values):
                    rim[pl.ds(level * RIM + row, PAD, stride=PAD), :] = value
            for k in range(PAD):
                value = rim[k * PAD : k * PAD + PAD, :]
                high = value.astype(jnp.bfloat16).astype(jnp.float32)
                both = jnp.concatenate([high, value - high], axis=0)
                place = pl.ds(pl.multiple_of(step * PAD * LANE + k * LANE, LANE), LANE)
                e_buf[pl.ds(slab, 2 * PAD), place] = both.astype(jnp.bfloat16)
            return carry

        whole = lon_count // (PAD * LANE)
        lax.fori_loop(0, whole, strip, 0, unroll=True)
        rest = lon_count - whole * PAD * LANE
        if rest:
            strip(whole, 0, tuple(min(LANE, rest - k * LANE) for k in range(PAD)))
    def replace(top, rows):
        rows = rows[0:PAD] + rows[PAD:]
        swapped = pltpu.roll(rows, RIM, 0)
        at = pl.multiple_of(jnp.where(top, 0, lat_rows - PAD), 8)
        fresh = jnp.where(top, row8, PAD - 1 - row8) < RIM
        cover = 2 * (lane8 % wave_count) < keep[pl.ds(at, PAD), :]
        for level, mine in enumerate(
            (jnp.where(top, rows, swapped), jnp.where(top, swapped, rows))
        ):
            place = pl.ds(pl.multiple_of(level * lat_rows + at, 8), PAD)
            spec[place, :] = jnp.where(fresh, jnp.where(cover, mine, 0.0), spec[place, :])

    halo_step(1, "wait_recv", odd)
    halo_step(0, "wait_recv", jnp.logical_not(odd))
    edge(odd, 0)
    halo_step(0, "wait_recv", odd & (wide < n_wide - 1))
    halo_step(1, "wait_recv", jnp.logical_not(odd) & (wide > 0))
    edge(jnp.logical_not(odd), 2 * PAD)
    rows = jnp.dot(e_buf[...], t_buf[...], preferred_element_type=jnp.float32)
    replace(odd, rows[0 : 2 * PAD])
    replace(jnp.logical_not(odd), rows[2 * PAD :])

    pl.semaphore_wait(entered, len(far))
    high, low = split(spec[...])
    chooser = pick[...].astype(jnp.bfloat16)
    moved = lax.dot_general(
        jnp.concatenate([chooser, chooser], axis=1),
        jnp.concatenate([high, low], axis=1),
        last_dims,
        preferred_element_type=jnp.float32,
    )
    for at in range(n_wide):
        sent[at] = moved[8 * at : 8 * at + 4, :]

    turns = [1 - 2 * ((wide // bit) % 2) for bit in bits]

    def fourier_copy(code):
        to_wide = wide
        for bit, turn in zip(bits, turns):
            if code // n_narrow & bit:
                to_wide = to_wide + bit * turn
        to_narrow = 1 - narrow if code % n_narrow else narrow
        return pltpu.make_async_remote_copy(
            src_ref=sent.at[to_wide],
            dst_ref=got.at[me],
            send_sem=four_send,
            recv_sem=four_recv.at[code // (n_narrow * mates)],
            device_id=(to_wide, to_narrow),
            device_id_type=MESH,
        )

    for code in range(total - 1, 0, -1):
        fourier_copy(code).start()
    got[me] = sent[wide]

    own_leg.wait()
    pltpu.make_async_remote_copy(
        src_ref=legendre,
        dst_ref=leg.at[1 - narrow],
        send_sem=leg_send,
        recv_sem=leg_recv.at[1 - narrow],
        device_id=(wide, 1 - narrow),
        device_id_type=MESH,
    ).wait_recv()

    degrees = degree[:, 0:wave_count]
    flat = ids((owned, wave_count), 1)
    held = 2 * (flat % half_waves) + flat // half_waves
    north, south = [], []
    for slot in range(n_narrow):
        wave = band_s[wide * n_narrow + slot]
        chosen = jnp.where((held == degrees) & (degrees >= wave), 1.0, 0.0)
        even = ((degrees + wave) % 2) == 0
        north.append(chosen.astype(jnp.bfloat16))
        south.append(jnp.where(even, chosen, -chosen).astype(jnp.bfloat16))
    leg_parts = [split(leg[slot]) for slot in range(n_narrow)]
    block = n_narrow * owned

    def rows_of(picks):
        return jnp.concatenate(
            [
                jnp.dot(picks[slot], leg_parts[slot][half], preferred_element_type=jnp.float32)
                for half in range(2)
                for slot in range(n_narrow)
            ],
            axis=0,
        )

    source, lane = ids((LANE, LANE), 0), ids((LANE, LANE), 1)
    lane_rows = ids((block, LANE), 1)
    tiles = leg.shape[2] // LANE
    for southern, picks in ((False, north), (True, south)):
        rows = rows_of(picks).astype(jnp.bfloat16)
        tall = jnp.concatenate([rows[:, LANE * a : LANE * a + LANE] for a in range(tiles)], axis=0)
        for half in range(2):
            within = lane % lat_rows
            if southern:
                within = lat_rows - 1 - within
            spread = jnp.where(source == half * lat_rows + within, 1.0, 0.0).astype(jnp.bfloat16)
            wide_rows = jnp.dot(tall, spread, preferred_element_type=jnp.float32)
            for a in range(tiles):
                lat_block = 2 * a + half
                if southern:
                    lat_block = n_wide - 1 - lat_block
                for part in range(2):
                    piece = wide_rows[(a * 2 + part) * block : (a * 2 + part + 1) * block]
                    for level in range(levels):
                        kept_piece = jnp.where(lane_rows // lat_rows == level, piece, 0.0)
                        first = (part * levels + level) * block
                        lx[first : first + block, LANE * lat_block : LANE * lat_block + LANE] = (
                            kept_piece.astype(jnp.bfloat16)
                        )

    product = jnp.zeros((16, LANE), jnp.float32)
    plane = mates * n_narrow
    for code in range(planes):
        arrived = got.at[pl.ds(0, plane - 1 if code == 0 else plane)]
        pltpu.make_async_copy(arrived, arrived, four_recv.at[code]).wait()
        from_far = far_at
        for bit in bits:
            if code * mates & bit:
                from_far = from_far + bit // mates * (1 - 2 * ((wide // bit) % 2))
        strip = []
        for at in range(mates):
            values = jnp.concatenate(
                [got[from_far * plane + n_narrow * at + j] for j in range(n_narrow)], axis=0
            )
            top_half, rest = split(values)
            strip.append(jnp.concatenate([top_half, rest], axis=0))
        columns = pl.ds(pl.multiple_of(from_far * (mates * LANE), mates * LANE), mates * LANE)
        product = product + lax.dot_general(
            jnp.concatenate(strip, axis=1), lx[:, columns], last_dims, preferred_element_type=jnp.float32
        )
    product = product[0:8] + product[8:16]
    product = product + pltpu.roll(product, LANE // 2, 1)
    by_level = []
    for level in range(levels):
        moved = product if level == 0 else pltpu.roll(product, LANE - level * block, 1)
        by_level.append(jnp.where(lane8 < owned, moved, pltpu.roll(moved, 6, 0)))
    for i in range(levels_all):
        result = sum(weights[i][level] * by_level[level] for level in range(levels))
        result = result + pltpu.roll(result, 4, 0)
        second = pltpu.roll(result, LANE - owned, 1)
        for c in range(2):
            out[c, i, 0:1, :] = result[c : c + 1, 0:owned]
            out[c, i, 1:2, :] = second[c : c + 1, 0:owned]
    others = got.at[pl.ds(0, total - 1)]
    pltpu.make_async_copy(others, others, four_send).wait()
    leg_copy.wait_send()
    halo_step(1, "wait_send", wide < n_wide - 1)
    halo_step(0, "wait_send", wide > 0)


def fused_fits(tracer, band_map, legendre, n_wide, n_narrow):
    levels, lat_rows = tracer.shape[0], tracer.shape[1]
    waves = band_map.shape[0]
    return (
        levels == 2
        and n_narrow == 2
        and lat_rows * levels == LANE
        and waves == n_wide * n_narrow
        and n_wide & (n_wide - 1) == 0
        and -(-tracer.shape[2] // LANE) % CHUNKS == 0
        and -(-tracer.shape[2] // LANE) % PAD == 0
        and tracer.shape[2] > PAD * LANE
        and 4 * waves == LANE
        and legendre.shape[3] * 2 == n_wide * lat_rows
        and 2 * n_wide * 4 == LANE
    )


def fused(
    tracer, courant, nlon_counts, band_map, owner_map, legendre, modes_to, modes_from, mode_rates
):
    n_wide = lax.axis_size("wide")
    n_narrow = lax.axis_size("narrow")
    levels, lat_rows, lon_count = tracer.shape
    waves = band_map.shape[0]
    total = n_wide * n_narrow
    table = fourier_table(lon_count, waves)
    lon_pad = table.shape[0]
    tall = lat_rows + 2 * PAD
    half = legendre.shape[3]
    levels_all = levels * n_narrow
    vmem, smem, dma = pltpu.VMEM, pltpu.SMEM, pltpu.SemaphoreType.DMA
    operands = (
        tracer, courant, nlon_counts, band_map, owner_map,
        legendre.reshape(waves, half), modes_to, modes_from, mode_rates, jnp.asarray(table),
    )
    return pl.pallas_call(
        functools.partial(fused_kernel, n_wide, n_narrow, lon_count),
        out_shape=vmem((2, levels_all, 2, waves // n_narrow), jnp.float32),
        in_specs=[pl.BlockSpec(memory_space=pltpu.HBM)] * 10,
        out_specs=pl.BlockSpec(memory_space=pltpu.VMEM),
        scratch_shapes=[
            vmem((levels, tall, lon_count), jnp.float32),
            vmem((levels, tall, lon_count), jnp.float32),
            vmem((lon_pad, LANE), jnp.bfloat16),
            vmem((2 * levels * lat_rows, lon_pad), jnp.bfloat16),
            vmem((4 * PAD, lon_pad), jnp.bfloat16),
            vmem((levels, PAD, lon_count), jnp.float32),
            vmem(((levels + 1) * PAD * TALL, LANE), jnp.float32),
            vmem(((levels + 1) * PAD * TALL, LANE), jnp.float32),
            vmem((PAD * PAD + PAD, LANE), jnp.float32),
            vmem((levels * lat_rows, LANE), jnp.float32),
            vmem((n_narrow, waves, half), jnp.float32),
            smem((lat_rows,), jnp.int32),
            smem((waves,), jnp.int32),
            smem((waves,), jnp.int32),
            smem((levels_all, levels_all), jnp.float32),
            smem((levels_all, levels_all), jnp.float32),
            smem((levels_all,), jnp.float32),
            vmem((8 * n_wide, LANE), jnp.float32),
            vmem((lat_rows, LANE), jnp.int32),
            vmem((waves // n_narrow, LANE), jnp.int32),
            vmem((n_wide, 4, LANE), jnp.float32),
            vmem((total, 4, LANE), jnp.float32),
            vmem((LANE, n_wide * LANE), jnp.bfloat16),
            dma((6,)),
            dma((CHUNKS, 2)),
            dma,
            dma((2, 3)),
            dma((2, 3)),
            dma,
            dma((n_narrow,)),
            dma,
            dma((n_wide,)),
            pltpu.SemaphoreType.REGULAR,
        ],
        compiler_params=pltpu.CompilerParams(
            collective_id=0, has_side_effects=True
        ),
    )(*(pltpu.with_memory_space_constraint(operand, pltpu.HBM) for operand in operands))


def program(tracer, courant, nlon_counts, band_map, owner_map, legendre, *modes):
    choose = (
        fused
        if fused_fits(
            tracer, band_map, legendre, lax.axis_size("wide"), lax.axis_size("narrow")
        )
        else body
    )
    return choose(tracer, courant, nlon_counts, band_map, owner_map, legendre, *modes)


def solution(mesh):
    placed = (
        P("narrow", "wide", None),
        P("narrow", "wide", None),
        P("wide"),
        P(),
        P(),
        P(("wide", "narrow"), None, None, None),
        P(),
        P(),
        P(),
    )
    return jax.shard_map(
        program, mesh=mesh, in_specs=placed, out_specs=P(None, None, "wide", "narrow"), check_vma=False
    )
```
